512 devices in a mesh: ep: 16 (over z), mx: 4 (over x), my: 8 (over y, core).
Axes of the slice: x: 4, y: 4, z: 16, core: 2. Of those that a mesh axis runs over, the one named last changes fastest.
Arguments:
- context: bfloat16 [16384, 2048], P(('ep', 'mx')), may hold values from -6 to 6
- resid_in: bfloat16 [16384, 2048], P(('ep', 'mx'), 'my'), may hold values from -70 to 70
- out_weight: bfloat16 [2048, 2048], P(None, 'my'), may hold values from -0.125 to 0.125
- norm_gain: float32 [2048], P('my'), may hold values from 0.5 to 1.5
- gate_weight: bfloat16 [8, 5632, 2048], P(None, ('ep', 'my'), 'mx'), may hold values from -0.125 to 0.125
- up_weight: bfloat16 [8, 5632, 2048], P(None, ('ep', 'my'), 'mx'), may hold values from -0.125 to 0.125
- down_weight: bfloat16 [8, 5632, 2048], P(None, ('ep', 'my'), 'mx'), may hold values from -0.078125 to 0.078125
- routes: int32 [16384, 2], P(('ep', 'mx')), may hold values from 0 to 7, all different within a row; in each aligned block of 256 rows (0 to 255, 256 to 511, ...) at most 96 rows name the same one
- gate_probs: float32 [16384, 2], P(('ep', 'mx')), may hold values from 0.05 to 1
- final_gain: float32 [2048], P('my'), may hold values from 0.5 to 1.5
Outputs:
- normed_out: bfloat16 [16384, 2048], P(('ep', 'mx'), 'my')
- stream_out: bfloat16 [16384, 2048], P(('ep', 'mx'), 'my')
The draws below stay inside these ranges and needn't reach their ends.
Inputs may be any that keep to these rules, and one draw needn't show every extreme that they name: `routes`: each row names 2 different experts; in each aligned block of 256 rows no expert is named by more than 96 rows, a bound that some block reaches.
All inputs are finite; a program needn't handle non-finite values.
Results may differ from the reference program's by a relative error of at most 0.012.
Values may be sent and summed in bfloat16 or wider, within the bound.
A program may use at most 128 MiB of HBM per device.

```python
import math
import jax
import jax.numpy as jnp
import numpy as np
from jax import lax

D = 2048
FF = 5632
EXPERTS = 8
TOPK = 2
TOK = 256
MOST = 96
ROWS = 16384
N_EP = 16
N_MY = 8


def draw_resid_in(key, part):
    key_base, key_cols, key_rows = jax.random.split(key, 3)
    base = jnp.clip(jax.random.normal(key_base, (ROWS, D), jnp.float32), -6.0, 6.0)
    column_pos = jnp.arange(D, dtype=jnp.float32) / (D - 1)
    rising = jnp.exp(math.log(3.0) * column_pos)
    column_spread = jnp.exp(jax.random.uniform(key_cols, (D,), jnp.float32) * math.log(3.4))
    row_scale = jnp.exp(jax.random.uniform(key_rows, (ROWS, 1), jnp.float32, -math.log(10.0), 0.0))
    values = base * row_scale * rising[None, :] * column_spread[None, :]
    return values.astype(jnp.bfloat16)


def level_of(key, shape, shards, low, top_value):
    level = 1.0
    for position, shards_of in shards:
        draws = jax.random.uniform(jax.random.fold_in(jax.random.fold_in(key, 6), position), (shards_of,), jnp.float32, low / len(shards), top_value / len(shards))
        level = level * jnp.repeat(jnp.exp(draws), shape[position] // shards_of).reshape((-1,) + (1,) * (len(shape) - 1 - position))
    return level


def shared_out(key, own, number, rows, number_of, top, reach, skew):
    sequence = jax.random.permutation(key, number_of)
    packed, ordinary = shares(number_of, rows * top, reach, skew, True), shares(number_of, rows * top, reach, skew, False)
    places = jnp.arange(number_of)

    def named(sizes, turn):
        used = int((sizes > 0).sum())
        fixed = max(1, used // 4)
        moved = fixed + (places - fixed + turn * (used - fixed)) % max(1, number_of - fixed)
        return jnp.zeros((number_of,), jnp.int32).at[sequence[jnp.where(places < fixed, places, moved)]].set(jnp.asarray(sizes, jnp.int32))

    sizes = jnp.where(number % 4 == 0, named(packed, number // 4), named(ordinary, number - number // 4 - 1))
    mixed = jax.random.permutation(jax.random.fold_in(own, 3), number_of)
    giver, receiver = mixed[0:number_of // 2 * 2:2], mixed[1:number_of // 2 * 2:2]
    slack = jnp.minimum(sizes[giver] - 1, reach - sizes[receiver]) // 2
    slack = jnp.where((giver == sequence[0]) | (receiver == sequence[0]) | (sizes[receiver] == 0), 0, jnp.maximum(slack, 0))
    moved = jax.random.randint(jax.random.fold_in(own, 4), (number_of // 2,), 0, 1 << 20) % (slack + 1)
    sizes = sizes.at[giver].add(-moved).at[receiver].add(moved)
    labels = jnp.searchsorted(jnp.cumsum(sizes), jnp.arange(rows * top), side="right").astype(jnp.int32)
    table = labels.reshape(top, rows).T
    table = table[jax.random.permutation(jax.random.fold_in(own, 1), rows)]
    turn = jax.random.randint(jax.random.fold_in(own, 2), (rows, 1), 0, top)
    return jnp.take_along_axis(table, (jnp.arange(top)[None, :] + turn) % top, axis=1)


def shares(count, total, reach, skew, full):
    loads = [(1 << 20) // math.isqrt(grade ** skew) + 1 for grade in range(1, count + 1)]
    largest = reach if full else min(reach, max(-(-total // count), total * loads[0] // sum(loads)))
    least = 1 if total - largest >= count - 1 else 0
    counts, rest = [largest] + [least] * (count - 1), total - largest - least * (count - 1)
    while rest > 0:
        free = [i for i in range(1, count) if counts[i] < largest] or [i for i in range(1, count) if counts[i] < reach]
        pool, left = sum([loads[i] for i in free]), rest
        for i in free:
            more = min(reach - counts[i], max(1, left * loads[i] // pool), rest)
            counts[i] = counts[i] + more
            rest = rest - more
    return np.array(counts)


def scatter_about(stream_key, extent, deviation, bound, cuts=(), kind=jnp.bfloat16):
    drawn = jax.random.normal(stream_key, extent, jnp.float32) * deviation
    if len(cuts) > 0:
        drawn = level_of(stream_key, extent, cuts, -0.22, 0.18) * drawn
    return jnp.clip(drawn, min=-bound, max=bound).astype(kind)


def setup_inputs(seed: int = 0) -> dict:
    seeds = jax.random.split(jax.random.key(seed), 11)
    context = scatter_about(seeds[0], (ROWS, D), 1.0, 6.0, ((0, 64),))
    resid_in = draw_resid_in(jax.random.fold_in(seeds[10], 71), 0)
    out_weight = scatter_about(seeds[2], (D, D), D ** -0.5, 0.125, ((1, 8),))
    norm_gain = jnp.clip(1.0 + 0.1 * jax.random.normal(seeds[3], (D,), jnp.float32), 0.5, 1.5)
    gate_weight = scatter_about(seeds[4], (EXPERTS, FF, D), D ** -0.5, 0.125, ((1, 128), (2, 4)))
    up_weight = scatter_about(seeds[5], (EXPERTS, FF, D), D ** -0.5, 0.125, ((1, 128), (2, 4)))
    down_weight = scatter_about(seeds[6], (EXPERTS, FF, D), FF ** -0.5, 0.078125, ((1, 128), (2, 4)))
    routes_keys = jax.random.split(jax.random.fold_in(seeds[7], 1), ROWS // TOK)
    routes_turns = jax.random.permutation(jax.random.fold_in(seeds[7], 3), ROWS // TOK)
    routes = jax.vmap(lambda own, number: shared_out(jax.random.fold_in(seeds[7], 2), own, number, TOK, EXPERTS, TOPK, MOST, 2))(routes_keys, routes_turns).reshape((ROWS, TOPK))
    gate_probs = jnp.clip(jnp.exp(math.log(1.0) - 2.9957323 * jax.random.uniform(seeds[8], (ROWS, TOPK), jnp.float32) ** level_of(seeds[8], (ROWS, TOPK), ((0, 64),), -0.2, 0.2)), 0.05, 1.0)
    final_gain = jnp.clip(1.0 + 0.1 * jax.random.normal(seeds[9], (D,), jnp.float32), 0.5, 1.5)
    return dict(context=context, resid_in=resid_in, out_weight=out_weight, norm_gain=norm_gain, gate_weight=gate_weight, up_weight=up_weight, down_weight=down_weight, routes=routes, gate_probs=gate_probs, final_gain=final_gain)


EPSILON = 1e-06

def apply_expert(operands):
    rows_in, w_gate, w_up, w_down = operands
    gate_proj = jnp.dot(rows_in, w_gate.T, preferred_element_type=jnp.float32)
    up_proj = jnp.dot(rows_in, w_up.T, preferred_element_type=jnp.float32)
    hidden = (jax.nn.silu(gate_proj) * up_proj).astype(jnp.bfloat16)
    piece = FF // (N_EP * N_MY)
    row_count = hidden.shape[0]
    hidden_split = hidden.reshape(row_count, N_EP, N_MY, piece)
    down_split = w_down.reshape(N_EP, N_MY, piece, D)
    total = jnp.zeros((row_count, D), jnp.float32)
    for group in range(N_MY):
        part_hidden = hidden_split[:, :, group, :].reshape(row_count, N_EP * piece)
        part_down = down_split[:, group].reshape(N_EP * piece, D)
        partial_sum = jnp.dot(part_hidden, part_down, preferred_element_type=jnp.float32).astype(jnp.bfloat16)
        partial_sum = lax.optimization_barrier(partial_sum)
        total = total + partial_sum.astype(jnp.float32)
    return total.astype(jnp.bfloat16)

def reference(context, resid_in, out_weight, norm_gain, gate_weight, up_weight, down_weight, routes, gate_probs, final_gain):
    projected = jnp.dot(context, out_weight, preferred_element_type=jnp.float32)
    stream = (projected + resid_in.astype(jnp.float32)).astype(jnp.bfloat16)
    stream_f = stream.astype(jnp.float32)
    scale_one = lax.rsqrt(lax.optimization_barrier(jnp.mean(stream_f * stream_f, axis=1, keepdims=True)) + EPSILON)
    normed = (stream_f * scale_one * norm_gain[None, :]).astype(jnp.bfloat16)
    blocks = ROWS // TOK
    chosen = routes.reshape(blocks, TOK * TOPK)
    onehot = (chosen[:, :, None] == jnp.arange(EXPERTS, dtype=jnp.int32)[None, None, :]).astype(jnp.int32)
    before = jnp.cumsum(onehot, axis=1) - onehot
    ranking = lax.optimization_barrier(jnp.sum(before * onehot, axis=2)).astype(jnp.int32)
    per_expert = blocks * MOST
    block_ids = jnp.arange(blocks, dtype=jnp.int32)[:, None]
    target = (chosen * per_expert + block_ids * MOST + ranking).reshape(-1).astype(jnp.int32)
    row_ids = jnp.arange(ROWS * TOPK, dtype=jnp.int32) // TOPK
    source = jnp.full((EXPERTS * per_expert,), ROWS, jnp.int32).at[target].set(row_ids)
    padded = jnp.concatenate([normed, jnp.zeros((1, D), jnp.bfloat16)], axis=0)
    grouped = padded[source].reshape(EXPERTS, per_expert, D)
    results = lax.map(apply_expert, (grouped, gate_weight, up_weight, down_weight))
    picked = results.reshape(EXPERTS * per_expert, D)[target].reshape(ROWS, TOPK, D).astype(jnp.float32)
    weights_norm = gate_probs / lax.optimization_barrier(jnp.sum(gate_probs, axis=1, keepdims=True))
    mixed = lax.optimization_barrier(jnp.sum(weights_norm[:, :, None] * picked, axis=1))
    updated = stream_f + mixed
    scale_two = lax.rsqrt(lax.optimization_barrier(jnp.mean(updated * updated, axis=1, keepdims=True)) + EPSILON)
    normed_out = (updated * scale_two * final_gain[None, :]).astype(jnp.bfloat16)
    return (normed_out, updated.astype(jnp.bfloat16))
```

```python
import jax
import jax.numpy as jnp
import numpy as np
from jax import lax
from jax.sharding import PartitionSpec as P

D = 2048
EXPERTS = 8
TOPK = 2
MOST = 96


EPSILON = 1e-06


def row_scale(stream_f):
    partial_sq = jnp.sum(stream_f * stream_f, axis=1)
    row_total = lax.psum(partial_sq, "my")
    return lax.rsqrt(row_total / D + EPSILON)


def shards(
    context,
    resid_in,
    out_weight,
    norm_gain,
    gate_weight,
    up_weight,
    down_weight,
    routes,
    gate_probs,
    final_gain,
):
    ep_count = lax.axis_size("ep")
    slot_dev = max(1, EXPERTS // ep_count)
    slot_total = slot_dev * ep_count
    replicas = slot_total // EXPERTS
    capacity = MOST // replicas
    tok_rows = context.shape[0]
    feat_block = resid_in.shape[1]
    piece_units = gate_weight.shape[1]
    slot_rows = ep_count * capacity

    expert_table = (
        np.arange(ep_count)[:, None] * slot_dev + np.arange(slot_dev)[None, :]
    ) // replicas
    stacked = jnp.stack([gate_weight, up_weight, down_weight], axis=0)
    chosen_rows = stacked[:, expert_table]
    got = lax.all_to_all(chosen_rows, "ep", split_axis=1, concat_axis=1, tiled=True)
    got = lax.all_gather(got, "mx", axis=4, tiled=True)
    got = jnp.transpose(got, (0, 2, 1, 3, 4)).reshape(3, slot_dev, ep_count * piece_units, D)
    w_gate, w_up, w_down = got[0], got[1], got[2]

    projected = jnp.dot(context, out_weight, preferred_element_type=jnp.float32)
    stream = (projected + resid_in.astype(jnp.float32)).astype(jnp.bfloat16)
    stream_f = stream.astype(jnp.float32)
    normed = (stream_f * row_scale(stream_f)[:, None] * norm_gain[None, :]).astype(jnp.bfloat16)
    chosen = routes.reshape(-1)
    onehot = (chosen[:, None] == jnp.arange(EXPERTS, dtype=jnp.int32)[None, :]).astype(jnp.int32)
    before = jnp.cumsum(onehot, axis=0) - onehot
    ranking = jnp.sum(before * onehot, axis=1)
    slot_index = chosen * replicas + ranking % replicas
    target = slot_index * capacity + ranking // replicas
    row_ids = jnp.arange(tok_rows * TOPK, dtype=jnp.int32) // TOPK
    source = jnp.full((slot_total * capacity,), tok_rows, jnp.int32).at[target].set(row_ids)
    padded = jnp.concatenate([normed, jnp.zeros((1, feat_block), jnp.bfloat16)], axis=0)
    packed = padded[source].reshape(ep_count, slot_dev, capacity, feat_block)
    landed = lax.all_to_all(packed, "ep", split_axis=0, concat_axis=0, tiled=True)
    gathered = lax.all_gather(landed, "my", axis=3, tiled=True)
    tokens_in = jnp.transpose(gathered, (1, 0, 2, 3)).reshape(slot_dev, slot_rows, D)

    gate_proj = jnp.einsum("srd,sfd->srf", tokens_in, w_gate, preferred_element_type=jnp.float32)
    up_proj = jnp.einsum("srd,sfd->srf", tokens_in, w_up, preferred_element_type=jnp.float32)
    hidden = (jax.nn.silu(gate_proj) * up_proj).astype(jnp.bfloat16)
    expert_out = jnp.einsum("srf,sfd->srd", hidden, w_down, preferred_element_type=jnp.float32)
    summed = lax.psum_scatter(
        expert_out.astype(jnp.bfloat16), "my", scatter_dimension=2, tiled=True
    )
    sent_back = summed.reshape(slot_dev, ep_count, capacity, feat_block)
    sent_back = jnp.transpose(sent_back, (1, 0, 2, 3))
    returned = lax.all_to_all(sent_back, "ep", split_axis=0, concat_axis=0, tiled=True).reshape(
        slot_total * capacity, feat_block
    )
    picked = returned[target].reshape(tok_rows, TOPK, feat_block).astype(jnp.float32)
    weights_norm = gate_probs / jnp.sum(gate_probs, axis=1, keepdims=True)
    mixed = jnp.sum(weights_norm[:, :, None] * picked, axis=1)
    updated = stream_f + mixed
    normed_out = (updated * row_scale(updated)[:, None] * final_gain[None, :]).astype(jnp.bfloat16)
    return (normed_out, updated.astype(jnp.bfloat16))


def solution(mesh):
    placed = (
        P(("ep", "mx"), None),
        P(("ep", "mx"), "my"),
        P(None, "my"),
        P("my"),
        P(None, ("ep", "my"), "mx"),
        P(None, ("ep", "my"), "mx"),
        P(None, ("ep", "my"), "mx"),
        P(("ep", "mx"), None),
        P(("ep", "mx"), None),
        P("my"),
    )
    return jax.shard_map(
        shards,
        mesh=mesh,
        in_specs=placed,
        out_specs=(P(("ep", "mx"), "my"), P(("ep", "mx"), "my")),
        check_vma=False,
    )
```

```python
import jax
import jax.numpy as jnp
import numpy as np
from jax import lax
from jax.sharding import PartitionSpec as P

D = 2048
EXPERTS = 8
TOPK = 2
MOST = 96


EPSILON = 1e-06


def row_scale(stream_f):
    partial_sq = jnp.sum(stream_f * stream_f, axis=1)
    row_total = lax.psum(partial_sq, "my")
    return lax.rsqrt(row_total / D + EPSILON)


def shards(
    context,
    resid_in,
    out_weight,
    norm_gain,
    gate_weight,
    up_weight,
    down_weight,
    routes,
    gate_probs,
    final_gain,
):
    ep_count = lax.axis_size("ep")
    slot_dev = max(1, EXPERTS // ep_count)
    slot_total = slot_dev * ep_count
    replicas = slot_total // EXPERTS
    capacity = MOST // replicas
    tok_rows = context.shape[0]
    feat_block = resid_in.shape[1]
    piece_units = gate_weight.shape[1]
    slot_rows = ep_count * capacity

    projected = jnp.dot(context, out_weight, preferred_element_type=jnp.float32)
    stream = (projected + resid_in.astype(jnp.float32)).astype(jnp.bfloat16)
    stream_f = stream.astype(jnp.float32)
    normed = (stream_f * row_scale(stream_f)[:, None] * norm_gain[None, :]).astype(jnp.bfloat16)
    chosen = routes.reshape(-1)
    onehot = (chosen[:, None] == jnp.arange(EXPERTS, dtype=jnp.int32)[None, :]).astype(jnp.int32)
    before = jnp.cumsum(onehot, axis=0) - onehot
    ranking = jnp.sum(before * onehot, axis=1)
    slot_index = chosen * replicas + ranking % replicas
    target = slot_index * capacity + ranking // replicas
    row_ids = jnp.arange(tok_rows * TOPK, dtype=jnp.int32) // TOPK
    source = jnp.full((slot_total * capacity,), tok_rows, jnp.int32).at[target].set(row_ids)
    padded = jnp.concatenate([normed, jnp.zeros((1, feat_block), jnp.bfloat16)], axis=0)
    packed = padded[source].reshape(ep_count, slot_dev, capacity, feat_block)
    landed = lax.all_to_all(packed, "ep", split_axis=0, concat_axis=0, tiled=True)
    gathered = lax.all_gather(landed, "my", axis=3, tiled=True)
    expert_table = (
        np.arange(ep_count)[:, None] * slot_dev + np.arange(slot_dev)[None, :]
    ) // replicas

    def fetch(weight, after):
        chosen_rows, _ = lax.optimization_barrier((weight[expert_table], after))
        got = lax.all_to_all(chosen_rows, "ep", split_axis=0, concat_axis=0, tiled=True)
        wide = lax.all_gather(got, "mx", axis=3, tiled=True)
        return got, jnp.transpose(wide, (1, 0, 2, 3)).reshape(slot_dev, ep_count * piece_units, D)

    raw_gate, w_gate = fetch(gate_weight, landed)
    raw_up, w_up = fetch(up_weight, raw_gate)
    _, w_down = fetch(down_weight, raw_up)
    tokens_in = jnp.transpose(gathered, (1, 0, 2, 3)).reshape(slot_dev, slot_rows, D)

    gate_proj = jnp.einsum("srd,sfd->srf", tokens_in, w_gate, preferred_element_type=jnp.float32)
    up_proj = jnp.einsum("srd,sfd->srf", tokens_in, w_up, preferred_element_type=jnp.float32)
    hidden = (jax.nn.silu(gate_proj) * up_proj).astype(jnp.bfloat16)
    expert_out = jnp.einsum("srf,sfd->srd", hidden, w_down, preferred_element_type=jnp.float32)
    summed = lax.psum_scatter(
        expert_out.astype(jnp.bfloat16), "my", scatter_dimension=2, tiled=True
    )
    sent_back = summed.reshape(slot_dev, ep_count, capacity, feat_block)
    sent_back = jnp.transpose(sent_back, (1, 0, 2, 3))
    returned = lax.all_to_all(sent_back, "ep", split_axis=0, concat_axis=0, tiled=True).reshape(
        slot_total * capacity, feat_block
    )
    picked = returned[target].reshape(tok_rows, TOPK, feat_block).astype(jnp.float32)
    weights_norm = gate_probs / jnp.sum(gate_probs, axis=1, keepdims=True)
    mixed = jnp.sum(weights_norm[:, :, None] * picked, axis=1)
    updated = stream_f + mixed
    normed_out = (updated * row_scale(updated)[:, None] * final_gain[None, :]).astype(jnp.bfloat16)
    return (normed_out, updated.astype(jnp.bfloat16))


def solution(mesh):
    placed = (
        P(("ep", "mx"), None),
        P(("ep", "mx"), "my"),
        P(None, "my"),
        P("my"),
        P(None, ("ep", "my"), "mx"),
        P(None, ("ep", "my"), "mx"),
        P(None, ("ep", "my"), "mx"),
        P(("ep", "mx"), None),
        P(("ep", "mx"), None),
        P("my"),
    )
    return jax.shard_map(
        shards,
        mesh=mesh,
        in_specs=placed,
        out_specs=(P(("ep", "mx"), "my"), P(("ep", "mx"), "my")),
        check_vma=False,
    )
```

```python
import functools

import jax
import jax.numpy as jnp
import numpy as np
from jax import lax
from jax.experimental import pallas as pl
from jax.experimental.pallas import tpu as pltpu
from jax.sharding import PartitionSpec as P

D = 2048
EXPERTS = 8
TOPK = 2
MOST = 96


EPSILON = 1e-06
MESH = pl.DeviceIdType.MESH


def move_kernel(n_ep, n_mx, w_ref, out_ref, send_z, recv_z, send_x, recv_x, local_sem):
    j = lax.axis_index("ep")
    a = lax.axis_index("mx")
    m = lax.axis_index("my")
    pending = []
    for k in range(w_ref.shape[0]):
        local = pltpu.make_async_copy(w_ref.at[k, j], out_ref.at[k, a, j], local_sem.at[k])
        local.start()
        along_z = []
        for d in range(1, n_ep):
            t = lax.rem(j + d, n_ep)
            copy = pltpu.make_async_remote_copy(
                src_ref=w_ref.at[k, t],
                dst_ref=out_ref.at[k, a, j],
                send_sem=send_z.at[k, d],
                recv_sem=recv_z.at[k, d],
                device_id=(t, a, m),
                device_id_type=MESH,
            )
            copy.start()
            along_z.append(copy)
        local.wait()
        for copy in along_z:
            copy.wait_recv()
        pending.extend(along_z)
        for e in range(1, n_mx):
            b = lax.rem(a + e, n_mx)
            copy = pltpu.make_async_remote_copy(
                src_ref=out_ref.at[k, a],
                dst_ref=out_ref.at[k, a],
                send_sem=send_x.at[k, e],
                recv_sem=recv_x.at[k, e],
                device_id=(j, b, m),
                device_id_type=MESH,
            )
            copy.start()
            pending.append(copy)
    for copy in pending:
        copy.wait_send()
    for k in range(w_ref.shape[0]):
        for e in range(1, n_mx):
            b = lax.rem(a + e, n_mx)
            pltpu.make_async_remote_copy(
                src_ref=out_ref.at[k, a],
                dst_ref=out_ref.at[k, a],
                send_sem=send_x.at[k, e],
                recv_sem=recv_x.at[k, e],
                device_id=(j, b, m),
                device_id_type=MESH,
            ).wait_recv()


def move_weights(stacked, n_ep, n_mx):
    count, _, units, wb = stacked.shape
    return pl.pallas_call(
        functools.partial(move_kernel, n_ep, n_mx),
        out_shape=jax.ShapeDtypeStruct((count, n_mx, n_ep, units, wb), stacked.dtype),
        in_specs=[pl.BlockSpec(memory_space=pl.ANY)],
        out_specs=pl.BlockSpec(memory_space=pl.ANY),
        scratch_shapes=[
            pltpu.SemaphoreType.DMA((count, n_ep)),
            pltpu.SemaphoreType.DMA((count, n_ep)),
            pltpu.SemaphoreType.DMA((count, n_mx)),
            pltpu.SemaphoreType.DMA((count, n_mx)),
            pltpu.SemaphoreType.DMA((count,)),
        ],
        compiler_params=pltpu.CompilerParams(has_side_effects=True),
    )(stacked)


def row_scale(stream_f):
    partial_sq = jnp.sum(stream_f * stream_f, axis=1)
    row_total = lax.psum(partial_sq, "my")
    return lax.rsqrt(row_total / D + EPSILON)


def shards(
    context,
    resid_in,
    out_weight,
    norm_gain,
    gate_weight,
    up_weight,
    down_weight,
    routes,
    gate_probs,
    final_gain,
):
    ep_count = lax.axis_size("ep")
    slot_dev = max(1, EXPERTS // ep_count)
    slot_total = slot_dev * ep_count
    replicas = slot_total // EXPERTS
    capacity = MOST // replicas
    tok_rows = context.shape[0]
    feat_block = resid_in.shape[1]
    piece_units = gate_weight.shape[1]
    slot_rows = ep_count * capacity

    projected = jnp.dot(context, out_weight, preferred_element_type=jnp.float32)
    stream = (projected + resid_in.astype(jnp.float32)).astype(jnp.bfloat16)
    stream_f = stream.astype(jnp.float32)
    normed = (stream_f * row_scale(stream_f)[:, None] * norm_gain[None, :]).astype(jnp.bfloat16)
    chosen = routes.reshape(-1)
    onehot = (chosen[:, None] == jnp.arange(EXPERTS, dtype=jnp.int32)[None, :]).astype(jnp.int32)
    before = jnp.cumsum(onehot, axis=0) - onehot
    ranking = jnp.sum(before * onehot, axis=1)
    slot_index = chosen * replicas + ranking % replicas
    target = slot_index * capacity + ranking // replicas
    row_ids = jnp.arange(tok_rows * TOPK, dtype=jnp.int32) // TOPK
    source = jnp.full((slot_total * capacity,), tok_rows, jnp.int32).at[target].set(row_ids)
    padded = jnp.concatenate([normed, jnp.zeros((1, feat_block), jnp.bfloat16)], axis=0)
    packed = padded[source].reshape(ep_count, slot_dev, capacity, feat_block)
    landed = lax.all_to_all(packed, "ep", split_axis=0, concat_axis=0, tiled=True)
    gathered = lax.all_gather(landed, "my", axis=3, tiled=True)
    expert_of_slot = np.arange(ep_count) // replicas
    stacked = jnp.stack([gate_weight, up_weight, down_weight], axis=0)[:, expert_of_slot]
    moved = move_weights(stacked, ep_count, lax.axis_size("mx"))
    w_gate, w_up, w_down = moved[0], moved[1], moved[2]
    tokens_in = jnp.transpose(gathered, (1, 0, 2, 3)).reshape(slot_dev, slot_rows, D)

    split_rows = tokens_in.reshape(slot_rows, w_gate.shape[0], w_gate.shape[3])
    gate_proj = jnp.einsum("rac,aspc->rsp", split_rows, w_gate, preferred_element_type=jnp.float32)
    up_proj = jnp.einsum("rac,aspc->rsp", split_rows, w_up, preferred_element_type=jnp.float32)
    hidden = (jax.nn.silu(gate_proj) * up_proj).astype(jnp.bfloat16)
    expert_out = jnp.einsum("rsp,aspc->rac", hidden, w_down, preferred_element_type=jnp.float32)
    expert_out = expert_out.reshape(slot_dev, slot_rows, D)
    summed = lax.psum_scatter(
        expert_out.astype(jnp.bfloat16), "my", scatter_dimension=2, tiled=True
    )
    sent_back = summed.reshape(slot_dev, ep_count, capacity, feat_block)
    sent_back = jnp.transpose(sent_back, (1, 0, 2, 3))
    returned = lax.all_to_all(sent_back, "ep", split_axis=0, concat_axis=0, tiled=True).reshape(
        slot_total * capacity, feat_block
    )
    picked = returned[target].reshape(tok_rows, TOPK, feat_block).astype(jnp.float32)
    weights_norm = gate_probs / jnp.sum(gate_probs, axis=1, keepdims=True)
    mixed = jnp.sum(weights_norm[:, :, None] * picked, axis=1)
    updated = stream_f + mixed
    normed_out = (updated * row_scale(updated)[:, None] * final_gain[None, :]).astype(jnp.bfloat16)
    return (normed_out, updated.astype(jnp.bfloat16))


def solution(mesh):
    placed = (
        P(("ep", "mx"), None),
        P(("ep", "mx"), "my"),
        P(None, "my"),
        P("my"),
        P(None, ("ep", "my"), "mx"),
        P(None, ("ep", "my"), "mx"),
        P(None, ("ep", "my"), "mx"),
        P(("ep", "mx"), None),
        P(("ep", "mx"), None),
        P("my"),
    )
    return jax.shard_map(
        shards,
        mesh=mesh,
        in_specs=placed,
        out_specs=(P(("ep", "mx"), "my"), P(("ep", "mx"), "my")),
        check_vma=False,
    )
```

```python
import functools

import jax
import jax.numpy as jnp
import numpy as np
from jax import lax
from jax.experimental import pallas as pl
from jax.experimental.pallas import tpu as pltpu
from jax.sharding import PartitionSpec as P

D = 2048
EXPERTS = 8
TOPK = 2
MOST = 96


EPSILON = 1e-06
MESH = pl.DeviceIdType.MESH


def remote(src, dst, send, recv, device):
    return pltpu.make_async_remote_copy(
        src_ref=src, dst_ref=dst, send_sem=send, recv_sem=recv,
        device_id=device, device_id_type=MESH,
    )


def move_kernel(n_ep, n_mx, n_my, replicas, packed_ref, gate_ref, up_ref, down_ref,
                tok_ref, out_ref, tok_sems, send_z, recv_z, send_x, recv_x, local_sem):
    j = lax.axis_index("ep")
    a = lax.axis_index("mx")
    m = lax.axis_index("my")
    fb = packed_ref.shape[2]
    wb = gate_ref.shape[2]
    cols_m = pl.ds(pl.multiple_of(m * fb, fb), fb)
    cols_a = pl.ds(pl.multiple_of(a * wb, wb), wb)
    pending = []
    tok_local = pltpu.make_async_copy(packed_ref.at[j], tok_ref.at[j, :, cols_m], tok_sems.at[0, 0])
    tok_local.start()
    tok_z = []
    for d in range(1, n_ep):
        t = lax.rem(j + d, n_ep)
        copy = remote(packed_ref.at[t], tok_ref.at[j, :, cols_m], tok_sems.at[1, d], tok_sems.at[2, d], (t, a, m))
        copy.start()
        tok_z.append(copy)
    weights = (gate_ref, up_ref, down_ref)

    def start_z(k):
        local = pltpu.make_async_copy(
            weights[k].at[j // replicas], out_ref.at[k, j, :, cols_a], local_sem.at[k])
        local.start()
        along_z = [local]
        for d in range(1, n_ep):
            t = lax.rem(j + d, n_ep)
            copy = remote(weights[k].at[t // replicas], out_ref.at[k, j, :, cols_a],
                          send_z.at[k, d], recv_z.at[k, d], (t, a, m))
            copy.start()
            along_z.append(copy)
        return along_z

    along_z = start_z(0)
    tok_local.wait()
    for copy in tok_z:
        copy.wait_recv()
    pending.extend(tok_z)
    tok_my = []
    for e in range(1, n_my):
        b = lax.rem(m + e, n_my)
        copy = remote(tok_ref.at[:, :, cols_m], tok_ref.at[:, :, cols_m], tok_sems.at[3, e], tok_sems.at[4, e], (j, a, b))
        copy.start()
        tok_my.append(copy)
    pending.extend(tok_my)
    x_copies = []
    for k in range(3):
        along_z[0].wait()
        for copy in along_z[1:]:
            copy.wait_recv()
        pending.extend(along_z[1:])
        if k + 1 < 3:
            along_z = start_z(k + 1)
        for e in range(1, n_mx):
            b = lax.rem(a + e, n_mx)
            copy = remote(out_ref.at[k, :, :, cols_a], out_ref.at[k, :, :, cols_a],
                          send_x.at[k, e], recv_x.at[k, e], (j, b, m))
            copy.start()
            x_copies.append(copy)
    pending.extend(x_copies)
    for copy in pending:
        copy.wait_send()
    for copy in tok_my + x_copies:
        copy.wait_recv()


def move_all(packed, gate_weight, up_weight, down_weight, n_ep, n_mx, n_my, replicas):
    _, rows, fb = packed.shape
    _, units, wb = gate_weight.shape
    return pl.pallas_call(
        functools.partial(move_kernel, n_ep, n_mx, n_my, replicas),
        out_shape=(
            jax.ShapeDtypeStruct((n_ep, rows, n_my * fb), packed.dtype),
            jax.ShapeDtypeStruct((3, n_ep, units, n_mx * wb), gate_weight.dtype),
        ),
        in_specs=[pl.BlockSpec(memory_space=pl.ANY)] * 4,
        out_specs=(pl.BlockSpec(memory_space=pl.ANY), pl.BlockSpec(memory_space=pl.ANY)),
        scratch_shapes=[
            pltpu.SemaphoreType.DMA((5, max(n_ep, n_my))),
            pltpu.SemaphoreType.DMA((3, n_ep)),
            pltpu.SemaphoreType.DMA((3, n_ep)),
            pltpu.SemaphoreType.DMA((3, n_mx)),
            pltpu.SemaphoreType.DMA((3, n_mx)),
            pltpu.SemaphoreType.DMA((3,)),
        ],
        compiler_params=pltpu.CompilerParams(has_side_effects=True),
    )(packed, gate_weight, up_weight, down_weight)


def row_scale(stream_f):
    partial_sq = jnp.sum(stream_f * stream_f, axis=1)
    row_total = lax.psum(partial_sq, "my")
    return lax.rsqrt(row_total / D + EPSILON)


def shards(
    context,
    resid_in,
    out_weight,
    norm_gain,
    gate_weight,
    up_weight,
    down_weight,
    routes,
    gate_probs,
    final_gain,
):
    ep_count = lax.axis_size("ep")
    slot_dev = max(1, EXPERTS // ep_count)
    slot_total = slot_dev * ep_count
    replicas = slot_total // EXPERTS
    capacity = MOST // replicas
    tok_rows = context.shape[0]
    feat_block = resid_in.shape[1]
    piece_units = gate_weight.shape[1]
    slot_rows = ep_count * capacity

    projected = jnp.dot(context, out_weight, preferred_element_type=jnp.float32)
    stream = (projected + resid_in.astype(jnp.float32)).astype(jnp.bfloat16)
    stream_f = stream.astype(jnp.float32)
    normed = (stream_f * row_scale(stream_f)[:, None] * norm_gain[None, :]).astype(jnp.bfloat16)
    chosen = routes.reshape(-1)
    onehot = (chosen[:, None] == jnp.arange(EXPERTS, dtype=jnp.int32)[None, :]).astype(jnp.int32)
    before = jnp.cumsum(onehot, axis=0) - onehot
    ranking = jnp.sum(before * onehot, axis=1)
    slot_index = chosen * replicas + ranking % replicas
    target = slot_index * capacity + ranking // replicas
    row_ids = jnp.arange(tok_rows * TOPK, dtype=jnp.int32) // TOPK
    source = jnp.full((slot_total * capacity,), tok_rows, jnp.int32).at[target].set(row_ids)
    padded = jnp.concatenate([normed, jnp.zeros((1, feat_block), jnp.bfloat16)], axis=0)
    packed = padded[source].reshape(ep_count, capacity, feat_block)
    tok, moved = move_all(
        packed, gate_weight, up_weight, down_weight,
        ep_count, lax.axis_size("mx"), lax.axis_size("my"), replicas,
    )
    tokens_in = tok.reshape(slot_rows, D)
    flat = moved.reshape(3, ep_count * piece_units, D)
    w_gate, w_up, w_down = flat[0], flat[1], flat[2]
    gate_proj = jnp.dot(tokens_in, w_gate.T, preferred_element_type=jnp.float32)
    up_proj = jnp.dot(tokens_in, w_up.T, preferred_element_type=jnp.float32)
    hidden = (jax.nn.silu(gate_proj) * up_proj).astype(jnp.bfloat16)
    expert_out = jnp.dot(hidden, w_down, preferred_element_type=jnp.float32)
    expert_out = expert_out.reshape(slot_dev, slot_rows, D)
    summed = lax.psum_scatter(
        expert_out.astype(jnp.bfloat16), "my", scatter_dimension=2, tiled=True
    )
    sent_back = summed.reshape(slot_dev, ep_count, capacity, feat_block)
    sent_back = jnp.transpose(sent_back, (1, 0, 2, 3))
    returned = lax.all_to_all(sent_back, "ep", split_axis=0, concat_axis=0, tiled=True).reshape(
        slot_total * capacity, feat_block
    )
    picked = returned[target].reshape(tok_rows, TOPK, feat_block).astype(jnp.float32)
    weights_norm = gate_probs / jnp.sum(gate_probs, axis=1, keepdims=True)
    mixed = jnp.sum(weights_norm[:, :, None] * picked, axis=1)
    updated = stream_f + mixed
    normed_out = (updated * row_scale(updated)[:, None] * final_gain[None, :]).astype(jnp.bfloat16)
    return (normed_out, updated.astype(jnp.bfloat16))


def solution(mesh):
    placed = (
        P(("ep", "mx"), None),
        P(("ep", "mx"), "my"),
        P(None, "my"),
        P("my"),
        P(None, ("ep", "my"), "mx"),
        P(None, ("ep", "my"), "mx"),
        P(None, ("ep", "my"), "mx"),
        P(("ep", "mx"), None),
        P(("ep", "mx"), None),
        P("my"),
    )
    return jax.shard_map(
        shards,
        mesh=mesh,
        in_specs=placed,
        out_specs=(P(("ep", "mx"), "my"), P(("ep", "mx"), "my")),
        check_vma=False,
    )
```

```python
import functools

import jax
import jax.numpy as jnp
import numpy as np
from jax import lax
from jax.experimental import pallas as pl
from jax.experimental.pallas import tpu as pltpu
from jax.sharding import PartitionSpec as P

D = 2048
EXPERTS = 8
TOPK = 2
MOST = 96


EPSILON = 1e-06
MESH = pl.DeviceIdType.MESH


def remote(src, dst, send, recv, device):
    return pltpu.make_async_remote_copy(
        src_ref=src, dst_ref=dst, send_sem=send, recv_sem=recv,
        device_id=device, device_id_type=MESH,
    )


def move_kernel(n_ep, n_mx, n_my, replicas, packed_ref, gate_ref, up_ref, down_ref,
                tok_ref, gate_out, up_out, down_out, tok_sems, send_z, recv_z, send_x, recv_x, local_sem):
    j = lax.axis_index("ep")
    a = lax.axis_index("mx")
    m = lax.axis_index("my")
    fb = packed_ref.shape[2]
    wb = gate_ref.shape[2]
    cols_m = pl.ds(pl.multiple_of(m * fb, fb), fb)
    cols_a = pl.ds(pl.multiple_of(a * wb, wb), wb)
    pending = []
    tok_local = pltpu.make_async_copy(packed_ref.at[j], tok_ref.at[j, :, cols_m], tok_sems.at[0, 0])
    tok_local.start()
    tok_z = []
    for d in range(1, n_ep):
        t = lax.rem(j + d, n_ep)
        copy = remote(packed_ref.at[t], tok_ref.at[j, :, cols_m], tok_sems.at[1, d], tok_sems.at[2, d], (t, a, m))
        copy.start()
        tok_z.append(copy)
    weights = (gate_ref, up_ref, down_ref)
    outs = (gate_out, up_out, down_out)

    def start_z(k):
        local = pltpu.make_async_copy(
            weights[k].at[j // replicas], outs[k].at[j, :, cols_a], local_sem.at[k])
        local.start()
        along_z = [local]
        for d in range(1, n_ep):
            t = lax.rem(j + d, n_ep)
            copy = remote(weights[k].at[t // replicas], outs[k].at[j, :, cols_a],
                          send_z.at[k, d], recv_z.at[k, d], (t, a, m))
            copy.start()
            along_z.append(copy)
        return along_z

    along_z = start_z(0)
    tok_local.wait()
    for copy in tok_z:
        copy.wait_recv()
    pending.extend(tok_z)
    tok_my = []
    for e in range(1, n_my):
        b = lax.rem(m + e, n_my)
        copy = remote(tok_ref.at[:, :, cols_m], tok_ref.at[:, :, cols_m], tok_sems.at[3, e], tok_sems.at[4, e], (j, a, b))
        copy.start()
        tok_my.append(copy)
    pending.extend(tok_my)
    x_copies = []
    for k in range(3):
        along_z[0].wait()
        for copy in along_z[1:]:
            copy.wait_recv()
        pending.extend(along_z[1:])
        if k + 1 < 3:
            along_z = start_z(k + 1)
        if n_mx == 4:
            right = lax.rem(a + 1, n_mx)
            left = lax.rem(a + n_mx - 1, n_mx)
            half = n_ep // 2
            to_right = remote(outs[k].at[:, :, cols_a], outs[k].at[:, :, cols_a],
                              send_x.at[k, 0], recv_x.at[k, 0], (j, right, m))
            to_left = remote(outs[k].at[:, :, cols_a], outs[k].at[:, :, cols_a],
                             send_x.at[k, 1], recv_x.at[k, 1], (j, left, m))
            to_right.start()
            to_left.start()
            cols_l = pl.ds(pl.multiple_of(left * wb, wb), wb)
            cols_r = pl.ds(pl.multiple_of(right * wb, wb), wb)
            to_right.wait_recv()
            fwd_right = remote(outs[k].at[pl.ds(0, half), :, cols_l], outs[k].at[pl.ds(0, half), :, cols_l],
                               send_x.at[k, 2], recv_x.at[k, 2], (j, right, m))
            fwd_right.start()
            to_left.wait_recv()
            fwd_left = remote(outs[k].at[pl.ds(half, half), :, cols_r], outs[k].at[pl.ds(half, half), :, cols_r],
                              send_x.at[k, 3], recv_x.at[k, 3], (j, left, m))
            fwd_left.start()
            pending.extend([to_right, to_left])
            x_copies.extend([fwd_right, fwd_left])
        else:
            for e in range(1, n_mx):
                b = lax.rem(a + e, n_mx)
                copy = remote(outs[k].at[:, :, cols_a], outs[k].at[:, :, cols_a],
                              send_x.at[k, e], recv_x.at[k, e], (j, b, m))
                copy.start()
                x_copies.append(copy)
    pending.extend(x_copies)
    for copy in pending:
        copy.wait_send()
    for copy in tok_my + x_copies:
        copy.wait_recv()


def move_all(packed, gate_weight, up_weight, down_weight, n_ep, n_mx, n_my, replicas):
    _, rows, fb = packed.shape
    _, units, wb = gate_weight.shape
    return pl.pallas_call(
        functools.partial(move_kernel, n_ep, n_mx, n_my, replicas),
        out_shape=(
            jax.ShapeDtypeStruct((n_ep, rows, n_my * fb), packed.dtype),
        ) + (jax.ShapeDtypeStruct((n_ep, units, n_mx * wb), gate_weight.dtype),) * 3,
        in_specs=[pl.BlockSpec(memory_space=pl.ANY)] * 4,
        out_specs=(pl.BlockSpec(memory_space=pl.ANY),) * 4,
        scratch_shapes=[
            pltpu.SemaphoreType.DMA((5, max(n_ep, n_my))),
            pltpu.SemaphoreType.DMA((3, n_ep)),
            pltpu.SemaphoreType.DMA((3, n_ep)),
            pltpu.SemaphoreType.DMA((3, max(n_mx, 4))),
            pltpu.SemaphoreType.DMA((3, max(n_mx, 4))),
            pltpu.SemaphoreType.DMA((3,)),
        ],
        compiler_params=pltpu.CompilerParams(has_side_effects=True),
    )(packed, gate_weight, up_weight, down_weight)


def row_scale(stream_f):
    partial_sq = jnp.sum(stream_f * stream_f, axis=1)
    row_total = lax.psum(partial_sq, "my")
    return lax.rsqrt(row_total / D + EPSILON)


def shards(
    context,
    resid_in,
    out_weight,
    norm_gain,
    gate_weight,
    up_weight,
    down_weight,
    routes,
    gate_probs,
    final_gain,
):
    ep_count = lax.axis_size("ep")
    slot_dev = max(1, EXPERTS // ep_count)
    slot_total = slot_dev * ep_count
    replicas = slot_total // EXPERTS
    capacity = MOST // replicas
    tok_rows = context.shape[0]
    feat_block = resid_in.shape[1]
    piece_units = gate_weight.shape[1]
    slot_rows = ep_count * capacity

    projected = jnp.dot(context, out_weight, preferred_element_type=jnp.float32)
    stream = (projected + resid_in.astype(jnp.float32)).astype(jnp.bfloat16)
    stream_f = stream.astype(jnp.float32)
    normed = (stream_f * row_scale(stream_f)[:, None] * norm_gain[None, :]).astype(jnp.bfloat16)
    chosen = routes.reshape(-1)
    onehot = (chosen[:, None] == jnp.arange(EXPERTS, dtype=jnp.int32)[None, :]).astype(jnp.int32)
    before = jnp.cumsum(onehot, axis=0) - onehot
    ranking = jnp.sum(before * onehot, axis=1)
    slot_index = chosen * replicas + ranking % replicas
    target = slot_index * capacity + ranking // replicas
    row_ids = jnp.arange(tok_rows * TOPK, dtype=jnp.int32) // TOPK
    source = jnp.full((slot_total * capacity,), tok_rows, jnp.int32).at[target].set(row_ids)
    padded = jnp.concatenate([normed, jnp.zeros((1, feat_block), jnp.bfloat16)], axis=0)
    packed = padded[source].reshape(ep_count, capacity, feat_block)
    tok, w_gate, w_up, w_down = move_all(
        packed, gate_weight, up_weight, down_weight,
        ep_count, lax.axis_size("mx"), lax.axis_size("my"), replicas,
    )
    tokens_in = tok.reshape(slot_rows, D)
    w_gate, w_up, w_down = (
        w.reshape(ep_count * piece_units, D) for w in (w_gate, w_up, w_down)
    )
    gate_proj = jnp.dot(tokens_in, w_gate.T, preferred_element_type=jnp.float32)
    up_proj = jnp.dot(tokens_in, w_up.T, preferred_element_type=jnp.float32)
    hidden = (jax.nn.silu(gate_proj) * up_proj).astype(jnp.bfloat16)
    expert_out = jnp.dot(hidden, w_down, preferred_element_type=jnp.float32)
    expert_out = expert_out.reshape(slot_dev, slot_rows, D)
    summed = lax.psum_scatter(
        expert_out.astype(jnp.bfloat16), "my", scatter_dimension=2, tiled=True
    )
    sent_back = summed.reshape(slot_dev, ep_count, capacity, feat_block)
    sent_back = jnp.transpose(sent_back, (1, 0, 2, 3))
    returned = lax.all_to_all(sent_back, "ep", split_axis=0, concat_axis=0, tiled=True).reshape(
        slot_total * capacity, feat_block
    )
    picked = returned[target].reshape(tok_rows, TOPK, feat_block).astype(jnp.float32)
    weights_norm = gate_probs / jnp.sum(gate_probs, axis=1, keepdims=True)
    mixed = jnp.sum(weights_norm[:, :, None] * picked, axis=1)
    updated = stream_f + mixed
    normed_out = (updated * row_scale(updated)[:, None] * final_gain[None, :]).astype(jnp.bfloat16)
    return (normed_out, updated.astype(jnp.bfloat16))


def solution(mesh):
    placed = (
        P(("ep", "mx"), None),
        P(("ep", "mx"), "my"),
        P(None, "my"),
        P("my"),
        P(None, ("ep", "my"), "mx"),
        P(None, ("ep", "my"), "mx"),
        P(None, ("ep", "my"), "mx"),
        P(("ep", "mx"), None),
        P(("ep", "mx"), None),
        P("my"),
    )
    return jax.shard_map(
        shards,
        mesh=mesh,
        in_specs=placed,
        out_specs=(P(("ep", "mx"), "my"), P(("ep", "mx"), "my")),
        check_vma=False,
    )
```

```python
import functools

import jax
import jax.numpy as jnp
import numpy as np
from jax import lax
from jax.experimental import pallas as pl
from jax.experimental.pallas import tpu as pltpu
from jax.sharding import PartitionSpec as P

D = 2048
EXPERTS = 8
TOPK = 2
MOST = 96


EPSILON = 1e-06
MESH = pl.DeviceIdType.MESH


def remote(src, dst, send, recv, device):
    return pltpu.make_async_remote_copy(
        src_ref=src, dst_ref=dst, send_sem=send, recv_sem=recv,
        device_id=device, device_id_type=MESH,
    )


def move_kernel(n_ep, n_mx, n_my, replicas, packed_ref, gate_ref, up_ref, down_ref,
                tok_ref, gate_out, up_out, down_out, tok_sems, send_z, recv_z, fwd_send, fwd_recv,
                send_x, recv_x, local_sem):
    j = lax.axis_index("ep")
    a = lax.axis_index("mx")
    m = lax.axis_index("my")
    fb = packed_ref.shape[2]
    wb = gate_ref.shape[2]
    cols_m = pl.ds(pl.multiple_of(m * fb, fb), fb)
    cols_a = pl.ds(pl.multiple_of(a * wb, wb), wb)
    pending = []
    tok_local = pltpu.make_async_copy(packed_ref.at[j], tok_ref.at[j, :, cols_m], tok_sems.at[0, 0])
    tok_local.start()
    tok_z = []
    for d in range(1, n_ep):
        t = lax.rem(j + d, n_ep)
        copy = remote(packed_ref.at[t], tok_ref.at[j, :, cols_m], tok_sems.at[1, d], tok_sems.at[2, d], (t, a, m))
        copy.start()
        tok_z.append(copy)
    weights = (gate_ref, up_ref, down_ref)
    outs = (gate_out, up_out, down_out)

    half_ring = n_ep // 2
    side = half_ring - 1
    parity = lax.rem(j, 2)
    partner = j + 1 - 2 * parity

    def start_direct(k):
        local = pltpu.make_async_copy(
            weights[k].at[j // replicas], outs[k].at[j, :, cols_a], local_sem.at[k])
        local.start()
        direct = []
        for d in range(1, side + 1):
            sign = 1 - 2 * lax.rem(j + d, 2)
            t = lax.rem(j + n_ep + sign * d, n_ep)
            copy = remote(weights[k].at[t // replicas], outs[k].at[j, :, cols_a],
                          send_z.at[k, d], recv_z.at[k, d], (t, a, m))
            copy.start()
            direct.append(copy)
        return local, direct

    def start_forward(k):
        forward = []
        for d in range(0, side + 1):
            src = lax.rem(j + n_ep - d + 2 * parity * d, n_ep)
            copy = remote(outs[k].at[src, :, cols_a], outs[k].at[src, :, cols_a],
                          fwd_send.at[k, d], fwd_recv.at[k, d], (partner, a, m))
            copy.start()
            forward.append(copy)
        return forward

    local, direct = start_direct(0)
    tok_local.wait()
    for copy in tok_z:
        copy.wait_recv()
    pending.extend(tok_z)
    tok_my = []
    for e in range(1, n_my):
        b = lax.rem(m + e, n_my)
        copy = remote(tok_ref.at[:, :, cols_m], tok_ref.at[:, :, cols_m], tok_sems.at[3, e], tok_sems.at[4, e], (j, a, b))
        copy.start()
        tok_my.append(copy)
    pending.extend(tok_my)
    x_copies = []
    for k in range(3):
        local.wait()
        for copy in direct:
            copy.wait_recv()
        pending.extend(direct)
        forward = start_forward(k)
        if k + 1 < 3:
            local, direct = start_direct(k + 1)
        for copy in forward:
            copy.wait_recv()
        pending.extend(forward)
        if n_mx == 4:
            right = lax.rem(a + 1, n_mx)
            left = lax.rem(a + n_mx - 1, n_mx)
            half = n_ep // 2
            to_right = remote(outs[k].at[:, :, cols_a], outs[k].at[:, :, cols_a],
                              send_x.at[k, 0], recv_x.at[k, 0], (j, right, m))
            to_left = remote(outs[k].at[:, :, cols_a], outs[k].at[:, :, cols_a],
                             send_x.at[k, 1], recv_x.at[k, 1], (j, left, m))
            to_right.start()
            to_left.start()
            cols_l = pl.ds(pl.multiple_of(left * wb, wb), wb)
            cols_r = pl.ds(pl.multiple_of(right * wb, wb), wb)
            to_right.wait_recv()
            fwd_right = remote(outs[k].at[pl.ds(0, half), :, cols_l], outs[k].at[pl.ds(0, half), :, cols_l],
                               send_x.at[k, 2], recv_x.at[k, 2], (j, right, m))
            fwd_right.start()
            to_left.wait_recv()
            fwd_left = remote(outs[k].at[pl.ds(half, half), :, cols_r], outs[k].at[pl.ds(half, half), :, cols_r],
                              send_x.at[k, 3], recv_x.at[k, 3], (j, left, m))
            fwd_left.start()
            pending.extend([to_right, to_left])
            x_copies.extend([fwd_right, fwd_left])
        else:
            for e in range(1, n_mx):
                b = lax.rem(a + e, n_mx)
                copy = remote(outs[k].at[:, :, cols_a], outs[k].at[:, :, cols_a],
                              send_x.at[k, e], recv_x.at[k, e], (j, b, m))
                copy.start()
                x_copies.append(copy)
    pending.extend(x_copies)
    for copy in pending:
        copy.wait_send()
    for copy in tok_my + x_copies:
        copy.wait_recv()


def move_all(packed, gate_weight, up_weight, down_weight, n_ep, n_mx, n_my, replicas):
    _, rows, fb = packed.shape
    _, units, wb = gate_weight.shape
    return pl.pallas_call(
        functools.partial(move_kernel, n_ep, n_mx, n_my, replicas),
        out_shape=(
            jax.ShapeDtypeStruct((n_ep, rows, n_my * fb), packed.dtype),
        ) + (jax.ShapeDtypeStruct((n_ep, units, n_mx * wb), gate_weight.dtype),) * 3,
        in_specs=[pl.BlockSpec(memory_space=pl.ANY)] * 4,
        out_specs=(pl.BlockSpec(memory_space=pl.ANY),) * 4,
        scratch_shapes=[
            pltpu.SemaphoreType.DMA((5, max(n_ep, n_my))),
            pltpu.SemaphoreType.DMA((3, n_ep)),
            pltpu.SemaphoreType.DMA((3, n_ep)),
            pltpu.SemaphoreType.DMA((3, n_ep)),
            pltpu.SemaphoreType.DMA((3, n_ep)),
            pltpu.SemaphoreType.DMA((3, max(n_mx, 4))),
            pltpu.SemaphoreType.DMA((3, max(n_mx, 4))),
            pltpu.SemaphoreType.DMA((3,)),
        ],
        compiler_params=pltpu.CompilerParams(has_side_effects=True),
    )(packed, gate_weight, up_weight, down_weight)


def row_scale(stream_f):
    partial_sq = jnp.sum(stream_f * stream_f, axis=1)
    row_total = lax.psum(partial_sq, "my")
    return lax.rsqrt(row_total / D + EPSILON)


def shards(
    context,
    resid_in,
    out_weight,
    norm_gain,
    gate_weight,
    up_weight,
    down_weight,
    routes,
    gate_probs,
    final_gain,
):
    ep_count = lax.axis_size("ep")
    slot_dev = max(1, EXPERTS // ep_count)
    slot_total = slot_dev * ep_count
    replicas = slot_total // EXPERTS
    capacity = MOST // replicas
    tok_rows = context.shape[0]
    feat_block = resid_in.shape[1]
    piece_units = gate_weight.shape[1]
    slot_rows = ep_count * capacity

    projected = jnp.dot(context, out_weight, preferred_element_type=jnp.float32)
    stream = (projected + resid_in.astype(jnp.float32)).astype(jnp.bfloat16)
    stream_f = stream.astype(jnp.float32)
    normed = (stream_f * row_scale(stream_f)[:, None] * norm_gain[None, :]).astype(jnp.bfloat16)
    chosen = routes.reshape(-1)
    onehot = (chosen[:, None] == jnp.arange(EXPERTS, dtype=jnp.int32)[None, :]).astype(jnp.int32)
    before = jnp.cumsum(onehot, axis=0) - onehot
    ranking = jnp.sum(before * onehot, axis=1)
    slot_index = chosen * replicas + ranking % replicas
    target = slot_index * capacity + ranking // replicas
    row_ids = jnp.arange(tok_rows * TOPK, dtype=jnp.int32) // TOPK
    source = jnp.full((slot_total * capacity,), tok_rows, jnp.int32).at[target].set(row_ids)
    padded = jnp.concatenate([normed, jnp.zeros((1, feat_block), jnp.bfloat16)], axis=0)
    packed = padded[source].reshape(ep_count, capacity, feat_block)
    tok, w_gate, w_up, w_down = move_all(
        packed, gate_weight, up_weight, down_weight,
        ep_count, lax.axis_size("mx"), lax.axis_size("my"), replicas,
    )
    tokens_in = tok.reshape(slot_rows, D)
    gate_proj = jnp.einsum("rd,spd->rsp", tokens_in, w_gate, preferred_element_type=jnp.float32)
    up_proj = jnp.einsum("rd,spd->rsp", tokens_in, w_up, preferred_element_type=jnp.float32)
    hidden = (jax.nn.silu(gate_proj) * up_proj).astype(jnp.bfloat16)
    expert_out = jnp.einsum("rsp,spd->rd", hidden, w_down, preferred_element_type=jnp.float32)
    expert_out = expert_out.reshape(slot_dev, slot_rows, D)
    summed = lax.psum_scatter(
        expert_out.astype(jnp.bfloat16), "my", scatter_dimension=2, tiled=True
    )
    sent_back = summed.reshape(slot_dev, ep_count, capacity, feat_block)
    sent_back = jnp.transpose(sent_back, (1, 0, 2, 3))
    returned = lax.all_to_all(sent_back, "ep", split_axis=0, concat_axis=0, tiled=True).reshape(
        slot_total * capacity, feat_block
    )
    picked = returned[target].reshape(tok_rows, TOPK, feat_block).astype(jnp.float32)
    weights_norm = gate_probs / jnp.sum(gate_probs, axis=1, keepdims=True)
    mixed = jnp.sum(weights_norm[:, :, None] * picked, axis=1)
    updated = stream_f + mixed
    normed_out = (updated * row_scale(updated)[:, None] * final_gain[None, :]).astype(jnp.bfloat16)
    return (normed_out, updated.astype(jnp.bfloat16))


def solution(mesh):
    placed = (
        P(("ep", "mx"), None),
        P(("ep", "mx"), "my"),
        P(None, "my"),
        P("my"),
        P(None, ("ep", "my"), "mx"),
        P(None, ("ep", "my"), "mx"),
        P(None, ("ep", "my"), "mx"),
        P(("ep", "mx"), None),
        P(("ep", "mx"), None),
        P("my"),
    )
    return jax.shard_map(
        shards,
        mesh=mesh,
        in_specs=placed,
        out_specs=(P(("ep", "mx"), "my"), P(("ep", "mx"), "my")),
        check_vma=False,
    )
```

```python
import functools

import jax
import jax.numpy as jnp
import numpy as np
from jax import lax
from jax.experimental import pallas as pl
from jax.experimental.pallas import tpu as pltpu
from jax.sharding import PartitionSpec as P

D = 2048
EXPERTS = 8
TOPK = 2
MOST = 96


EPSILON = 1e-06
MESH = pl.DeviceIdType.MESH


def remote(src, dst, send, recv, device):
    return pltpu.make_async_remote_copy(
        src_ref=src, dst_ref=dst, send_sem=send, recv_sem=recv,
        device_id=device, device_id_type=MESH,
    )


def move_kernel(n_ep, n_mx, n_my, replicas, packed_ref, gate_ref, up_ref, down_ref,
                tok_ref, gate_out, up_out, down_out, tok_sems, send_z, recv_z, fwd_send, fwd_recv,
                send_x, recv_x, local_sem):
    j = lax.axis_index("ep")
    a = lax.axis_index("mx")
    m = lax.axis_index("my")
    fb = packed_ref.shape[2]
    wb = gate_ref.shape[2]
    cols_m = pl.ds(pl.multiple_of(m * fb, fb), fb)
    cols_a = pl.ds(pl.multiple_of(a * wb, wb), wb)
    pending = []
    tok_local = pltpu.make_async_copy(packed_ref.at[j], tok_ref.at[j, :, cols_m], tok_sems.at[0, 0])
    tok_local.start()
    tok_z = []
    for d in range(1, n_ep):
        t = lax.rem(j + d, n_ep)
        copy = remote(packed_ref.at[t], tok_ref.at[j, :, cols_m], tok_sems.at[1, d], tok_sems.at[2, d], (t, a, m))
        copy.start()
        tok_z.append(copy)
    weights = (gate_ref, up_ref, down_ref)
    outs = (gate_out, up_out, down_out)

    half_ring = n_ep // 2
    side = half_ring - 1
    parity = lax.rem(j, 2)
    partner = j + 1 - 2 * parity

    def start_direct(k):
        local = pltpu.make_async_copy(
            weights[k].at[j // replicas], outs[k].at[j, :, cols_a], local_sem.at[k])
        local.start()
        direct = []
        for d in range(1, side + 1):
            sign = 1 - 2 * lax.rem(j + d, 2)
            t = lax.rem(j + n_ep + sign * d, n_ep)
            copy = remote(weights[k].at[t // replicas], outs[k].at[j, :, cols_a],
                          send_z.at[k, d], recv_z.at[k, d], (t, a, m))
            copy.start()
            direct.append(copy)
        return local, direct

    def start_forward(k):
        forward = []
        for d in range(0, side + 1):
            src = lax.rem(j + n_ep - d + 2 * parity * d, n_ep)
            copy = remote(outs[k].at[src, :, cols_a], outs[k].at[src, :, cols_a],
                          fwd_send.at[k, d], fwd_recv.at[k, d], (partner, a, m))
            copy.start()
            forward.append(copy)
        return forward

    local, direct = start_direct(0)
    tok_local.wait()
    for copy in tok_z:
        copy.wait_recv()
    pending.extend(tok_z)
    tok_my = []
    for e in range(1, n_my):
        b = lax.rem(m + e, n_my)
        copy = remote(tok_ref.at[:, :, cols_m], tok_ref.at[:, :, cols_m], tok_sems.at[3, e], tok_sems.at[4, e], (j, a, b))
        copy.start()
        tok_my.append(copy)
    pending.extend(tok_my)
    x_copies = []
    for k in range(3):
        local.wait()
        for copy in direct:
            copy.wait_recv()
        pending.extend(direct)
        forward = start_forward(k)
        if k + 1 < 3:
            local, direct = start_direct(k + 1)
        for copy in forward:
            copy.wait_recv()
        pending.extend(forward)
        if n_mx == 4:
            right = lax.rem(a + 1, n_mx)
            left = lax.rem(a + n_mx - 1, n_mx)
            half = n_ep // 2
            to_right = remote(outs[k].at[:, :, cols_a], outs[k].at[:, :, cols_a],
                              send_x.at[k, 0], recv_x.at[k, 0], (j, right, m))
            to_left = remote(outs[k].at[:, :, cols_a], outs[k].at[:, :, cols_a],
                             send_x.at[k, 1], recv_x.at[k, 1], (j, left, m))
            to_right.start()
            to_left.start()
            cols_l = pl.ds(pl.multiple_of(left * wb, wb), wb)
            cols_r = pl.ds(pl.multiple_of(right * wb, wb), wb)
            to_right.wait_recv()
            fwd_right = remote(outs[k].at[pl.ds(0, half), :, cols_l], outs[k].at[pl.ds(0, half), :, cols_l],
                               send_x.at[k, 2], recv_x.at[k, 2], (j, right, m))
            fwd_right.start()
            to_left.wait_recv()
            fwd_left = remote(outs[k].at[pl.ds(half, half), :, cols_r], outs[k].at[pl.ds(half, half), :, cols_r],
                              send_x.at[k, 3], recv_x.at[k, 3], (j, left, m))
            fwd_left.start()
            pending.extend([to_right, to_left])
            x_copies.extend([fwd_right, fwd_left])
        else:
            for e in range(1, n_mx):
                b = lax.rem(a + e, n_mx)
                copy = remote(outs[k].at[:, :, cols_a], outs[k].at[:, :, cols_a],
                              send_x.at[k, e], recv_x.at[k, e], (j, b, m))
                copy.start()
                x_copies.append(copy)
    pending.extend(x_copies)
    for copy in pending:
        copy.wait_send()
    for copy in tok_my + x_copies:
        copy.wait_recv()


def move_all(packed, gate_weight, up_weight, down_weight, n_ep, n_mx, n_my, replicas):
    _, rows, fb = packed.shape
    _, units, wb = gate_weight.shape
    return pl.pallas_call(
        functools.partial(move_kernel, n_ep, n_mx, n_my, replicas),
        out_shape=(
            jax.ShapeDtypeStruct((n_ep, rows, n_my * fb), packed.dtype),
        ) + (jax.ShapeDtypeStruct((n_ep, units, n_mx * wb), gate_weight.dtype),) * 3,
        in_specs=[pl.BlockSpec(memory_space=pl.ANY)] * 4,
        out_specs=(pl.BlockSpec(memory_space=pl.ANY),) * 4,
        scratch_shapes=[
            pltpu.SemaphoreType.DMA((5, max(n_ep, n_my))),
            pltpu.SemaphoreType.DMA((3, n_ep)),
            pltpu.SemaphoreType.DMA((3, n_ep)),
            pltpu.SemaphoreType.DMA((3, n_ep)),
            pltpu.SemaphoreType.DMA((3, n_ep)),
            pltpu.SemaphoreType.DMA((3, max(n_mx, 4))),
            pltpu.SemaphoreType.DMA((3, max(n_mx, 4))),
            pltpu.SemaphoreType.DMA((3,)),
        ],
        compiler_params=pltpu.CompilerParams(has_side_effects=True),
    )(packed, gate_weight, up_weight, down_weight)


def sum_kernel(n_my, x_ref, o_ref, slots, send, recv):
    j = lax.axis_index("ep")
    a = lax.axis_index("mx")
    m = lax.axis_index("my")
    slots[m] = x_ref[...]
    copies = []
    for e in range(1, n_my):
        b = lax.rem(m + e, n_my)
        copy = remote(x_ref, slots.at[m], send.at[e], recv.at[e], (j, a, b))
        copy.start()
        copies.append(copy)
    for copy in copies:
        copy.wait_send()
    for copy in copies:
        copy.wait_recv()
    o_ref[...] = jnp.sum(slots[...], axis=0)


def sum_over_my(values):
    n_my = lax.axis_size("my")
    row = values.reshape(1, -1)
    total = pl.pallas_call(
        functools.partial(sum_kernel, n_my),
        out_shape=jax.ShapeDtypeStruct(row.shape, row.dtype),
        in_specs=[pl.BlockSpec(memory_space=pltpu.VMEM)],
        out_specs=pl.BlockSpec(memory_space=pltpu.VMEM),
        scratch_shapes=[
            pltpu.VMEM((n_my,) + row.shape, row.dtype),
            pltpu.SemaphoreType.DMA((n_my,)),
            pltpu.SemaphoreType.DMA((n_my,)),
        ],
        compiler_params=pltpu.CompilerParams(has_side_effects=True),
    )(row)
    return total.reshape(values.shape)


def row_scale(stream_f):
    partial_sq = jnp.sum(stream_f * stream_f, axis=1)
    row_total = sum_over_my(partial_sq)
    return lax.rsqrt(row_total / D + EPSILON)


def shards(
    context,
    resid_in,
    out_weight,
    norm_gain,
    gate_weight,
    up_weight,
    down_weight,
    routes,
    gate_probs,
    final_gain,
):
    ep_count = lax.axis_size("ep")
    slot_dev = max(1, EXPERTS // ep_count)
    slot_total = slot_dev * ep_count
    replicas = slot_total // EXPERTS
    capacity = MOST // replicas
    tok_rows = context.shape[0]
    feat_block = resid_in.shape[1]
    piece_units = gate_weight.shape[1]
    slot_rows = ep_count * capacity

    projected = jnp.dot(context, out_weight, preferred_element_type=jnp.float32)
    stream = (projected + resid_in.astype(jnp.float32)).astype(jnp.bfloat16)
    stream_f = stream.astype(jnp.float32)
    normed = (stream_f * row_scale(stream_f)[:, None] * norm_gain[None, :]).astype(jnp.bfloat16)
    chosen = routes.reshape(-1)
    onehot = (chosen[:, None] == jnp.arange(EXPERTS, dtype=jnp.int32)[None, :]).astype(jnp.int32)
    before = jnp.cumsum(onehot, axis=0) - onehot
    ranking = jnp.sum(before * onehot, axis=1)
    slot_index = chosen * replicas + ranking % replicas
    target = slot_index * capacity + ranking // replicas
    row_ids = jnp.arange(tok_rows * TOPK, dtype=jnp.int32) // TOPK
    source = jnp.full((slot_total * capacity,), tok_rows, jnp.int32).at[target].set(row_ids)
    padded = jnp.concatenate([normed, jnp.zeros((1, feat_block), jnp.bfloat16)], axis=0)
    packed = padded[source].reshape(ep_count, capacity, feat_block)
    tok, w_gate, w_up, w_down = move_all(
        packed, gate_weight, up_weight, down_weight,
        ep_count, lax.axis_size("mx"), lax.axis_size("my"), replicas,
    )
    tokens_in = tok.reshape(slot_rows, D)
    gate_proj = jnp.einsum("rd,spd->rsp", tokens_in, w_gate, preferred_element_type=jnp.float32)
    up_proj = jnp.einsum("rd,spd->rsp", tokens_in, w_up, preferred_element_type=jnp.float32)
    hidden = (jax.nn.silu(gate_proj) * up_proj).astype(jnp.bfloat16)
    expert_out = jnp.einsum("rsp,spd->rd", hidden, w_down, preferred_element_type=jnp.float32)
    expert_out = expert_out.reshape(slot_dev, slot_rows, D)
    summed = lax.psum_scatter(
        expert_out.astype(jnp.bfloat16), "my", scatter_dimension=2, tiled=True
    )
    sent_back = summed.reshape(slot_dev, ep_count, capacity, feat_block)
    sent_back = jnp.transpose(sent_back, (1, 0, 2, 3))
    returned = lax.all_to_all(sent_back, "ep", split_axis=0, concat_axis=0, tiled=True).reshape(
        slot_total * capacity, feat_block
    )
    picked = returned[target].reshape(tok_rows, TOPK, feat_block).astype(jnp.float32)
    weights_norm = gate_probs / jnp.sum(gate_probs, axis=1, keepdims=True)
    mixed = jnp.sum(weights_norm[:, :, None] * picked, axis=1)
    updated = stream_f + mixed
    normed_out = (updated * row_scale(updated)[:, None] * final_gain[None, :]).astype(jnp.bfloat16)
    return (normed_out, updated.astype(jnp.bfloat16))


def solution(mesh):
    placed = (
        P(("ep", "mx"), None),
        P(("ep", "mx"), "my"),
        P(None, "my"),
        P("my"),
        P(None, ("ep", "my"), "mx"),
        P(None, ("ep", "my"), "mx"),
        P(None, ("ep", "my"), "mx"),
        P(("ep", "mx"), None),
        P(("ep", "mx"), None),
        P("my"),
    )
    return jax.shard_map(
        shards,
        mesh=mesh,
        in_specs=placed,
        out_specs=(P(("ep", "mx"), "my"), P(("ep", "mx"), "my")),
        check_vma=False,
    )
```

```python
import functools

import jax
import jax.numpy as jnp
import numpy as np
from jax import lax
from jax.experimental import pallas as pl
from jax.experimental.pallas import tpu as pltpu
from jax.sharding import PartitionSpec as P

D = 2048
EXPERTS = 8
TOPK = 2
MOST = 96


EPSILON = 1e-06
MESH = pl.DeviceIdType.MESH


def remote(src, dst, send, recv, device):
    return pltpu.make_async_remote_copy(
        src_ref=src, dst_ref=dst, send_sem=send, recv_sem=recv,
        device_id=device, device_id_type=MESH,
    )


def move_kernel(n_ep, n_mx, n_my, replicas, packed_ref, gate_ref, up_ref, down_ref,
                tok_ref, gate_out, up_out, down_out, tok_sems, send_z, recv_z, fwd_send, fwd_recv,
                send_x, recv_x, local_sem):
    j = lax.axis_index("ep")
    a = lax.axis_index("mx")
    m = lax.axis_index("my")
    fb = packed_ref.shape[2]
    wb = gate_ref.shape[2]
    cols_m = pl.ds(pl.multiple_of(m * fb, fb), fb)
    cols_a = pl.ds(pl.multiple_of(a * wb, wb), wb)
    pending = []
    tok_local = pltpu.make_async_copy(packed_ref.at[j], tok_ref.at[j, :, cols_m], tok_sems.at[0, 0])
    tok_local.start()
    tok_z = []
    for d in range(1, n_ep):
        t = lax.rem(j + d, n_ep)
        copy = remote(packed_ref.at[t], tok_ref.at[j, :, cols_m], tok_sems.at[1, d], tok_sems.at[2, d], (t, a, m))
        copy.start()
        tok_z.append(copy)
    weights = (gate_ref, up_ref, down_ref)
    outs = (gate_out, up_out, down_out)

    half_ring = n_ep // 2
    side = half_ring - 1
    parity = lax.rem(j, 2)
    partner = j + 1 - 2 * parity

    def start_direct(k):
        local = pltpu.make_async_copy(
            weights[k].at[j // replicas], outs[k].at[j, :, cols_a], local_sem.at[k])
        local.start()
        direct = []
        for d in range(1, side + 1):
            sign = 1 - 2 * lax.rem(j + d, 2)
            t = lax.rem(j + n_ep + sign * d, n_ep)
            copy = remote(weights[k].at[t // replicas], outs[k].at[j, :, cols_a],
                          send_z.at[k, d], recv_z.at[k, d], (t, a, m))
            copy.start()
            direct.append(copy)
        return local, direct

    def start_forward(k):
        forward = []
        for d in range(0, side + 1):
            src = lax.rem(j + n_ep - d + 2 * parity * d, n_ep)
            copy = remote(outs[k].at[src, :, cols_a], outs[k].at[src, :, cols_a],
                          fwd_send.at[k, d], fwd_recv.at[k, d], (partner, a, m))
            copy.start()
            forward.append(copy)
        return forward

    local, direct = start_direct(0)
    tok_local.wait()
    for copy in tok_z:
        copy.wait_recv()
    pending.extend(tok_z)
    tok_my = []
    for e in range(1, n_my):
        b = lax.rem(m + e, n_my)
        copy = remote(tok_ref.at[:, :, cols_m], tok_ref.at[:, :, cols_m], tok_sems.at[3, e], tok_sems.at[4, e], (j, a, b))
        copy.start()
        tok_my.append(copy)
    pending.extend(tok_my)
    x_copies = []
    for k in range(3):
        local.wait()
        for copy in direct:
            copy.wait_recv()
        pending.extend(direct)
        forward = start_forward(k)
        if k + 1 < 3:
            local, direct = start_direct(k + 1)
        for copy in forward:
            copy.wait_recv()
        pending.extend(forward)
        if n_mx == 4:
            right = lax.rem(a + 1, n_mx)
            left = lax.rem(a + n_mx - 1, n_mx)
            half = n_ep // 2
            to_right = remote(outs[k].at[:, :, cols_a], outs[k].at[:, :, cols_a],
                              send_x.at[k, 0], recv_x.at[k, 0], (j, right, m))
            to_left = remote(outs[k].at[:, :, cols_a], outs[k].at[:, :, cols_a],
                             send_x.at[k, 1], recv_x.at[k, 1], (j, left, m))
            to_right.start()
            to_left.start()
            cols_l = pl.ds(pl.multiple_of(left * wb, wb), wb)
            cols_r = pl.ds(pl.multiple_of(right * wb, wb), wb)
            to_right.wait_recv()
            fwd_right = remote(outs[k].at[pl.ds(0, half), :, cols_l], outs[k].at[pl.ds(0, half), :, cols_l],
                               send_x.at[k, 2], recv_x.at[k, 2], (j, right, m))
            fwd_right.start()
            to_left.wait_recv()
            fwd_left = remote(outs[k].at[pl.ds(half, half), :, cols_r], outs[k].at[pl.ds(half, half), :, cols_r],
                              send_x.at[k, 3], recv_x.at[k, 3], (j, left, m))
            fwd_left.start()
            pending.extend([to_right, to_left])
            x_copies.extend([fwd_right, fwd_left])
        else:
            for e in range(1, n_mx):
                b = lax.rem(a + e, n_mx)
                copy = remote(outs[k].at[:, :, cols_a], outs[k].at[:, :, cols_a],
                              send_x.at[k, e], recv_x.at[k, e], (j, b, m))
                copy.start()
                x_copies.append(copy)
    pending.extend(x_copies)
    for copy in pending:
        copy.wait_send()
    for copy in tok_my + x_copies:
        copy.wait_recv()


def move_all(packed, gate_weight, up_weight, down_weight, n_ep, n_mx, n_my, replicas):
    _, rows, fb = packed.shape
    _, units, wb = gate_weight.shape
    return pl.pallas_call(
        functools.partial(move_kernel, n_ep, n_mx, n_my, replicas),
        out_shape=(
            jax.ShapeDtypeStruct((n_ep, rows, n_my * fb), packed.dtype),
        ) + (jax.ShapeDtypeStruct((n_ep, units, n_mx * wb), gate_weight.dtype),) * 3,
        in_specs=[pl.BlockSpec(memory_space=pl.ANY)] * 4,
        out_specs=(pl.BlockSpec(memory_space=pl.ANY),) * 4,
        scratch_shapes=[
            pltpu.SemaphoreType.DMA((5, max(n_ep, n_my))),
            pltpu.SemaphoreType.DMA((3, n_ep)),
            pltpu.SemaphoreType.DMA((3, n_ep)),
            pltpu.SemaphoreType.DMA((3, n_ep)),
            pltpu.SemaphoreType.DMA((3, n_ep)),
            pltpu.SemaphoreType.DMA((3, max(n_mx, 4))),
            pltpu.SemaphoreType.DMA((3, max(n_mx, 4))),
            pltpu.SemaphoreType.DMA((3,)),
        ],
        compiler_params=pltpu.CompilerParams(has_side_effects=True),
    )(packed, gate_weight, up_weight, down_weight)


def back_kernel(n_ep, n_my, ex_ref, out_ref, rx_core, chip_part, rx_y, result, sems):
    j = lax.axis_index("ep")
    a = lax.axis_index("mx")
    m = lax.axis_index("my")
    fb = out_ref.shape[2]
    cap = out_ref.shape[1]
    chips = n_my // 2
    core = lax.rem(m, 2)
    y = m // 2
    partner = m + 1 - 2 * core
    barrier = pltpu.get_barrier_semaphore()
    peers = [(j, a, partner)]
    peers += [(j, a, lax.rem(y + e, chips) * 2 + core) for e in range(1, chips)]
    peers += [(lax.rem(j + d, n_ep), a, m) for d in range(1, n_ep)]
    for peer in peers:
        pl.semaphore_signal(barrier, inc=1, device_id=peer, device_id_type=MESH)
    pl.semaphore_wait(barrier, len(peers))

    def cols(block):
        return pl.ds(pl.multiple_of(block * fb, fb), fb)

    to_core = []
    for i in range(chips):
        copy = remote(ex_ref.at[:, cols(1 - core + 2 * i)], rx_core.at[i],
                      sems.at[0, i], sems.at[1, i], (j, a, partner))
        copy.start()
        to_core.append(copy)
    for copy in to_core:
        copy.wait_recv()
    for i in range(chips):
        own = ex_ref[:, cols(core + 2 * i)].astype(jnp.float32)
        chip_part[i] = (own + rx_core[i].astype(jnp.float32)).astype(chip_part.dtype)
    to_y = []
    for e in range(1, chips):
        other = lax.rem(y + e, chips)
        copy = remote(chip_part.at[other], rx_y.at[e - 1],
                      sems.at[2, e], sems.at[3, e], (j, a, other * 2 + core))
        copy.start()
        to_y.append(copy)
    for copy in to_y:
        copy.wait_recv()
    total = chip_part[y].astype(jnp.float32)
    for e in range(1, chips):
        total = total + rx_y[e - 1].astype(jnp.float32)
    result[...] = total.astype(result.dtype)
    local = pltpu.make_async_copy(result.at[pl.ds(j * cap, cap)], out_ref.at[j], sems.at[4, 0])
    local.start()
    to_z = []
    for d in range(1, n_ep):
        t = lax.rem(j + d, n_ep)
        copy = remote(result.at[pl.ds(t * cap, cap)], out_ref.at[j],
                      sems.at[5, d], sems.at[6, d], (t, a, m))
        copy.start()
        to_z.append(copy)
    local.wait()
    for copy in to_core + to_y + to_z:
        copy.wait_send()
    for copy in to_z:
        copy.wait_recv()


def send_back(ex, n_ep, n_my, cap):
    rows, width = ex.shape
    fb = width // n_my
    return pl.pallas_call(
        functools.partial(back_kernel, n_ep, n_my),
        out_shape=jax.ShapeDtypeStruct((n_ep, cap, fb), ex.dtype),
        in_specs=[pl.BlockSpec(memory_space=pltpu.VMEM)],
        out_specs=pl.BlockSpec(memory_space=pl.ANY),
        scratch_shapes=[
            pltpu.VMEM((n_my // 2, rows, fb), ex.dtype),
            pltpu.VMEM((n_my // 2, rows, fb), ex.dtype),
            pltpu.VMEM((n_my // 2 - 1, rows, fb), ex.dtype),
            pltpu.VMEM((rows, fb), ex.dtype),
            pltpu.SemaphoreType.DMA((7, max(n_ep, n_my))),
        ],
        compiler_params=pltpu.CompilerParams(has_side_effects=True, collective_id=1),
    )(ex)


def row_scale(stream_f):
    partial_sq = jnp.sum(stream_f * stream_f, axis=1)
    row_total = lax.psum(partial_sq, "my")
    return lax.rsqrt(row_total / D + EPSILON)


def shards(
    context,
    resid_in,
    out_weight,
    norm_gain,
    gate_weight,
    up_weight,
    down_weight,
    routes,
    gate_probs,
    final_gain,
):
    ep_count = lax.axis_size("ep")
    slot_dev = max(1, EXPERTS // ep_count)
    slot_total = slot_dev * ep_count
    replicas = slot_total // EXPERTS
    capacity = MOST // replicas
    tok_rows = context.shape[0]
    feat_block = resid_in.shape[1]
    piece_units = gate_weight.shape[1]
    slot_rows = ep_count * capacity

    projected = jnp.dot(context, out_weight, preferred_element_type=jnp.float32)
    stream = (projected + resid_in.astype(jnp.float32)).astype(jnp.bfloat16)
    stream_f = stream.astype(jnp.float32)
    normed = (stream_f * row_scale(stream_f)[:, None] * norm_gain[None, :]).astype(jnp.bfloat16)
    chosen = routes.reshape(-1)
    onehot = (chosen[:, None] == jnp.arange(EXPERTS, dtype=jnp.int32)[None, :]).astype(jnp.int32)
    before = jnp.cumsum(onehot, axis=0) - onehot
    ranking = jnp.sum(before * onehot, axis=1)
    slot_index = chosen * replicas + ranking % replicas
    target = slot_index * capacity + ranking // replicas
    row_ids = jnp.arange(tok_rows * TOPK, dtype=jnp.int32) // TOPK
    source = jnp.full((slot_total * capacity,), tok_rows, jnp.int32).at[target].set(row_ids)
    padded = jnp.concatenate([normed, jnp.zeros((1, feat_block), jnp.bfloat16)], axis=0)
    packed = padded[source].reshape(ep_count, capacity, feat_block)
    tok, w_gate, w_up, w_down = move_all(
        packed, gate_weight, up_weight, down_weight,
        ep_count, lax.axis_size("mx"), lax.axis_size("my"), replicas,
    )
    tokens_in = tok.reshape(slot_rows, D)
    gate_proj = jnp.einsum("rd,spd->rsp", tokens_in, w_gate, preferred_element_type=jnp.float32)
    up_proj = jnp.einsum("rd,spd->rsp", tokens_in, w_up, preferred_element_type=jnp.float32)
    hidden = (jax.nn.silu(gate_proj) * up_proj).astype(jnp.bfloat16)
    expert_out = jnp.einsum("rsp,spd->rd", hidden, w_down, preferred_element_type=jnp.float32)
    expert_out = expert_out.reshape(slot_dev, slot_rows, D)
    returned = send_back(
        expert_out.reshape(slot_rows, D).astype(jnp.bfloat16), ep_count, lax.axis_size("my"), capacity
    ).reshape(slot_total * capacity, feat_block)
    picked = returned[target].reshape(tok_rows, TOPK, feat_block).astype(jnp.float32)
    weights_norm = gate_probs / jnp.sum(gate_probs, axis=1, keepdims=True)
    mixed = jnp.sum(weights_norm[:, :, None] * picked, axis=1)
    updated = stream_f + mixed
    normed_out = (updated * row_scale(updated)[:, None] * final_gain[None, :]).astype(jnp.bfloat16)
    return (normed_out, updated.astype(jnp.bfloat16))


def solution(mesh):
    placed = (
        P(("ep", "mx"), None),
        P(("ep", "mx"), "my"),
        P(None, "my"),
        P("my"),
        P(None, ("ep", "my"), "mx"),
        P(None, ("ep", "my"), "mx"),
        P(None, ("ep", "my"), "mx"),
        P(("ep", "mx"), None),
        P(("ep", "mx"), None),
        P("my"),
    )
    return jax.shard_map(
        shards,
        mesh=mesh,
        in_specs=placed,
        out_specs=(P(("ep", "mx"), "my"), P(("ep", "mx"), "my")),
        check_vma=False,
    )
```

```python
import functools

import jax
import jax.numpy as jnp
import numpy as np
from jax import lax
from jax.experimental import pallas as pl
from jax.experimental.pallas import tpu as pltpu
from jax.sharding import PartitionSpec as P

D = 2048
EXPERTS = 8
TOPK = 2
MOST = 96


EPSILON = 1e-06
MESH = pl.DeviceIdType.MESH


def remote(src, dst, send, recv, device):
    return pltpu.make_async_remote_copy(
        src_ref=src, dst_ref=dst, send_sem=send, recv_sem=recv,
        device_id=device, device_id_type=MESH,
    )


def move_kernel(n_ep, n_mx, n_my, replicas, packed_ref, gate_ref, up_ref, down_ref,
                tok_ref, gate_out, up_out, down_out, tok_sems, send_z, recv_z, fwd_send, fwd_recv,
                send_x, recv_x, local_sem):
    j = lax.axis_index("ep")
    a = lax.axis_index("mx")
    m = lax.axis_index("my")
    fb = packed_ref.shape[2]
    wb = gate_ref.shape[2]
    cols_m = pl.ds(pl.multiple_of(m * fb, fb), fb)
    cols_a = pl.ds(pl.multiple_of(a * wb, wb), wb)
    barrier = pltpu.get_barrier_semaphore()
    peers = [(lax.rem(j + d, n_ep), a, m) for d in range(1, n_ep)]
    peers += [(j, lax.rem(a + e, n_mx), m) for e in range(1, n_mx)]
    peers += [(j, a, lax.rem(m + e, n_my)) for e in range(1, n_my)]
    for peer in peers:
        pl.semaphore_signal(barrier, inc=1, device_id=peer, device_id_type=MESH)
    pl.semaphore_wait(barrier, len(peers))
    pending = []
    tok_local = pltpu.make_async_copy(packed_ref.at[j], tok_ref.at[j, :, cols_m], tok_sems.at[0, 0])
    tok_local.start()
    tok_z = []
    for d in range(1, n_ep):
        t = lax.rem(j + d, n_ep)
        copy = remote(packed_ref.at[t], tok_ref.at[j, :, cols_m], tok_sems.at[1, d], tok_sems.at[2, d], (t, a, m))
        copy.start()
        tok_z.append(copy)
    weights = (gate_ref, up_ref, down_ref)
    outs = (gate_out, up_out, down_out)

    half_ring = n_ep // 2
    side = half_ring - 1
    parity = lax.rem(j, 2)
    partner = j + 1 - 2 * parity

    def start_direct(k):
        local = pltpu.make_async_copy(
            weights[k].at[j // replicas], outs[k].at[j, :, cols_a], local_sem.at[k])
        local.start()
        direct = []
        for d in range(1, side + 1):
            sign = 1 - 2 * lax.rem(j + d, 2)
            t = lax.rem(j + n_ep + sign * d, n_ep)
            copy = remote(weights[k].at[t // replicas], outs[k].at[j, :, cols_a],
                          send_z.at[k, d], recv_z.at[k, d], (t, a, m))
            copy.start()
            direct.append(copy)
        return local, direct

    def start_forward(k):
        forward = []
        for d in range(0, side + 1):
            src = lax.rem(j + n_ep - d + 2 * parity * d, n_ep)
            copy = remote(outs[k].at[src, :, cols_a], outs[k].at[src, :, cols_a],
                          fwd_send.at[k, d], fwd_recv.at[k, d], (partner, a, m))
            copy.start()
            forward.append(copy)
        return forward

    local, direct = start_direct(0)
    tok_local.wait()
    for copy in tok_z:
        copy.wait_recv()
    pending.extend(tok_z)
    tok_my = []
    for e in range(1, n_my):
        b = lax.rem(m + e, n_my)
        copy = remote(tok_ref.at[:, :, cols_m], tok_ref.at[:, :, cols_m], tok_sems.at[3, e], tok_sems.at[4, e], (j, a, b))
        copy.start()
        tok_my.append(copy)
    pending.extend(tok_my)
    x_copies = []
    for k in range(3):
        local.wait()
        for copy in direct:
            copy.wait_recv()
        pending.extend(direct)
        forward = start_forward(k)
        if k + 1 < 3:
            local, direct = start_direct(k + 1)
        for copy in forward:
            copy.wait_recv()
        pending.extend(forward)
        if n_mx == 4:
            right = lax.rem(a + 1, n_mx)
            left = lax.rem(a + n_mx - 1, n_mx)
            half = n_ep // 2
            to_right = remote(outs[k].at[:, :, cols_a], outs[k].at[:, :, cols_a],
                              send_x.at[k, 0], recv_x.at[k, 0], (j, right, m))
            to_left = remote(outs[k].at[:, :, cols_a], outs[k].at[:, :, cols_a],
                             send_x.at[k, 1], recv_x.at[k, 1], (j, left, m))
            to_right.start()
            to_left.start()
            cols_l = pl.ds(pl.multiple_of(left * wb, wb), wb)
            cols_r = pl.ds(pl.multiple_of(right * wb, wb), wb)
            to_right.wait_recv()
            fwd_right = remote(outs[k].at[pl.ds(0, half), :, cols_l], outs[k].at[pl.ds(0, half), :, cols_l],
                               send_x.at[k, 2], recv_x.at[k, 2], (j, right, m))
            fwd_right.start()
            to_left.wait_recv()
            fwd_left = remote(outs[k].at[pl.ds(half, half), :, cols_r], outs[k].at[pl.ds(half, half), :, cols_r],
                              send_x.at[k, 3], recv_x.at[k, 3], (j, left, m))
            fwd_left.start()
            pending.extend([to_right, to_left])
            x_copies.extend([fwd_right, fwd_left])
        else:
            for e in range(1, n_mx):
                b = lax.rem(a + e, n_mx)
                copy = remote(outs[k].at[:, :, cols_a], outs[k].at[:, :, cols_a],
                              send_x.at[k, e], recv_x.at[k, e], (j, b, m))
                copy.start()
                x_copies.append(copy)
    pending.extend(x_copies)
    for copy in pending:
        copy.wait_send()
    for copy in tok_my + x_copies:
        copy.wait_recv()


def move_all(packed, gate_weight, up_weight, down_weight, n_ep, n_mx, n_my, replicas):
    _, rows, fb = packed.shape
    _, units, wb = gate_weight.shape
    return pl.pallas_call(
        functools.partial(move_kernel, n_ep, n_mx, n_my, replicas),
        out_shape=(
            jax.ShapeDtypeStruct((n_ep, rows, n_my * fb), packed.dtype),
        ) + (jax.ShapeDtypeStruct((n_ep, units, n_mx * wb), gate_weight.dtype),) * 3,
        in_specs=[pl.BlockSpec(memory_space=pl.ANY)] * 4,
        out_specs=(pl.BlockSpec(memory_space=pl.ANY),) * 4,
        scratch_shapes=[
            pltpu.SemaphoreType.DMA((5, max(n_ep, n_my))),
            pltpu.SemaphoreType.DMA((3, n_ep)),
            pltpu.SemaphoreType.DMA((3, n_ep)),
            pltpu.SemaphoreType.DMA((3, n_ep)),
            pltpu.SemaphoreType.DMA((3, n_ep)),
            pltpu.SemaphoreType.DMA((3, max(n_mx, 4))),
            pltpu.SemaphoreType.DMA((3, max(n_mx, 4))),
            pltpu.SemaphoreType.DMA((3,)),
        ],
        compiler_params=pltpu.CompilerParams(has_side_effects=True, collective_id=0),
    )(packed, gate_weight, up_weight, down_weight)


def back_kernel(n_ep, n_my, ex_ref, out_ref, rx_core, chip_part, rx_y, result, sems):
    j = lax.axis_index("ep")
    a = lax.axis_index("mx")
    m = lax.axis_index("my")
    fb = out_ref.shape[2]
    cap = out_ref.shape[1]
    chips = n_my // 2
    core = lax.rem(m, 2)
    y = m // 2
    partner = m + 1 - 2 * core
    barrier = pltpu.get_barrier_semaphore()
    peers = [(j, a, partner)]
    peers += [(j, a, lax.rem(y + e, chips) * 2 + core) for e in range(1, chips)]
    peers += [(lax.rem(j + d, n_ep), a, m) for d in range(1, n_ep)]
    for peer in peers:
        pl.semaphore_signal(barrier, inc=1, device_id=peer, device_id_type=MESH)
    pl.semaphore_wait(barrier, len(peers))

    def cols(block):
        return pl.ds(pl.multiple_of(block * fb, fb), fb)

    to_core = []
    for i in range(chips):
        copy = remote(ex_ref.at[:, cols(1 - core + 2 * i)], rx_core.at[i],
                      sems.at[0, i], sems.at[1, i], (j, a, partner))
        copy.start()
        to_core.append(copy)
    for copy in to_core:
        copy.wait_recv()
    for i in range(chips):
        own = ex_ref[:, cols(core + 2 * i)].astype(jnp.float32)
        chip_part[i] = (own + rx_core[i].astype(jnp.float32)).astype(chip_part.dtype)
    to_y = []
    for e in range(1, chips):
        other = lax.rem(y + e, chips)
        copy = remote(chip_part.at[other], rx_y.at[e - 1],
                      sems.at[2, e], sems.at[3, e], (j, a, other * 2 + core))
        copy.start()
        to_y.append(copy)
    for copy in to_y:
        copy.wait_recv()
    total = chip_part[y].astype(jnp.float32)
    for e in range(1, chips):
        total = total + rx_y[e - 1].astype(jnp.float32)
    result[...] = total.astype(result.dtype)
    local = pltpu.make_async_copy(result.at[pl.ds(j * cap, cap)], out_ref.at[j], sems.at[4, 0])
    local.start()
    to_z = []
    for d in range(1, n_ep):
        t = lax.rem(j + d, n_ep)
        copy = remote(result.at[pl.ds(t * cap, cap)], out_ref.at[j],
                      sems.at[5, d], sems.at[6, d], (t, a, m))
        copy.start()
        to_z.append(copy)
    local.wait()
    for copy in to_core + to_y + to_z:
        copy.wait_send()
    for copy in to_z:
        copy.wait_recv()


def send_back(ex, n_ep, n_my, cap):
    rows, width = ex.shape
    fb = width // n_my
    return pl.pallas_call(
        functools.partial(back_kernel, n_ep, n_my),
        out_shape=jax.ShapeDtypeStruct((n_ep, cap, fb), ex.dtype),
        in_specs=[pl.BlockSpec(memory_space=pltpu.VMEM)],
        out_specs=pl.BlockSpec(memory_space=pl.ANY),
        scratch_shapes=[
            pltpu.VMEM((n_my // 2, rows, fb), ex.dtype),
            pltpu.VMEM((n_my // 2, rows, fb), ex.dtype),
            pltpu.VMEM((n_my // 2 - 1, rows, fb), ex.dtype),
            pltpu.VMEM((rows, fb), ex.dtype),
            pltpu.SemaphoreType.DMA((7, max(n_ep, n_my))),
        ],
        compiler_params=pltpu.CompilerParams(has_side_effects=True, collective_id=1),
    )(ex)


def row_scale(stream_f):
    partial_sq = jnp.sum(stream_f * stream_f, axis=1)
    row_total = lax.psum(partial_sq, "my")
    return lax.rsqrt(row_total / D + EPSILON)


def shards(
    context,
    resid_in,
    out_weight,
    norm_gain,
    gate_weight,
    up_weight,
    down_weight,
    routes,
    gate_probs,
    final_gain,
):
    ep_count = lax.axis_size("ep")
    slot_dev = max(1, EXPERTS // ep_count)
    slot_total = slot_dev * ep_count
    replicas = slot_total // EXPERTS
    capacity = MOST // replicas
    tok_rows = context.shape[0]
    feat_block = resid_in.shape[1]
    piece_units = gate_weight.shape[1]
    slot_rows = ep_count * capacity

    projected = jnp.dot(context, out_weight, preferred_element_type=jnp.float32)
    stream = (projected + resid_in.astype(jnp.float32)).astype(jnp.bfloat16)
    stream_f = stream.astype(jnp.float32)
    normed = (stream_f * row_scale(stream_f)[:, None] * norm_gain[None, :]).astype(jnp.bfloat16)
    chosen = routes.reshape(-1)
    onehot = (chosen[:, None] == jnp.arange(EXPERTS, dtype=jnp.int32)[None, :]).astype(jnp.int32)
    before = jnp.cumsum(onehot, axis=0) - onehot
    ranking = jnp.sum(before * onehot, axis=1)
    slot_index = chosen * replicas + ranking % replicas
    target = slot_index * capacity + ranking // replicas
    row_ids = jnp.arange(tok_rows * TOPK, dtype=jnp.int32) // TOPK
    source = jnp.full((slot_total * capacity,), tok_rows, jnp.int32).at[target].set(row_ids)
    padded = jnp.concatenate([normed, jnp.zeros((1, feat_block), jnp.bfloat16)], axis=0)
    packed = padded[source].reshape(ep_count, capacity, feat_block)
    tok, w_gate, w_up, w_down = move_all(
        packed, gate_weight, up_weight, down_weight,
        ep_count, lax.axis_size("mx"), lax.axis_size("my"), replicas,
    )
    tokens_in = tok.reshape(slot_rows, D)
    gate_proj = jnp.einsum("rd,spd->rsp", tokens_in, w_gate, preferred_element_type=jnp.float32)
    up_proj = jnp.einsum("rd,spd->rsp", tokens_in, w_up, preferred_element_type=jnp.float32)
    hidden = (jax.nn.silu(gate_proj) * up_proj).astype(jnp.bfloat16)
    expert_out = jnp.einsum("rsp,spd->rd", hidden, w_down, preferred_element_type=jnp.float32)
    expert_out = expert_out.reshape(slot_dev, slot_rows, D)
    returned = send_back(
        expert_out.reshape(slot_rows, D).astype(jnp.bfloat16), ep_count, lax.axis_size("my"), capacity
    ).reshape(slot_total * capacity, feat_block)
    picked = returned[target].reshape(tok_rows, TOPK, feat_block).astype(jnp.float32)
    weights_norm = gate_probs / jnp.sum(gate_probs, axis=1, keepdims=True)
    mixed = jnp.sum(weights_norm[:, :, None] * picked, axis=1)
    updated = stream_f + mixed
    normed_out = (updated * row_scale(updated)[:, None] * final_gain[None, :]).astype(jnp.bfloat16)
    return (normed_out, updated.astype(jnp.bfloat16))


def solution(mesh):
    placed = (
        P(("ep", "mx"), None),
        P(("ep", "mx"), "my"),
        P(None, "my"),
        P("my"),
        P(None, ("ep", "my"), "mx"),
        P(None, ("ep", "my"), "mx"),
        P(None, ("ep", "my"), "mx"),
        P(("ep", "mx"), None),
        P(("ep", "mx"), None),
        P("my"),
    )
    return jax.shard_map(
        shards,
        mesh=mesh,
        in_specs=placed,
        out_specs=(P(("ep", "mx"), "my"), P(("ep", "mx"), "my")),
        check_vma=False,
    )
```

```python
import functools

import jax
import jax.numpy as jnp
import numpy as np
from jax import lax
from jax.experimental import pallas as pl
from jax.experimental.pallas import tpu as pltpu
from jax.sharding import PartitionSpec as P

D = 2048
EXPERTS = 8
TOPK = 2
MOST = 96


EPSILON = 1e-06
MESH = pl.DeviceIdType.MESH


def remote(src, dst, send, recv, device):
    return pltpu.make_async_remote_copy(
        src_ref=src, dst_ref=dst, send_sem=send, recv_sem=recv,
        device_id=device, device_id_type=MESH,
    )


def move_kernel(n_ep, n_mx, n_my, replicas, packed_ref, gate_ref, up_ref, down_ref,
                tok_ref, gate_out, up_out, down_out, tok_sems, send_z, recv_z, fwd_send, fwd_recv,
                send_x, recv_x, local_sem):
    j = lax.axis_index("ep")
    a = lax.axis_index("mx")
    m = lax.axis_index("my")
    fb = packed_ref.shape[2]
    wb = gate_ref.shape[2]
    cols_m = pl.ds(pl.multiple_of(m * fb, fb), fb)
    cols_a = pl.ds(pl.multiple_of(a * wb, wb), wb)
    barrier = pltpu.get_barrier_semaphore()
    peers = [(lax.rem(j + d, n_ep), a, m) for d in range(1, n_ep)]
    peers += [(j, lax.rem(a + e, n_mx), m) for e in range(1, n_mx)]
    peers += [(j, a, lax.rem(m + e, n_my)) for e in range(1, n_my)]
    for peer in peers:
        pl.semaphore_signal(barrier, inc=1, device_id=peer, device_id_type=MESH)
    pl.semaphore_wait(barrier, len(peers))
    pending = []
    tok_local = pltpu.make_async_copy(packed_ref.at[j], tok_ref.at[j, :, cols_m], tok_sems.at[0, 0])
    tok_local.start()
    tok_z = []
    for d in range(1, n_ep):
        t = lax.rem(j + d, n_ep)
        copy = remote(packed_ref.at[t], tok_ref.at[j, :, cols_m], tok_sems.at[1, d], tok_sems.at[2, d], (t, a, m))
        copy.start()
        tok_z.append(copy)
    weights = (gate_ref, up_ref, down_ref)
    outs = (gate_out, up_out, down_out)

    half_ring = n_ep // 2
    side = half_ring - 1
    parity = lax.rem(j, 2)
    partner = j + 1 - 2 * parity

    def start_direct(k):
        local = pltpu.make_async_copy(
            weights[k].at[j // replicas], outs[k].at[j, :, cols_a], local_sem.at[k])
        local.start()
        direct = []
        for d in range(1, side + 1):
            sign = 1 - 2 * lax.rem(j + d, 2)
            t = lax.rem(j + n_ep + sign * d, n_ep)
            copy = remote(weights[k].at[t // replicas], outs[k].at[j, :, cols_a],
                          send_z.at[k, d], recv_z.at[k, d], (t, a, m))
            copy.start()
            direct.append(copy)
        return local, direct

    def start_forward(k):
        forward = []
        for d in range(0, side + 1):
            src = lax.rem(j + n_ep - d + 2 * parity * d, n_ep)
            copy = remote(outs[k].at[src, :, cols_a], outs[k].at[src, :, cols_a],
                          fwd_send.at[k, d], fwd_recv.at[k, d], (partner, a, m))
            copy.start()
            forward.append(copy)
        return forward

    local, direct = start_direct(0)
    tok_local.wait()
    for copy in tok_z:
        copy.wait_recv()
    pending.extend(tok_z)
    tok_my = []
    for e in range(1, n_my):
        b = lax.rem(m + e, n_my)
        copy = remote(tok_ref.at[:, :, cols_m], tok_ref.at[:, :, cols_m], tok_sems.at[3, e], tok_sems.at[4, e], (j, a, b))
        copy.start()
        tok_my.append(copy)
    pending.extend(tok_my)
    x_copies = []
    for k in range(3):
        local.wait()
        for copy in direct:
            copy.wait_recv()
        pending.extend(direct)
        forward = start_forward(k)
        if k + 1 < 3:
            local, direct = start_direct(k + 1)
        for copy in forward:
            copy.wait_recv()
        pending.extend(forward)
        if n_mx == 4:
            right = lax.rem(a + 1, n_mx)
            left = lax.rem(a + n_mx - 1, n_mx)
            half = n_ep // 2
            to_right = remote(outs[k].at[:, :, cols_a], outs[k].at[:, :, cols_a],
                              send_x.at[k, 0], recv_x.at[k, 0], (j, right, m))
            to_left = remote(outs[k].at[:, :, cols_a], outs[k].at[:, :, cols_a],
                             send_x.at[k, 1], recv_x.at[k, 1], (j, left, m))
            to_right.start()
            to_left.start()
            cols_l = pl.ds(pl.multiple_of(left * wb, wb), wb)
            cols_r = pl.ds(pl.multiple_of(right * wb, wb), wb)
            to_right.wait_recv()
            fwd_right = remote(outs[k].at[pl.ds(0, half), :, cols_l], outs[k].at[pl.ds(0, half), :, cols_l],
                               send_x.at[k, 2], recv_x.at[k, 2], (j, right, m))
            fwd_right.start()
            to_left.wait_recv()
            fwd_left = remote(outs[k].at[pl.ds(half, half), :, cols_r], outs[k].at[pl.ds(half, half), :, cols_r],
                              send_x.at[k, 3], recv_x.at[k, 3], (j, left, m))
            fwd_left.start()
            pending.extend([to_right, to_left])
            x_copies.extend([fwd_right, fwd_left])
        else:
            for e in range(1, n_mx):
                b = lax.rem(a + e, n_mx)
                copy = remote(outs[k].at[:, :, cols_a], outs[k].at[:, :, cols_a],
                              send_x.at[k, e], recv_x.at[k, e], (j, b, m))
                copy.start()
                x_copies.append(copy)
    pending.extend(x_copies)
    for copy in pending:
        copy.wait_send()
    for copy in tok_my + x_copies:
        copy.wait_recv()


def move_all(packed, gate_weight, up_weight, down_weight, n_ep, n_mx, n_my, replicas):
    _, rows, fb = packed.shape
    _, units, wb = gate_weight.shape
    return pl.pallas_call(
        functools.partial(move_kernel, n_ep, n_mx, n_my, replicas),
        out_shape=(
            jax.ShapeDtypeStruct((n_ep, rows, n_my * fb), packed.dtype),
        ) + (jax.ShapeDtypeStruct((n_ep, units, n_mx * wb), gate_weight.dtype),) * 3,
        in_specs=[pl.BlockSpec(memory_space=pl.ANY)] * 4,
        out_specs=(pl.BlockSpec(memory_space=pl.ANY),) * 4,
        scratch_shapes=[
            pltpu.SemaphoreType.DMA((5, max(n_ep, n_my))),
            pltpu.SemaphoreType.DMA((3, n_ep)),
            pltpu.SemaphoreType.DMA((3, n_ep)),
            pltpu.SemaphoreType.DMA((3, n_ep)),
            pltpu.SemaphoreType.DMA((3, n_ep)),
            pltpu.SemaphoreType.DMA((3, max(n_mx, 4))),
            pltpu.SemaphoreType.DMA((3, max(n_mx, 4))),
            pltpu.SemaphoreType.DMA((3,)),
        ],
        compiler_params=pltpu.CompilerParams(has_side_effects=True, collective_id=0),
    )(packed, gate_weight, up_weight, down_weight)


def back_kernel(n_ep, n_my, ex_ref, out_ref, rx_core, chip_part, rx_y, result, sems):
    j = lax.axis_index("ep")
    a = lax.axis_index("mx")
    m = lax.axis_index("my")
    fb = out_ref.shape[2]
    cap = out_ref.shape[1]
    chips = n_my // 2
    core = lax.rem(m, 2)
    y = m // 2
    partner = m + 1 - 2 * core
    barrier = pltpu.get_barrier_semaphore()
    peers = [(j, a, partner)]
    peers += [(j, a, lax.rem(y + e, chips) * 2 + core) for e in range(1, chips)]
    peers += [(lax.rem(j + d, n_ep), a, m) for d in range(1, n_ep)]
    for peer in peers:
        pl.semaphore_signal(barrier, inc=1, device_id=peer, device_id_type=MESH)
    pl.semaphore_wait(barrier, len(peers))

    def cols(block):
        return pl.ds(pl.multiple_of(block * fb, fb), fb)

    to_core = []
    for i in range(chips):
        copy = remote(ex_ref.at[:, cols(1 - core + 2 * i)], rx_core.at[i],
                      sems.at[0, i], sems.at[1, i], (j, a, partner))
        copy.start()
        to_core.append(copy)
    for copy in to_core:
        copy.wait_recv()
    for i in range(chips):
        own = ex_ref[:, cols(core + 2 * i)].astype(jnp.float32)
        chip_part[i] = (own + rx_core[i].astype(jnp.float32)).astype(chip_part.dtype)
    to_y = []
    for e in range(1, chips):
        other = lax.rem(y + e, chips)
        copy = remote(chip_part.at[other], rx_y.at[e - 1],
                      sems.at[2, e], sems.at[3, e], (j, a, other * 2 + core))
        copy.start()
        to_y.append(copy)
    for copy in to_y:
        copy.wait_recv()
    total = chip_part[y].astype(jnp.float32)
    for e in range(1, chips):
        total = total + rx_y[e - 1].astype(jnp.float32)
    result[...] = total.astype(result.dtype)
    local = pltpu.make_async_copy(result.at[pl.ds(j * cap, cap)], out_ref.at[j], sems.at[4, 0])
    local.start()
    to_z = []
    for d in range(1, n_ep):
        t = lax.rem(j + d, n_ep)
        copy = remote(result.at[pl.ds(t * cap, cap)], out_ref.at[j],
                      sems.at[5, d], sems.at[6, d], (t, a, m))
        copy.start()
        to_z.append(copy)
    local.wait()
    for copy in to_core + to_y + to_z:
        copy.wait_send()
    for copy in to_z:
        copy.wait_recv()


def send_back(ex, n_ep, n_my, cap):
    rows, width = ex.shape
    fb = width // n_my
    return pl.pallas_call(
        functools.partial(back_kernel, n_ep, n_my),
        out_shape=jax.ShapeDtypeStruct((n_ep, cap, fb), ex.dtype),
        in_specs=[pl.BlockSpec(memory_space=pltpu.VMEM)],
        out_specs=pl.BlockSpec(memory_space=pl.ANY),
        scratch_shapes=[
            pltpu.VMEM((n_my // 2, rows, fb), ex.dtype),
            pltpu.VMEM((n_my // 2, rows, fb), ex.dtype),
            pltpu.VMEM((n_my // 2 - 1, rows, fb), ex.dtype),
            pltpu.VMEM((rows, fb), ex.dtype),
            pltpu.SemaphoreType.DMA((7, max(n_ep, n_my))),
        ],
        compiler_params=pltpu.CompilerParams(has_side_effects=True, collective_id=1),
    )(ex)


def sum_kernel(n_my, x_ref, o_ref, slots, send, recv):
    j = lax.axis_index("ep")
    a = lax.axis_index("mx")
    m = lax.axis_index("my")
    barrier = pltpu.get_barrier_semaphore()
    for e in range(1, n_my):
        pl.semaphore_signal(barrier, inc=1, device_id=(j, a, lax.rem(m + e, n_my)), device_id_type=MESH)
    pl.semaphore_wait(barrier, n_my - 1)
    slots[m] = x_ref[...]
    copies = []
    for e in range(1, n_my):
        b = lax.rem(m + e, n_my)
        copy = remote(x_ref, slots.at[m], send.at[e], recv.at[e], (j, a, b))
        copy.start()
        copies.append(copy)
    for copy in copies:
        copy.wait_send()
    for copy in copies:
        copy.wait_recv()
    o_ref[...] = jnp.sum(slots[...], axis=0)


def sum_over_my(values, kernel_id):
    n_my = lax.axis_size("my")
    row = values.reshape(1, -1)
    total = pl.pallas_call(
        functools.partial(sum_kernel, n_my),
        out_shape=jax.ShapeDtypeStruct(row.shape, row.dtype),
        in_specs=[pl.BlockSpec(memory_space=pltpu.VMEM)],
        out_specs=pl.BlockSpec(memory_space=pltpu.VMEM),
        scratch_shapes=[
            pltpu.VMEM((n_my,) + row.shape, row.dtype),
            pltpu.SemaphoreType.DMA((n_my,)),
            pltpu.SemaphoreType.DMA((n_my,)),
        ],
        compiler_params=pltpu.CompilerParams(has_side_effects=True, collective_id=kernel_id),
    )(row)
    return total.reshape(values.shape)


def row_scale(stream_f, kernel_id):
    partial_sq = jnp.sum(stream_f * stream_f, axis=1)
    row_total = sum_over_my(partial_sq, kernel_id)
    return lax.rsqrt(row_total / D + EPSILON)


def shards(
    context,
    resid_in,
    out_weight,
    norm_gain,
    gate_weight,
    up_weight,
    down_weight,
    routes,
    gate_probs,
    final_gain,
):
    ep_count = lax.axis_size("ep")
    slot_dev = max(1, EXPERTS // ep_count)
    slot_total = slot_dev * ep_count
    replicas = slot_total // EXPERTS
    capacity = MOST // replicas
    tok_rows = context.shape[0]
    feat_block = resid_in.shape[1]
    piece_units = gate_weight.shape[1]
    slot_rows = ep_count * capacity

    projected = jnp.dot(context, out_weight, preferred_element_type=jnp.float32)
    stream = (projected + resid_in.astype(jnp.float32)).astype(jnp.bfloat16)
    stream_f = stream.astype(jnp.float32)
    normed = (stream_f * row_scale(stream_f, 2)[:, None] * norm_gain[None, :]).astype(jnp.bfloat16)
    chosen = routes.reshape(-1)
    onehot = (chosen[:, None] == jnp.arange(EXPERTS, dtype=jnp.int32)[None, :]).astype(jnp.int32)
    before = jnp.cumsum(onehot, axis=0) - onehot
    ranking = jnp.sum(before * onehot, axis=1)
    slot_index = chosen * replicas + ranking % replicas
    target = slot_index * capacity + ranking // replicas
    row_ids = jnp.arange(tok_rows * TOPK, dtype=jnp.int32) // TOPK
    source = jnp.full((slot_total * capacity,), tok_rows, jnp.int32).at[target].set(row_ids)
    padded = jnp.concatenate([normed, jnp.zeros((1, feat_block), jnp.bfloat16)], axis=0)
    packed = padded[source].reshape(ep_count, capacity, feat_block)
    tok, w_gate, w_up, w_down = move_all(
        packed, gate_weight, up_weight, down_weight,
        ep_count, lax.axis_size("mx"), lax.axis_size("my"), replicas,
    )
    tokens_in = tok.reshape(slot_rows, D)
    gate_proj = jnp.einsum("rd,spd->rsp", tokens_in, w_gate, preferred_element_type=jnp.float32)
    up_proj = jnp.einsum("rd,spd->rsp", tokens_in, w_up, preferred_element_type=jnp.float32)
    hidden = (jax.nn.silu(gate_proj) * up_proj).astype(jnp.bfloat16)
    expert_out = jnp.einsum("rsp,spd->rd", hidden, w_down, preferred_element_type=jnp.float32)
    expert_out = expert_out.reshape(slot_dev, slot_rows, D)
    returned = send_back(
        expert_out.reshape(slot_rows, D).astype(jnp.bfloat16), ep_count, lax.axis_size("my"), capacity
    ).reshape(slot_total * capacity, feat_block)
    picked = returned[target].reshape(tok_rows, TOPK, feat_block).astype(jnp.float32)
    weights_norm = gate_probs / jnp.sum(gate_probs, axis=1, keepdims=True)
    mixed = jnp.sum(weights_norm[:, :, None] * picked, axis=1)
    updated = stream_f + mixed
    normed_out = (updated * row_scale(updated, 3)[:, None] * final_gain[None, :]).astype(jnp.bfloat16)
    return (normed_out, updated.astype(jnp.bfloat16))


def solution(mesh):
    placed = (
        P(("ep", "mx"), None),
        P(("ep", "mx"), "my"),
        P(None, "my"),
        P("my"),
        P(None, ("ep", "my"), "mx"),
        P(None, ("ep", "my"), "mx"),
        P(None, ("ep", "my"), "mx"),
        P(("ep", "mx"), None),
        P(("ep", "mx"), None),
        P("my"),
    )
    return jax.shard_map(
        shards,
        mesh=mesh,
        in_specs=placed,
        out_specs=(P(("ep", "mx"), "my"), P(("ep", "mx"), "my")),
        check_vma=False,
    )
```

```python
import functools

import jax
import jax.numpy as jnp
import numpy as np
from jax import lax
from jax.experimental import pallas as pl
from jax.experimental.pallas import tpu as pltpu
from jax.sharding import PartitionSpec as P

D = 2048
EXPERTS = 8
TOPK = 2
MOST = 96


EPSILON = 1e-06
MESH = pl.DeviceIdType.MESH


def remote(src, dst, send, recv, device):
    return pltpu.make_async_remote_copy(
        src_ref=src, dst_ref=dst, send_sem=send, recv_sem=recv,
        device_id=device, device_id_type=MESH,
    )


def move_kernel(n_ep, n_mx, n_my, replicas, packed_ref, gate_ref, up_ref, down_ref,
                tok_ref, gate_out, up_out, down_out, tok_sems, send_z, recv_z, fwd_send, fwd_recv,
                send_x, recv_x, local_sem):
    j = lax.axis_index("ep")
    a = lax.axis_index("mx")
    m = lax.axis_index("my")
    fb = packed_ref.shape[2]
    wb = gate_ref.shape[2]
    cols_m = pl.ds(pl.multiple_of(m * fb, fb), fb)
    cols_a = pl.ds(pl.multiple_of(a * wb, wb), wb)
    barrier = pltpu.get_barrier_semaphore()
    peers = [(lax.rem(j + d, n_ep), a, m) for d in range(1, n_ep)]
    peers += [(j, lax.rem(a + e, n_mx), m) for e in range(1, n_mx)]
    peers += [(j, a, lax.rem(m + e, n_my)) for e in range(1, n_my)]
    for peer in peers:
        pl.semaphore_signal(barrier, inc=1, device_id=peer, device_id_type=MESH)
    pl.semaphore_wait(barrier, len(peers))
    pending = []
    weights = (gate_ref, up_ref, down_ref)
    outs = (gate_out, up_out, down_out)

    half_ring = n_ep // 2
    side = half_ring - 1
    parity = lax.rem(j, 2)
    partner = j + 1 - 2 * parity

    def start_direct(k):
        local = pltpu.make_async_copy(
            weights[k].at[j // replicas], outs[k].at[j, :, cols_a], local_sem.at[k])
        local.start()
        direct = []
        for d in range(1, side + 1):
            sign = 1 - 2 * lax.rem(j + d, 2)
            t = lax.rem(j + n_ep + sign * d, n_ep)
            copy = remote(weights[k].at[t // replicas], outs[k].at[j, :, cols_a],
                          send_z.at[k, d], recv_z.at[k, d], (t, a, m))
            copy.start()
            direct.append(copy)
        return local, direct

    def start_forward(k):
        forward = []
        for d in range(0, side + 1):
            src = lax.rem(j + n_ep - d + 2 * parity * d, n_ep)
            copy = remote(outs[k].at[src, :, cols_a], outs[k].at[src, :, cols_a],
                          fwd_send.at[k, d], fwd_recv.at[k, d], (partner, a, m))
            copy.start()
            forward.append(copy)
        return forward

    local, direct = start_direct(0)
    tok_local = pltpu.make_async_copy(packed_ref.at[j], tok_ref.at[j, :, cols_m], tok_sems.at[0, 0])
    tok_local.start()
    tok_z = []
    for d in range(1, n_ep):
        t = lax.rem(j + d, n_ep)
        copy = remote(packed_ref.at[t], tok_ref.at[j, :, cols_m], tok_sems.at[1, d], tok_sems.at[2, d], (t, a, m))
        copy.start()
        tok_z.append(copy)
    tok_my = []
    x_copies = []
    for k in range(3):
        local.wait()
        for copy in direct:
            copy.wait_recv()
        pending.extend(direct)
        forward = start_forward(k)
        if k + 1 < 3:
            local, direct = start_direct(k + 1)
        for copy in forward:
            copy.wait_recv()
        pending.extend(forward)
        if n_mx == 4:
            right = lax.rem(a + 1, n_mx)
            left = lax.rem(a + n_mx - 1, n_mx)
            half = n_ep // 2
            to_right = remote(outs[k].at[:, :, cols_a], outs[k].at[:, :, cols_a],
                              send_x.at[k, 0], recv_x.at[k, 0], (j, right, m))
            to_left = remote(outs[k].at[:, :, cols_a], outs[k].at[:, :, cols_a],
                             send_x.at[k, 1], recv_x.at[k, 1], (j, left, m))
            to_right.start()
            to_left.start()
            cols_l = pl.ds(pl.multiple_of(left * wb, wb), wb)
            cols_r = pl.ds(pl.multiple_of(right * wb, wb), wb)
            to_right.wait_recv()
            fwd_right = remote(outs[k].at[pl.ds(0, half), :, cols_l], outs[k].at[pl.ds(0, half), :, cols_l],
                               send_x.at[k, 2], recv_x.at[k, 2], (j, right, m))
            fwd_right.start()
            to_left.wait_recv()
            fwd_left = remote(outs[k].at[pl.ds(half, half), :, cols_r], outs[k].at[pl.ds(half, half), :, cols_r],
                              send_x.at[k, 3], recv_x.at[k, 3], (j, left, m))
            fwd_left.start()
            pending.extend([to_right, to_left])
            x_copies.extend([fwd_right, fwd_left])
        else:
            for e in range(1, n_mx):
                b = lax.rem(a + e, n_mx)
                copy = remote(outs[k].at[:, :, cols_a], outs[k].at[:, :, cols_a],
                              send_x.at[k, e], recv_x.at[k, e], (j, b, m))
                copy.start()
                x_copies.append(copy)
        if k == 0:
            tok_local.wait()
            for copy in tok_z:
                copy.wait_recv()
            pending.extend(tok_z)
            for e in range(1, n_my):
                b = lax.rem(m + e, n_my)
                copy = remote(tok_ref.at[:, :, cols_m], tok_ref.at[:, :, cols_m], tok_sems.at[3, e], tok_sems.at[4, e], (j, a, b))
                copy.start()
                tok_my.append(copy)
            pending.extend(tok_my)
    pending.extend(x_copies)
    for copy in pending:
        copy.wait_send()
    for copy in tok_my + x_copies:
        copy.wait_recv()


def move_all(packed, gate_weight, up_weight, down_weight, n_ep, n_mx, n_my, replicas):
    _, rows, fb = packed.shape
    _, units, wb = gate_weight.shape
    return pl.pallas_call(
        functools.partial(move_kernel, n_ep, n_mx, n_my, replicas),
        out_shape=(
            jax.ShapeDtypeStruct((n_ep, rows, n_my * fb), packed.dtype),
        ) + (jax.ShapeDtypeStruct((n_ep, units, n_mx * wb), gate_weight.dtype),) * 3,
        in_specs=[pl.BlockSpec(memory_space=pl.ANY)] * 4,
        out_specs=(pl.BlockSpec(memory_space=pl.ANY),) * 4,
        scratch_shapes=[
            pltpu.SemaphoreType.DMA((5, max(n_ep, n_my))),
            pltpu.SemaphoreType.DMA((3, n_ep)),
            pltpu.SemaphoreType.DMA((3, n_ep)),
            pltpu.SemaphoreType.DMA((3, n_ep)),
            pltpu.SemaphoreType.DMA((3, n_ep)),
            pltpu.SemaphoreType.DMA((3, max(n_mx, 4))),
            pltpu.SemaphoreType.DMA((3, max(n_mx, 4))),
            pltpu.SemaphoreType.DMA((3,)),
        ],
        compiler_params=pltpu.CompilerParams(has_side_effects=True, collective_id=0),
    )(packed, gate_weight, up_weight, down_weight)


def back_kernel(n_ep, n_my, ex_ref, out_ref, rx_core, chip_part, rx_y, result, sems):
    j = lax.axis_index("ep")
    a = lax.axis_index("mx")
    m = lax.axis_index("my")
    fb = out_ref.shape[2]
    cap = out_ref.shape[1]
    chips = n_my // 2
    core = lax.rem(m, 2)
    y = m // 2
    partner = m + 1 - 2 * core
    barrier = pltpu.get_barrier_semaphore()
    peers = [(j, a, partner)]
    peers += [(j, a, lax.rem(y + e, chips) * 2 + core) for e in range(1, chips)]
    peers += [(lax.rem(j + d, n_ep), a, m) for d in range(1, n_ep)]
    for peer in peers:
        pl.semaphore_signal(barrier, inc=1, device_id=peer, device_id_type=MESH)
    pl.semaphore_wait(barrier, len(peers))

    def cols(block):
        return pl.ds(pl.multiple_of(block * fb, fb), fb)

    to_core = []
    for i in range(chips):
        copy = remote(ex_ref.at[:, cols(1 - core + 2 * i)], rx_core.at[i],
                      sems.at[0, i], sems.at[1, i], (j, a, partner))
        copy.start()
        to_core.append(copy)
    for copy in to_core:
        copy.wait_recv()
    for i in range(chips):
        own = ex_ref[:, cols(core + 2 * i)].astype(jnp.float32)
        chip_part[i] = (own + rx_core[i].astype(jnp.float32)).astype(chip_part.dtype)
    to_y = []
    for e in range(1, chips):
        other = lax.rem(y + e, chips)
        copy = remote(chip_part.at[other], rx_y.at[e - 1],
                      sems.at[2, e], sems.at[3, e], (j, a, other * 2 + core))
        copy.start()
        to_y.append(copy)
    for copy in to_y:
        copy.wait_recv()
    total = chip_part[y].astype(jnp.float32)
    for e in range(1, chips):
        total = total + rx_y[e - 1].astype(jnp.float32)
    result[...] = total.astype(result.dtype)
    local = pltpu.make_async_copy(result.at[pl.ds(j * cap, cap)], out_ref.at[j], sems.at[4, 0])
    local.start()
    to_z = []
    for d in range(1, n_ep):
        t = lax.rem(j + d, n_ep)
        copy = remote(result.at[pl.ds(t * cap, cap)], out_ref.at[j],
                      sems.at[5, d], sems.at[6, d], (t, a, m))
        copy.start()
        to_z.append(copy)
    local.wait()
    for copy in to_core + to_y + to_z:
        copy.wait_send()
    for copy in to_z:
        copy.wait_recv()


def send_back(ex, n_ep, n_my, cap):
    rows, width = ex.shape
    fb = width // n_my
    return pl.pallas_call(
        functools.partial(back_kernel, n_ep, n_my),
        out_shape=jax.ShapeDtypeStruct((n_ep, cap, fb), ex.dtype),
        in_specs=[pl.BlockSpec(memory_space=pltpu.VMEM)],
        out_specs=pl.BlockSpec(memory_space=pl.ANY),
        scratch_shapes=[
            pltpu.VMEM((n_my // 2, rows, fb), ex.dtype),
            pltpu.VMEM((n_my // 2, rows, fb), ex.dtype),
            pltpu.VMEM((n_my // 2 - 1, rows, fb), ex.dtype),
            pltpu.VMEM((rows, fb), ex.dtype),
            pltpu.SemaphoreType.DMA((7, max(n_ep, n_my))),
        ],
        compiler_params=pltpu.CompilerParams(has_side_effects=True, collective_id=1),
    )(ex)


def sum_kernel(n_my, x_ref, o_ref, slots, send, recv):
    j = lax.axis_index("ep")
    a = lax.axis_index("mx")
    m = lax.axis_index("my")
    barrier = pltpu.get_barrier_semaphore()
    for e in range(1, n_my):
        pl.semaphore_signal(barrier, inc=1, device_id=(j, a, lax.rem(m + e, n_my)), device_id_type=MESH)
    pl.semaphore_wait(barrier, n_my - 1)
    slots[m] = x_ref[...]
    copies = []
    for e in range(1, n_my):
        b = lax.rem(m + e, n_my)
        copy = remote(x_ref, slots.at[m], send.at[e], recv.at[e], (j, a, b))
        copy.start()
        copies.append(copy)
    for copy in copies:
        copy.wait_send()
    for copy in copies:
        copy.wait_recv()
    o_ref[...] = jnp.sum(slots[...], axis=0)


def sum_over_my(values, kernel_id):
    n_my = lax.axis_size("my")
    row = values.reshape(1, -1)
    total = pl.pallas_call(
        functools.partial(sum_kernel, n_my),
        out_shape=jax.ShapeDtypeStruct(row.shape, row.dtype),
        in_specs=[pl.BlockSpec(memory_space=pltpu.VMEM)],
        out_specs=pl.BlockSpec(memory_space=pltpu.VMEM),
        scratch_shapes=[
            pltpu.VMEM((n_my,) + row.shape, row.dtype),
            pltpu.SemaphoreType.DMA((n_my,)),
            pltpu.SemaphoreType.DMA((n_my,)),
        ],
        compiler_params=pltpu.CompilerParams(has_side_effects=True, collective_id=kernel_id),
    )(row)
    return total.reshape(values.shape)


def row_scale(stream_f, kernel_id):
    partial_sq = jnp.sum(stream_f * stream_f, axis=1)
    row_total = sum_over_my(partial_sq, kernel_id)
    return lax.rsqrt(row_total / D + EPSILON)


def shards(
    context,
    resid_in,
    out_weight,
    norm_gain,
    gate_weight,
    up_weight,
    down_weight,
    routes,
    gate_probs,
    final_gain,
):
    ep_count = lax.axis_size("ep")
    slot_dev = max(1, EXPERTS // ep_count)
    slot_total = slot_dev * ep_count
    replicas = slot_total // EXPERTS
    capacity = MOST // replicas
    tok_rows = context.shape[0]
    feat_block = resid_in.shape[1]
    piece_units = gate_weight.shape[1]
    slot_rows = ep_count * capacity

    projected = jnp.dot(context, out_weight, preferred_element_type=jnp.float32)
    stream = (projected + resid_in.astype(jnp.float32)).astype(jnp.bfloat16)
    stream_f = stream.astype(jnp.float32)
    normed = (stream_f * row_scale(stream_f, 2)[:, None] * norm_gain[None, :]).astype(jnp.bfloat16)
    chosen = routes.reshape(-1)
    onehot = (chosen[:, None] == jnp.arange(EXPERTS, dtype=jnp.int32)[None, :]).astype(jnp.int32)
    before = jnp.cumsum(onehot, axis=0) - onehot
    ranking = jnp.sum(before * onehot, axis=1)
    slot_index = chosen * replicas + ranking % replicas
    target = slot_index * capacity + ranking // replicas
    row_ids = jnp.arange(tok_rows * TOPK, dtype=jnp.int32) // TOPK
    source = jnp.full((slot_total * capacity,), tok_rows, jnp.int32).at[target].set(row_ids)
    padded = jnp.concatenate([normed, jnp.zeros((1, feat_block), jnp.bfloat16)], axis=0)
    packed = padded[source].reshape(ep_count, capacity, feat_block)
    tok, w_gate, w_up, w_down = move_all(
        packed, gate_weight, up_weight, down_weight,
        ep_count, lax.axis_size("mx"), lax.axis_size("my"), replicas,
    )
    tokens_in = tok.reshape(slot_rows, D)
    gate_proj = jnp.einsum("rd,spd->rsp", tokens_in, w_gate, preferred_element_type=jnp.float32)
    up_proj = jnp.einsum("rd,spd->rsp", tokens_in, w_up, preferred_element_type=jnp.float32)
    hidden = (jax.nn.silu(gate_proj) * up_proj).astype(jnp.bfloat16)
    expert_out = jnp.einsum("rsp,spd->rd", hidden, w_down, preferred_element_type=jnp.float32)
    expert_out = expert_out.reshape(slot_dev, slot_rows, D)
    returned = send_back(
        expert_out.reshape(slot_rows, D).astype(jnp.bfloat16), ep_count, lax.axis_size("my"), capacity
    ).reshape(slot_total * capacity, feat_block)
    picked = returned[target].reshape(tok_rows, TOPK, feat_block).astype(jnp.float32)
    weights_norm = gate_probs / jnp.sum(gate_probs, axis=1, keepdims=True)
    mixed = jnp.sum(weights_norm[:, :, None] * picked, axis=1)
    updated = stream_f + mixed
    normed_out = (updated * row_scale(updated, 3)[:, None] * final_gain[None, :]).astype(jnp.bfloat16)
    return (normed_out, updated.astype(jnp.bfloat16))


def solution(mesh):
    placed = (
        P(("ep", "mx"), None),
        P(("ep", "mx"), "my"),
        P(None, "my"),
        P("my"),
        P(None, ("ep", "my"), "mx"),
        P(None, ("ep", "my"), "mx"),
        P(None, ("ep", "my"), "mx"),
        P(("ep", "mx"), None),
        P(("ep", "mx"), None),
        P("my"),
    )
    return jax.shard_map(
        shards,
        mesh=mesh,
        in_specs=placed,
        out_specs=(P(("ep", "mx"), "my"), P(("ep", "mx"), "my")),
        check_vma=False,
    )
```

```python
import functools

import jax
import jax.numpy as jnp
import numpy as np
from jax import lax
from jax.experimental import pallas as pl
from jax.experimental.pallas import tpu as pltpu
from jax.sharding import PartitionSpec as P

D = 2048
EXPERTS = 8
TOPK = 2
MOST = 96


EPSILON = 1e-06
MESH = pl.DeviceIdType.MESH


def remote(src, dst, send, recv, device):
    return pltpu.make_async_remote_copy(
        src_ref=src, dst_ref=dst, send_sem=send, recv_sem=recv,
        device_id=device, device_id_type=MESH,
    )


def move_kernel(n_ep, n_mx, n_my, replicas, packed_ref, gate_ref, up_ref, down_ref,
                tok_ref, gate_out, up_out, down_out, tok_sems, send_z, recv_z, fwd_send, fwd_recv,
                send_x, recv_x, local_sem):
    j = lax.axis_index("ep")
    a = lax.axis_index("mx")
    m = lax.axis_index("my")
    fb = packed_ref.shape[2]
    wb = gate_ref.shape[2]
    cols_m = pl.ds(pl.multiple_of(m * fb, fb), fb)
    cols_a = pl.ds(pl.multiple_of(a * wb, wb), wb)
    barrier = pltpu.get_barrier_semaphore()
    peers = [(lax.rem(j + d, n_ep), a, m) for d in range(1, n_ep)]
    peers += [(j, lax.rem(a + e, n_mx), m) for e in range(1, n_mx)]
    peers += [(j, a, lax.rem(m + e, n_my)) for e in range(1, n_my)]
    for peer in peers:
        pl.semaphore_signal(barrier, inc=1, device_id=peer, device_id_type=MESH)
    pl.semaphore_wait(barrier, len(peers))
    pending = []
    weights = (gate_ref, up_ref, down_ref)
    outs = (gate_out, up_out, down_out)

    half_ring = n_ep // 2
    side = half_ring - 1
    parity = lax.rem(j, 2)
    partner = j + 1 - 2 * parity

    def start_direct(k):
        local = pltpu.make_async_copy(
            weights[k].at[j // replicas], outs[k].at[j, :, cols_a], local_sem.at[k])
        local.start()
        direct = []
        for d in range(1, side + 1):
            sign = 1 - 2 * lax.rem(j + d, 2)
            t = lax.rem(j + n_ep + sign * d, n_ep)
            copy = remote(weights[k].at[t // replicas], outs[k].at[j, :, cols_a],
                          send_z.at[k, d], recv_z.at[k, d], (t, a, m))
            copy.start()
            direct.append(copy)
        return local, direct

    def start_forward(k):
        forward = []
        for d in range(0, side + 1):
            src = lax.rem(j + n_ep - d + 2 * parity * d, n_ep)
            copy = remote(outs[k].at[src, :, cols_a], outs[k].at[src, :, cols_a],
                          fwd_send.at[k, d], fwd_recv.at[k, d], (partner, a, m))
            copy.start()
            forward.append(copy)
        return forward

    local, direct = start_direct(0)
    tok_local = pltpu.make_async_copy(packed_ref.at[j], tok_ref.at[j, :, cols_m], tok_sems.at[0, 0])
    tok_local.start()
    tok_z = []
    for d in range(1, n_ep):
        t = lax.rem(j + d, n_ep)
        copy = remote(packed_ref.at[t], tok_ref.at[j, :, cols_m], tok_sems.at[1, d], tok_sems.at[2, d], (t, a, m))
        copy.start()
        tok_z.append(copy)
    tok_my = []
    x_copies = []
    for k in range(3):
        local.wait()
        for copy in direct:
            copy.wait_recv()
        pending.extend(direct)
        forward = start_forward(k)
        if k + 1 < 3:
            local, direct = start_direct(k + 1)
        for copy in forward:
            copy.wait_recv()
        pending.extend(forward)
        if n_mx == 4:
            right = lax.rem(a + 1, n_mx)
            left = lax.rem(a + n_mx - 1, n_mx)
            half = n_ep // 2
            to_right = remote(outs[k].at[:, :, cols_a], outs[k].at[:, :, cols_a],
                              send_x.at[k, 0], recv_x.at[k, 0], (j, right, m))
            to_left = remote(outs[k].at[:, :, cols_a], outs[k].at[:, :, cols_a],
                             send_x.at[k, 1], recv_x.at[k, 1], (j, left, m))
            to_right.start()
            to_left.start()
            cols_l = pl.ds(pl.multiple_of(left * wb, wb), wb)
            cols_r = pl.ds(pl.multiple_of(right * wb, wb), wb)
            to_right.wait_recv()
            fwd_right = remote(outs[k].at[pl.ds(0, half), :, cols_l], outs[k].at[pl.ds(0, half), :, cols_l],
                               send_x.at[k, 2], recv_x.at[k, 2], (j, right, m))
            fwd_right.start()
            to_left.wait_recv()
            fwd_left = remote(outs[k].at[pl.ds(half, half), :, cols_r], outs[k].at[pl.ds(half, half), :, cols_r],
                              send_x.at[k, 3], recv_x.at[k, 3], (j, left, m))
            fwd_left.start()
            pending.extend([to_right, to_left])
            x_copies.extend([fwd_right, fwd_left])
        else:
            for e in range(1, n_mx):
                b = lax.rem(a + e, n_mx)
                copy = remote(outs[k].at[:, :, cols_a], outs[k].at[:, :, cols_a],
                              send_x.at[k, e], recv_x.at[k, e], (j, b, m))
                copy.start()
                x_copies.append(copy)
        if k == 0:
            tok_local.wait()
            for copy in tok_z:
                copy.wait_recv()
            pending.extend(tok_z)
            for e in range(1, n_my):
                b = lax.rem(m + e, n_my)
                copy = remote(tok_ref.at[:, :, cols_m], tok_ref.at[:, :, cols_m], tok_sems.at[3, e], tok_sems.at[4, e], (j, a, b))
                copy.start()
                tok_my.append(copy)
            pending.extend(tok_my)
    pending.extend(x_copies)
    for copy in pending:
        copy.wait_send()
    for copy in tok_my + x_copies:
        copy.wait_recv()


def move_all(packed, gate_weight, up_weight, down_weight, n_ep, n_mx, n_my, replicas):
    _, rows, fb = packed.shape
    _, units, wb = gate_weight.shape
    return pl.pallas_call(
        functools.partial(move_kernel, n_ep, n_mx, n_my, replicas),
        out_shape=(
            jax.ShapeDtypeStruct((n_ep, rows, n_my * fb), packed.dtype),
        ) + (jax.ShapeDtypeStruct((n_ep, units, n_mx * wb), gate_weight.dtype),) * 3,
        in_specs=[pl.BlockSpec(memory_space=pl.ANY)] * 4,
        out_specs=(pl.BlockSpec(memory_space=pl.ANY),) * 4,
        scratch_shapes=[
            pltpu.SemaphoreType.DMA((5, max(n_ep, n_my))),
            pltpu.SemaphoreType.DMA((3, n_ep)),
            pltpu.SemaphoreType.DMA((3, n_ep)),
            pltpu.SemaphoreType.DMA((3, n_ep)),
            pltpu.SemaphoreType.DMA((3, n_ep)),
            pltpu.SemaphoreType.DMA((3, max(n_mx, 4))),
            pltpu.SemaphoreType.DMA((3, max(n_mx, 4))),
            pltpu.SemaphoreType.DMA((3,)),
        ],
        compiler_params=pltpu.CompilerParams(has_side_effects=True, collective_id=0),
    )(packed, gate_weight, up_weight, down_weight)


def back_kernel(n_ep, n_my, ex_ref, out_ref, rx_core, chip_part, rx_y, result, sems):
    j = lax.axis_index("ep")
    a = lax.axis_index("mx")
    m = lax.axis_index("my")
    fb = out_ref.shape[2]
    cap = out_ref.shape[1]
    chips = n_my // 2
    core = lax.rem(m, 2)
    y = m // 2
    partner = m + 1 - 2 * core
    barrier = pltpu.get_barrier_semaphore()
    peers = [(j, a, partner)]
    peers += [(j, a, lax.rem(y + e, chips) * 2 + core) for e in range(1, chips)]
    peers += [(lax.rem(j + d, n_ep), a, m) for d in range(1, n_ep)]
    for peer in peers:
        pl.semaphore_signal(barrier, inc=1, device_id=peer, device_id_type=MESH)
    pl.semaphore_wait(barrier, len(peers))

    def cols(block):
        return pl.ds(pl.multiple_of(block * fb, fb), fb)

    to_core = []
    for i in range(chips):
        copy = remote(ex_ref.at[:, cols(1 - core + 2 * i)], rx_core.at[i],
                      sems.at[0, i], sems.at[1, i], (j, a, partner))
        copy.start()
        to_core.append(copy)
    for copy in to_core:
        copy.wait_recv()
    for i in range(chips):
        own = ex_ref[:, cols(core + 2 * i)].astype(jnp.float32)
        chip_part[i] = (own + rx_core[i].astype(jnp.float32)).astype(chip_part.dtype)
    rows = result.shape[0]
    half_rows = rows // 2
    half_slots = n_ep // 2
    to_y = []
    for h in range(2):
        part = pl.ds(h * half_rows, half_rows)
        for e in range(1, chips):
            other = lax.rem(y + e, chips)
            copy = remote(chip_part.at[other, part], rx_y.at[e - 1, part],
                          sems.at[2 + 2 * h, e], sems.at[3 + 2 * h, e], (j, a, other * 2 + core))
            copy.start()
            to_y.append(copy)
    to_z = []
    for h in range(2):
        part = pl.ds(h * half_rows, half_rows)
        for copy in to_y[h * (chips - 1):(h + 1) * (chips - 1)]:
            copy.wait_recv()
        total = chip_part[y, part].astype(jnp.float32)
        for e in range(1, chips):
            total = total + rx_y[e - 1, part].astype(jnp.float32)
        result[part] = total.astype(result.dtype)
        for t in range(h * half_slots, (h + 1) * half_slots):
            rows_t = result.at[pl.ds(t * cap, cap)]

            @pl.when(t == j)
            def _():
                local = pltpu.make_async_copy(rows_t, out_ref.at[j], sems.at[6, t])
                local.start()
                local.wait()

            copy = remote(rows_t, out_ref.at[j], sems.at[7, t], sems.at[8, j], (t, a, m))

            @pl.when(t != j)
            def _():
                copy.start()

            to_z.append((t, copy))
    for copy in to_core + to_y:
        copy.wait_send()
    for t, copy in to_z:
        @pl.when(t != j)
        def _():
            copy.wait_send()
    for s in range(n_ep):
        incoming = remote(result.at[pl.ds(0, cap)], out_ref.at[s], sems.at[7, s], sems.at[8, s], (s, a, m))

        @pl.when(s != j)
        def _():
            incoming.wait_recv()


def send_back(ex, n_ep, n_my, cap):
    rows, width = ex.shape
    fb = width // n_my
    return pl.pallas_call(
        functools.partial(back_kernel, n_ep, n_my),
        out_shape=jax.ShapeDtypeStruct((n_ep, cap, fb), ex.dtype),
        in_specs=[pl.BlockSpec(memory_space=pltpu.VMEM)],
        out_specs=pl.BlockSpec(memory_space=pl.ANY),
        scratch_shapes=[
            pltpu.VMEM((n_my // 2, rows, fb), ex.dtype),
            pltpu.VMEM((n_my // 2, rows, fb), ex.dtype),
            pltpu.VMEM((n_my // 2 - 1, rows, fb), ex.dtype),
            pltpu.VMEM((rows, fb), ex.dtype),
            pltpu.SemaphoreType.DMA((9, max(n_ep, n_my))),
        ],
        compiler_params=pltpu.CompilerParams(has_side_effects=True, collective_id=1),
    )(ex)


def sum_kernel(n_my, x_ref, o_ref, slots, send, recv):
    j = lax.axis_index("ep")
    a = lax.axis_index("mx")
    m = lax.axis_index("my")
    barrier = pltpu.get_barrier_semaphore()
    for e in range(1, n_my):
        pl.semaphore_signal(barrier, inc=1, device_id=(j, a, lax.rem(m + e, n_my)), device_id_type=MESH)
    pl.semaphore_wait(barrier, n_my - 1)
    slots[m] = x_ref[...]
    copies = []
    for e in range(1, n_my):
        b = lax.rem(m + e, n_my)
        copy = remote(x_ref, slots.at[m], send.at[e], recv.at[e], (j, a, b))
        copy.start()
        copies.append(copy)
    for copy in copies:
        copy.wait_send()
    for copy in copies:
        copy.wait_recv()
    o_ref[...] = jnp.sum(slots[...], axis=0)


def sum_over_my(values, kernel_id):
    n_my = lax.axis_size("my")
    row = values.reshape(1, -1)
    total = pl.pallas_call(
        functools.partial(sum_kernel, n_my),
        out_shape=jax.ShapeDtypeStruct(row.shape, row.dtype),
        in_specs=[pl.BlockSpec(memory_space=pltpu.VMEM)],
        out_specs=pl.BlockSpec(memory_space=pltpu.VMEM),
        scratch_shapes=[
            pltpu.VMEM((n_my,) + row.shape, row.dtype),
            pltpu.SemaphoreType.DMA((n_my,)),
            pltpu.SemaphoreType.DMA((n_my,)),
        ],
        compiler_params=pltpu.CompilerParams(has_side_effects=True, collective_id=kernel_id),
    )(row)
    return total.reshape(values.shape)


def row_scale(stream_f, kernel_id):
    partial_sq = jnp.sum(stream_f * stream_f, axis=1)
    row_total = sum_over_my(partial_sq, kernel_id)
    return lax.rsqrt(row_total / D + EPSILON)


def shards(
    context,
    resid_in,
    out_weight,
    norm_gain,
    gate_weight,
    up_weight,
    down_weight,
    routes,
    gate_probs,
    final_gain,
):
    ep_count = lax.axis_size("ep")
    slot_dev = max(1, EXPERTS // ep_count)
    slot_total = slot_dev * ep_count
    replicas = slot_total // EXPERTS
    capacity = MOST // replicas
    tok_rows = context.shape[0]
    feat_block = resid_in.shape[1]
    piece_units = gate_weight.shape[1]
    slot_rows = ep_count * capacity

    projected = jnp.dot(context, out_weight, preferred_element_type=jnp.float32)
    stream = (projected + resid_in.astype(jnp.float32)).astype(jnp.bfloat16)
    stream_f = stream.astype(jnp.float32)
    normed = (stream_f * row_scale(stream_f, 2)[:, None] * norm_gain[None, :]).astype(jnp.bfloat16)
    chosen = routes.reshape(-1)
    onehot = (chosen[:, None] == jnp.arange(EXPERTS, dtype=jnp.int32)[None, :]).astype(jnp.int32)
    before = jnp.cumsum(onehot, axis=0) - onehot
    ranking = jnp.sum(before * onehot, axis=1)
    slot_index = chosen * replicas + ranking % replicas
    target = slot_index * capacity + ranking // replicas
    row_ids = jnp.arange(tok_rows * TOPK, dtype=jnp.int32) // TOPK
    source = jnp.full((slot_total * capacity,), tok_rows, jnp.int32).at[target].set(row_ids)
    padded = jnp.concatenate([normed, jnp.zeros((1, feat_block), jnp.bfloat16)], axis=0)
    packed = padded[source].reshape(ep_count, capacity, feat_block)
    tok, w_gate, w_up, w_down = move_all(
        packed, gate_weight, up_weight, down_weight,
        ep_count, lax.axis_size("mx"), lax.axis_size("my"), replicas,
    )
    tokens_in = tok.reshape(slot_rows, D)
    gate_proj = jnp.einsum("rd,spd->rsp", tokens_in, w_gate, preferred_element_type=jnp.float32)
    up_proj = jnp.einsum("rd,spd->rsp", tokens_in, w_up, preferred_element_type=jnp.float32)
    hidden = (jax.nn.silu(gate_proj) * up_proj).astype(jnp.bfloat16)
    expert_out = jnp.einsum("rsp,spd->rd", hidden, w_down, preferred_element_type=jnp.float32)
    expert_out = expert_out.reshape(slot_dev, slot_rows, D)
    returned = send_back(
        expert_out.reshape(slot_rows, D).astype(jnp.bfloat16), ep_count, lax.axis_size("my"), capacity
    ).reshape(slot_total * capacity, feat_block)
    picked = returned[target].reshape(tok_rows, TOPK, feat_block).astype(jnp.float32)
    weights_norm = gate_probs / jnp.sum(gate_probs, axis=1, keepdims=True)
    mixed = jnp.sum(weights_norm[:, :, None] * picked, axis=1)
    updated = stream_f + mixed
    normed_out = (updated * row_scale(updated, 3)[:, None] * final_gain[None, :]).astype(jnp.bfloat16)
    return (normed_out, updated.astype(jnp.bfloat16))


def solution(mesh):
    placed = (
        P(("ep", "mx"), None),
        P(("ep", "mx"), "my"),
        P(None, "my"),
        P("my"),
        P(None, ("ep", "my"), "mx"),
        P(None, ("ep", "my"), "mx"),
        P(None, ("ep", "my"), "mx"),
        P(("ep", "mx"), None),
        P(("ep", "mx"), None),
        P("my"),
    )
    return jax.shard_map(
        shards,
        mesh=mesh,
        in_specs=placed,
        out_specs=(P(("ep", "mx"), "my"), P(("ep", "mx"), "my")),
        check_vma=False,
    )
```

```python
import functools

import jax
import jax.numpy as jnp
import numpy as np
from jax import lax
from jax.experimental import pallas as pl
from jax.experimental.pallas import tpu as pltpu
from jax.sharding import PartitionSpec as P

D = 2048
EXPERTS = 8
TOPK = 2
MOST = 96


EPSILON = 1e-06
MESH = pl.DeviceIdType.MESH


def remote(src, dst, send, recv, device):
    return pltpu.make_async_remote_copy(
        src_ref=src, dst_ref=dst, send_sem=send, recv_sem=recv,
        device_id=device, device_id_type=MESH,
    )


def move_kernel(n_ep, n_mx, n_my, replicas, packed_ref, gate_ref, up_ref, down_ref,
                tok_ref, gate_out, up_out, down_out, tok_sems, send_z, recv_z, fwd_send, fwd_recv,
                send_x, recv_x, local_sem):
    j = lax.axis_index("ep")
    a = lax.axis_index("mx")
    m = lax.axis_index("my")
    fb = packed_ref.shape[2]
    wb = gate_ref.shape[2]
    cols_m = pl.ds(pl.multiple_of(m * fb, fb), fb)
    cols_a = pl.ds(pl.multiple_of(a * wb, wb), wb)
    barrier = pltpu.get_barrier_semaphore()
    peers = [(lax.rem(j + d, n_ep), a, m) for d in range(1, n_ep)]
    peers += [(j, lax.rem(a + e, n_mx), m) for e in range(1, n_mx)]
    peers += [(j, a, lax.rem(m + e, n_my)) for e in range(1, n_my)]
    for peer in peers:
        pl.semaphore_signal(barrier, inc=1, device_id=peer, device_id_type=MESH)
    pl.semaphore_wait(barrier, len(peers))
    pending = []
    weights = (gate_ref, up_ref, down_ref)
    outs = (gate_out, up_out, down_out)

    half_ring = n_ep // 2
    side = half_ring - 1
    parity = lax.rem(j, 2)
    partner = j + 1 - 2 * parity

    def start_direct(k):
        local = pltpu.make_async_copy(
            weights[k].at[j // replicas], outs[k].at[j, :, cols_a], local_sem.at[k])
        local.start()
        direct = []
        for d in range(1, side + 1):
            sign = 1 - 2 * lax.rem(j + d, 2)
            t = lax.rem(j + n_ep + sign * d, n_ep)
            copy = remote(weights[k].at[t // replicas], outs[k].at[j, :, cols_a],
                          send_z.at[k, d], recv_z.at[k, d], (t, a, m))
            copy.start()
            direct.append(copy)
        return local, direct

    def start_forward(k):
        forward = []
        for d in range(0, side + 1):
            src = lax.rem(j + n_ep - d + 2 * parity * d, n_ep)
            copy = remote(outs[k].at[src, :, cols_a], outs[k].at[src, :, cols_a],
                          fwd_send.at[k, d], fwd_recv.at[k, d], (partner, a, m))
            copy.start()
            forward.append(copy)
        return forward

    waves = [start_direct(0), start_direct(1)]
    tok_local = pltpu.make_async_copy(packed_ref.at[j], tok_ref.at[j, :, cols_m], tok_sems.at[0, 0])
    tok_local.start()
    tok_z = []
    for d in range(1, n_ep):
        t = lax.rem(j + d, n_ep)
        copy = remote(packed_ref.at[t], tok_ref.at[j, :, cols_m], tok_sems.at[1, d], tok_sems.at[2, d], (t, a, m))
        copy.start()
        tok_z.append(copy)
    tok_my = []
    x_copies = []
    for k in range(3):
        local, direct = waves[k]
        local.wait()
        for copy in direct:
            copy.wait_recv()
        pending.extend(direct)
        forward = start_forward(k)
        if k + 2 < 3:
            waves.append(start_direct(k + 2))
        for copy in forward:
            copy.wait_recv()
        pending.extend(forward)
        if n_mx == 4:
            right = lax.rem(a + 1, n_mx)
            left = lax.rem(a + n_mx - 1, n_mx)
            half = n_ep // 2
            to_right = remote(outs[k].at[:, :, cols_a], outs[k].at[:, :, cols_a],
                              send_x.at[k, 0], recv_x.at[k, 0], (j, right, m))
            to_left = remote(outs[k].at[:, :, cols_a], outs[k].at[:, :, cols_a],
                             send_x.at[k, 1], recv_x.at[k, 1], (j, left, m))
            to_right.start()
            to_left.start()
            cols_l = pl.ds(pl.multiple_of(left * wb, wb), wb)
            cols_r = pl.ds(pl.multiple_of(right * wb, wb), wb)
            to_right.wait_recv()
            fwd_right = remote(outs[k].at[pl.ds(0, half), :, cols_l], outs[k].at[pl.ds(0, half), :, cols_l],
                               send_x.at[k, 2], recv_x.at[k, 2], (j, right, m))
            fwd_right.start()
            to_left.wait_recv()
            fwd_left = remote(outs[k].at[pl.ds(half, half), :, cols_r], outs[k].at[pl.ds(half, half), :, cols_r],
                              send_x.at[k, 3], recv_x.at[k, 3], (j, left, m))
            fwd_left.start()
            pending.extend([to_right, to_left])
            x_copies.extend([fwd_right, fwd_left])
        else:
            for e in range(1, n_mx):
                b = lax.rem(a + e, n_mx)
                copy = remote(outs[k].at[:, :, cols_a], outs[k].at[:, :, cols_a],
                              send_x.at[k, e], recv_x.at[k, e], (j, b, m))
                copy.start()
                x_copies.append(copy)
        if k == 0:
            tok_local.wait()
            for copy in tok_z:
                copy.wait_recv()
            pending.extend(tok_z)
            for e in range(1, n_my):
                b = lax.rem(m + e, n_my)
                copy = remote(tok_ref.at[:, :, cols_m], tok_ref.at[:, :, cols_m], tok_sems.at[3, e], tok_sems.at[4, e], (j, a, b))
                copy.start()
                tok_my.append(copy)
            pending.extend(tok_my)
    pending.extend(x_copies)
    for copy in pending:
        copy.wait_send()
    for copy in tok_my + x_copies:
        copy.wait_recv()


def move_all(packed, gate_weight, up_weight, down_weight, n_ep, n_mx, n_my, replicas):
    _, rows, fb = packed.shape
    _, units, wb = gate_weight.shape
    return pl.pallas_call(
        functools.partial(move_kernel, n_ep, n_mx, n_my, replicas),
        out_shape=(
            jax.ShapeDtypeStruct((n_ep, rows, n_my * fb), packed.dtype),
        ) + (jax.ShapeDtypeStruct((n_ep, units, n_mx * wb), gate_weight.dtype),) * 3,
        in_specs=[pl.BlockSpec(memory_space=pl.ANY)] * 4,
        out_specs=(pl.BlockSpec(memory_space=pl.ANY),) * 4,
        scratch_shapes=[
            pltpu.SemaphoreType.DMA((5, max(n_ep, n_my))),
            pltpu.SemaphoreType.DMA((3, n_ep)),
            pltpu.SemaphoreType.DMA((3, n_ep)),
            pltpu.SemaphoreType.DMA((3, n_ep)),
            pltpu.SemaphoreType.DMA((3, n_ep)),
            pltpu.SemaphoreType.DMA((3, max(n_mx, 4))),
            pltpu.SemaphoreType.DMA((3, max(n_mx, 4))),
            pltpu.SemaphoreType.DMA((3,)),
        ],
        compiler_params=pltpu.CompilerParams(has_side_effects=True, collective_id=0),
    )(packed, gate_weight, up_weight, down_weight)


def back_kernel(n_ep, n_my, ex_ref, out_ref, rx_core, chip_part, rx_y, result, sems):
    j = lax.axis_index("ep")
    a = lax.axis_index("mx")
    m = lax.axis_index("my")
    fb = out_ref.shape[2]
    cap = out_ref.shape[1]
    chips = n_my // 2
    core = lax.rem(m, 2)
    y = m // 2
    partner = m + 1 - 2 * core
    barrier = pltpu.get_barrier_semaphore()
    peers = [(j, a, partner)]
    peers += [(j, a, lax.rem(y + e, chips) * 2 + core) for e in range(1, chips)]
    peers += [(lax.rem(j + d, n_ep), a, m) for d in range(1, n_ep)]
    for peer in peers:
        pl.semaphore_signal(barrier, inc=1, device_id=peer, device_id_type=MESH)
    pl.semaphore_wait(barrier, len(peers))

    def cols(block):
        return pl.ds(pl.multiple_of(block * fb, fb), fb)

    to_core = []
    for i in range(chips):
        copy = remote(ex_ref.at[:, cols(1 - core + 2 * i)], rx_core.at[i],
                      sems.at[0, i], sems.at[1, i], (j, a, partner))
        copy.start()
        to_core.append(copy)
    for copy in to_core:
        copy.wait_recv()
    for i in range(chips):
        own = ex_ref[:, cols(core + 2 * i)].astype(jnp.float32)
        chip_part[i] = (own + rx_core[i].astype(jnp.float32)).astype(chip_part.dtype)
    rows = result.shape[0]
    half_rows = rows // 2
    half_slots = n_ep // 2
    to_y = []
    for h in range(2):
        part = pl.ds(h * half_rows, half_rows)
        for e in range(1, chips):
            other = lax.rem(y + e, chips)
            copy = remote(chip_part.at[other, part], rx_y.at[e - 1, part],
                          sems.at[2 + 2 * h, e], sems.at[3 + 2 * h, e], (j, a, other * 2 + core))
            copy.start()
            to_y.append(copy)
    to_z = []
    for h in range(2):
        part = pl.ds(h * half_rows, half_rows)
        for copy in to_y[h * (chips - 1):(h + 1) * (chips - 1)]:
            copy.wait_recv()
        total = chip_part[y, part].astype(jnp.float32)
        for e in range(1, chips):
            total = total + rx_y[e - 1, part].astype(jnp.float32)
        result[part] = total.astype(result.dtype)
        for t in range(h * half_slots, (h + 1) * half_slots):
            rows_t = result.at[pl.ds(t * cap, cap)]

            @pl.when(t == j)
            def _():
                local = pltpu.make_async_copy(rows_t, out_ref.at[j], sems.at[6, t])
                local.start()
                local.wait()

            copy = remote(rows_t, out_ref.at[j], sems.at[7, t], sems.at[8, j], (t, a, m))

            @pl.when(t != j)
            def _():
                copy.start()

            to_z.append((t, copy))
    for copy in to_core + to_y:
        copy.wait_send()
    for t, copy in to_z:
        @pl.when(t != j)
        def _():
            copy.wait_send()
    for s in range(n_ep):
        incoming = remote(result.at[pl.ds(0, cap)], out_ref.at[s], sems.at[7, s], sems.at[8, s], (s, a, m))

        @pl.when(s != j)
        def _():
            incoming.wait_recv()


def send_back(ex, n_ep, n_my, cap):
    rows, width = ex.shape
    fb = width // n_my
    return pl.pallas_call(
        functools.partial(back_kernel, n_ep, n_my),
        out_shape=jax.ShapeDtypeStruct((n_ep, cap, fb), ex.dtype),
        in_specs=[pl.BlockSpec(memory_space=pltpu.VMEM)],
        out_specs=pl.BlockSpec(memory_space=pl.ANY),
        scratch_shapes=[
            pltpu.VMEM((n_my // 2, rows, fb), ex.dtype),
            pltpu.VMEM((n_my // 2, rows, fb), ex.dtype),
            pltpu.VMEM((n_my // 2 - 1, rows, fb), ex.dtype),
            pltpu.VMEM((rows, fb), ex.dtype),
            pltpu.SemaphoreType.DMA((9, max(n_ep, n_my))),
        ],
        compiler_params=pltpu.CompilerParams(has_side_effects=True, collective_id=1),
    )(ex)


def sum_kernel(n_my, x_ref, o_ref, slots, send, recv):
    j = lax.axis_index("ep")
    a = lax.axis_index("mx")
    m = lax.axis_index("my")
    barrier = pltpu.get_barrier_semaphore()
    for e in range(1, n_my):
        pl.semaphore_signal(barrier, inc=1, device_id=(j, a, lax.rem(m + e, n_my)), device_id_type=MESH)
    pl.semaphore_wait(barrier, n_my - 1)
    slots[m] = x_ref[...]
    copies = []
    for e in range(1, n_my):
        b = lax.rem(m + e, n_my)
        copy = remote(x_ref, slots.at[m], send.at[e], recv.at[e], (j, a, b))
        copy.start()
        copies.append(copy)
    for copy in copies:
        copy.wait_send()
    for copy in copies:
        copy.wait_recv()
    o_ref[...] = jnp.sum(slots[...], axis=0)


def sum_over_my(values, kernel_id):
    n_my = lax.axis_size("my")
    row = values.reshape(1, -1)
    total = pl.pallas_call(
        functools.partial(sum_kernel, n_my),
        out_shape=jax.ShapeDtypeStruct(row.shape, row.dtype),
        in_specs=[pl.BlockSpec(memory_space=pltpu.VMEM)],
        out_specs=pl.BlockSpec(memory_space=pltpu.VMEM),
        scratch_shapes=[
            pltpu.VMEM((n_my,) + row.shape, row.dtype),
            pltpu.SemaphoreType.DMA((n_my,)),
            pltpu.SemaphoreType.DMA((n_my,)),
        ],
        compiler_params=pltpu.CompilerParams(has_side_effects=True, collective_id=kernel_id),
    )(row)
    return total.reshape(values.shape)


def row_scale(stream_f, kernel_id):
    partial_sq = jnp.sum(stream_f * stream_f, axis=1)
    row_total = sum_over_my(partial_sq, kernel_id)
    return lax.rsqrt(row_total / D + EPSILON)


def shards(
    context,
    resid_in,
    out_weight,
    norm_gain,
    gate_weight,
    up_weight,
    down_weight,
    routes,
    gate_probs,
    final_gain,
):
    ep_count = lax.axis_size("ep")
    slot_dev = max(1, EXPERTS // ep_count)
    slot_total = slot_dev * ep_count
    replicas = slot_total // EXPERTS
    capacity = MOST // replicas
    tok_rows = context.shape[0]
    feat_block = resid_in.shape[1]
    piece_units = gate_weight.shape[1]
    slot_rows = ep_count * capacity

    projected = jnp.dot(context, out_weight, preferred_element_type=jnp.float32)
    stream = (projected + resid_in.astype(jnp.float32)).astype(jnp.bfloat16)
    stream_f = stream.astype(jnp.float32)
    normed = (stream_f * row_scale(stream_f, 2)[:, None] * norm_gain[None, :]).astype(jnp.bfloat16)
    chosen = routes.reshape(-1)
    onehot = (chosen[:, None] == jnp.arange(EXPERTS, dtype=jnp.int32)[None, :]).astype(jnp.int32)
    before = jnp.cumsum(onehot, axis=0) - onehot
    ranking = jnp.sum(before * onehot, axis=1)
    slot_index = chosen * replicas + ranking % replicas
    target = slot_index * capacity + ranking // replicas
    row_ids = jnp.arange(tok_rows * TOPK, dtype=jnp.int32) // TOPK
    source = jnp.full((slot_total * capacity,), tok_rows, jnp.int32).at[target].set(row_ids)
    padded = jnp.concatenate([normed, jnp.zeros((1, feat_block), jnp.bfloat16)], axis=0)
    packed = padded[source].reshape(ep_count, capacity, feat_block)
    tok, w_gate, w_up, w_down = move_all(
        packed, gate_weight, up_weight, down_weight,
        ep_count, lax.axis_size("mx"), lax.axis_size("my"), replicas,
    )
    tokens_in = tok.reshape(slot_rows, D)
    gate_proj = jnp.einsum("rd,spd->rsp", tokens_in, w_gate, preferred_element_type=jnp.float32)
    up_proj = jnp.einsum("rd,spd->rsp", tokens_in, w_up, preferred_element_type=jnp.float32)
    hidden = (jax.nn.silu(gate_proj) * up_proj).astype(jnp.bfloat16)
    expert_out = jnp.einsum("rsp,spd->rd", hidden, w_down, preferred_element_type=jnp.float32)
    expert_out = expert_out.reshape(slot_dev, slot_rows, D)
    returned = send_back(
        expert_out.reshape(slot_rows, D).astype(jnp.bfloat16), ep_count, lax.axis_size("my"), capacity
    ).reshape(slot_total * capacity, feat_block)
    picked = returned[target].reshape(tok_rows, TOPK, feat_block).astype(jnp.float32)
    weights_norm = gate_probs / jnp.sum(gate_probs, axis=1, keepdims=True)
    mixed = jnp.sum(weights_norm[:, :, None] * picked, axis=1)
    updated = stream_f + mixed
    normed_out = (updated * row_scale(updated, 3)[:, None] * final_gain[None, :]).astype(jnp.bfloat16)
    return (normed_out, updated.astype(jnp.bfloat16))


def solution(mesh):
    placed = (
        P(("ep", "mx"), None),
        P(("ep", "mx"), "my"),
        P(None, "my"),
        P("my"),
        P(None, ("ep", "my"), "mx"),
        P(None, ("ep", "my"), "mx"),
        P(None, ("ep", "my"), "mx"),
        P(("ep", "mx"), None),
        P(("ep", "mx"), None),
        P("my"),
    )
    return jax.shard_map(
        shards,
        mesh=mesh,
        in_specs=placed,
        out_specs=(P(("ep", "mx"), "my"), P(("ep", "mx"), "my")),
        check_vma=False,
    )
```

```python
import functools

import jax
import jax.numpy as jnp
import numpy as np
from jax import lax
from jax.experimental import pallas as pl
from jax.experimental.pallas import tpu as pltpu
from jax.sharding import PartitionSpec as P

D = 2048
EXPERTS = 8
TOPK = 2
MOST = 96


EPSILON = 1e-06
MESH = pl.DeviceIdType.MESH


def remote(src, dst, send, recv, device):
    return pltpu.make_async_remote_copy(
        src_ref=src, dst_ref=dst, send_sem=send, recv_sem=recv,
        device_id=device, device_id_type=MESH,
    )


def move_kernel(n_ep, n_mx, n_my, replicas, packed_ref, gate_ref, up_ref, down_ref,
                tok_ref, gate_out, up_out, down_out, tok_sems, send_z, recv_z, fwd_send, fwd_recv,
                send_x, recv_x, local_sem):
    j = lax.axis_index("ep")
    a = lax.axis_index("mx")
    m = lax.axis_index("my")
    fb = packed_ref.shape[2]
    wb = gate_ref.shape[2]
    cols_m = pl.ds(pl.multiple_of(m * fb, fb), fb)
    cols_a = pl.ds(pl.multiple_of(a * wb, wb), wb)
    barrier = pltpu.get_barrier_semaphore()
    peers = [(lax.rem(j + d, n_ep), a, m) for d in range(1, n_ep)]
    peers += [(j, lax.rem(a + e, n_mx), m) for e in range(1, n_mx)]
    peers += [(j, a, lax.rem(m + e, n_my)) for e in range(1, n_my)]
    for peer in peers:
        pl.semaphore_signal(barrier, inc=1, device_id=peer, device_id_type=MESH)
    pl.semaphore_wait(barrier, len(peers))
    pending = []
    weights = (gate_ref, up_ref, down_ref)
    outs = (gate_out, up_out, down_out)

    half_ring = n_ep // 2
    side = half_ring - 1
    parity = lax.rem(j, 2)
    partner = j + 1 - 2 * parity

    def start_direct(k):
        local = pltpu.make_async_copy(
            weights[k].at[j // replicas], outs[k].at[j, :, cols_a], local_sem.at[k])
        local.start()
        direct = []
        for d in range(1, side + 1):
            sign = 1 - 2 * lax.rem(j + d, 2)
            t = lax.rem(j + n_ep + sign * d, n_ep)
            copy = remote(weights[k].at[t // replicas], outs[k].at[j, :, cols_a],
                          send_z.at[k, d], recv_z.at[k, d], (t, a, m))
            copy.start()
            direct.append(copy)
        return local, direct

    def start_forward(k):
        forward = []
        for d in range(0, side + 1):
            src = lax.rem(j + n_ep - d + 2 * parity * d, n_ep)
            copy = remote(outs[k].at[src, :, cols_a], outs[k].at[src, :, cols_a],
                          fwd_send.at[k, d], fwd_recv.at[k, d], (partner, a, m))
            copy.start()
            forward.append(copy)
        return forward

    local, direct = start_direct(0)
    tok_local = pltpu.make_async_copy(packed_ref.at[j], tok_ref.at[j, :, cols_m], tok_sems.at[0, 0])
    tok_local.start()
    tok_z = []
    for d in range(1, n_ep):
        t = lax.rem(j + d, n_ep)
        copy = remote(packed_ref.at[t], tok_ref.at[j, :, cols_m], tok_sems.at[1, d], tok_sems.at[2, d], (t, a, m))
        copy.start()
        tok_z.append(copy)
    tok_my = []
    x_copies = []
    for k in range(3):
        local.wait()
        for copy in direct:
            copy.wait_recv()
        pending.extend(direct)
        forward = start_forward(k)
        if k + 1 < 3:
            local, direct = start_direct(k + 1)
        for copy in forward:
            copy.wait_recv()
        pending.extend(forward)
        if n_mx == 4:
            right = lax.rem(a + 1, n_mx)
            left = lax.rem(a + n_mx - 1, n_mx)
            half = n_ep // 2
            to_right = remote(outs[k].at[:, :, cols_a], outs[k].at[:, :, cols_a],
                              send_x.at[k, 0], recv_x.at[k, 0], (j, right, m))
            to_left = remote(outs[k].at[:, :, cols_a], outs[k].at[:, :, cols_a],
                             send_x.at[k, 1], recv_x.at[k, 1], (j, left, m))
            to_right.start()
            to_left.start()
            cols_l = pl.ds(pl.multiple_of(left * wb, wb), wb)
            cols_r = pl.ds(pl.multiple_of(right * wb, wb), wb)
            to_right.wait_recv()
            fwd_right = remote(outs[k].at[pl.ds(0, half), :, cols_l], outs[k].at[pl.ds(0, half), :, cols_l],
                               send_x.at[k, 2], recv_x.at[k, 2], (j, right, m))
            fwd_right.start()
            to_left.wait_recv()
            fwd_left = remote(outs[k].at[pl.ds(half, half), :, cols_r], outs[k].at[pl.ds(half, half), :, cols_r],
                              send_x.at[k, 3], recv_x.at[k, 3], (j, left, m))
            fwd_left.start()
            pending.extend([to_right, to_left])
            x_copies.extend([fwd_right, fwd_left])
        else:
            for e in range(1, n_mx):
                b = lax.rem(a + e, n_mx)
                copy = remote(outs[k].at[:, :, cols_a], outs[k].at[:, :, cols_a],
                              send_x.at[k, e], recv_x.at[k, e], (j, b, m))
                copy.start()
                x_copies.append(copy)
        if k == 0:
            tok_local.wait()
            for copy in tok_z:
                copy.wait_recv()
            pending.extend(tok_z)
            for e in range(1, n_my):
                b = lax.rem(m + e, n_my)
                copy = remote(tok_ref.at[:, :, cols_m], tok_ref.at[:, :, cols_m], tok_sems.at[3, e], tok_sems.at[4, e], (j, a, b))
                copy.start()
                tok_my.append(copy)
            pending.extend(tok_my)
    pending.extend(x_copies)
    for copy in pending:
        copy.wait_send()
    for copy in tok_my + x_copies:
        copy.wait_recv()


def move_all(packed, gate_weight, up_weight, down_weight, n_ep, n_mx, n_my, replicas):
    _, rows, fb = packed.shape
    _, units, wb = gate_weight.shape
    return pl.pallas_call(
        functools.partial(move_kernel, n_ep, n_mx, n_my, replicas),
        out_shape=(
            jax.ShapeDtypeStruct((n_ep, rows, n_my * fb), packed.dtype),
        ) + (jax.ShapeDtypeStruct((n_ep, units, n_mx * wb), gate_weight.dtype),) * 3,
        in_specs=[pl.BlockSpec(memory_space=pl.ANY)] * 4,
        out_specs=(pl.BlockSpec(memory_space=pl.ANY),) * 4,
        scratch_shapes=[
            pltpu.SemaphoreType.DMA((5, max(n_ep, n_my))),
            pltpu.SemaphoreType.DMA((3, n_ep)),
            pltpu.SemaphoreType.DMA((3, n_ep)),
            pltpu.SemaphoreType.DMA((3, n_ep)),
            pltpu.SemaphoreType.DMA((3, n_ep)),
            pltpu.SemaphoreType.DMA((3, max(n_mx, 4))),
            pltpu.SemaphoreType.DMA((3, max(n_mx, 4))),
            pltpu.SemaphoreType.DMA((3,)),
        ],
        compiler_params=pltpu.CompilerParams(has_side_effects=True, collective_id=0),
    )(packed, gate_weight, up_weight, down_weight)


def back_kernel(n_ep, n_my, ex_ref, out_ref, rx_core, chip_part, rx_y, result, sems):
    j = lax.axis_index("ep")
    a = lax.axis_index("mx")
    m = lax.axis_index("my")
    fb = out_ref.shape[2]
    cap = out_ref.shape[1]
    chips = n_my // 2
    core = lax.rem(m, 2)
    y = m // 2
    partner = m + 1 - 2 * core
    barrier = pltpu.get_barrier_semaphore()
    peers = [(j, a, partner)]
    peers += [(j, a, lax.rem(y + e, chips) * 2 + core) for e in range(1, chips)]
    peers += [(lax.rem(j + d, n_ep), a, m) for d in range(1, n_ep)]
    for peer in peers:
        pl.semaphore_signal(barrier, inc=1, device_id=peer, device_id_type=MESH)
    pl.semaphore_wait(barrier, len(peers))

    def cols(block):
        return pl.ds(pl.multiple_of(block * fb, fb), fb)

    rows = result.shape[0]
    half_rows = rows // 2
    half_slots = n_ep // 2
    to_core = []
    for h in range(2):
        part = pl.ds(h * half_rows, half_rows)
        for i in range(chips):
            copy = remote(ex_ref.at[part, cols(1 - core + 2 * i)], rx_core.at[i, part],
                          sems.at[0, i + chips * h], sems.at[1, i + chips * h], (j, a, partner))
            copy.start()
            to_core.append(copy)
    to_y = []
    for h in range(2):
        part = pl.ds(h * half_rows, half_rows)
        for copy in to_core[h * chips:(h + 1) * chips]:
            copy.wait_recv()
        for i in range(chips):
            own = ex_ref[part, cols(core + 2 * i)].astype(jnp.float32)
            chip_part[i, part] = (own + rx_core[i, part].astype(jnp.float32)).astype(chip_part.dtype)
        for e in range(1, chips):
            other = lax.rem(y + e, chips)
            copy = remote(chip_part.at[other, part], rx_y.at[e - 1, part],
                          sems.at[2 + 2 * h, e], sems.at[3 + 2 * h, e], (j, a, other * 2 + core))
            copy.start()
            to_y.append(copy)
    to_z = []
    for h in range(2):
        part = pl.ds(h * half_rows, half_rows)
        for copy in to_y[h * (chips - 1):(h + 1) * (chips - 1)]:
            copy.wait_recv()
        total = chip_part[y, part].astype(jnp.float32)
        for e in range(1, chips):
            total = total + rx_y[e - 1, part].astype(jnp.float32)
        result[part] = total.astype(result.dtype)
        for t in range(h * half_slots, (h + 1) * half_slots):
            rows_t = result.at[pl.ds(t * cap, cap)]

            @pl.when(t == j)
            def _():
                local = pltpu.make_async_copy(rows_t, out_ref.at[j], sems.at[6, t])
                local.start()
                local.wait()

            copy = remote(rows_t, out_ref.at[j], sems.at[7, t], sems.at[8, j], (t, a, m))

            @pl.when(t != j)
            def _():
                copy.start()

            to_z.append((t, copy))
    for copy in to_core + to_y:
        copy.wait_send()
    for t, copy in to_z:
        @pl.when(t != j)
        def _():
            copy.wait_send()
    for s in range(n_ep):
        incoming = remote(result.at[pl.ds(0, cap)], out_ref.at[s], sems.at[7, s], sems.at[8, s], (s, a, m))

        @pl.when(s != j)
        def _():
            incoming.wait_recv()


def send_back(ex, n_ep, n_my, cap):
    rows, width = ex.shape
    fb = width // n_my
    return pl.pallas_call(
        functools.partial(back_kernel, n_ep, n_my),
        out_shape=jax.ShapeDtypeStruct((n_ep, cap, fb), ex.dtype),
        in_specs=[pl.BlockSpec(memory_space=pltpu.VMEM)],
        out_specs=pl.BlockSpec(memory_space=pl.ANY),
        scratch_shapes=[
            pltpu.VMEM((n_my // 2, rows, fb), ex.dtype),
            pltpu.VMEM((n_my // 2, rows, fb), ex.dtype),
            pltpu.VMEM((n_my // 2 - 1, rows, fb), ex.dtype),
            pltpu.VMEM((rows, fb), ex.dtype),
            pltpu.SemaphoreType.DMA((9, max(n_ep, n_my))),
        ],
        compiler_params=pltpu.CompilerParams(has_side_effects=True, collective_id=1),
    )(ex)


def sum_kernel(n_my, x_ref, o_ref, slots, send, recv):
    j = lax.axis_index("ep")
    a = lax.axis_index("mx")
    m = lax.axis_index("my")
    barrier = pltpu.get_barrier_semaphore()
    for e in range(1, n_my):
        pl.semaphore_signal(barrier, inc=1, device_id=(j, a, lax.rem(m + e, n_my)), device_id_type=MESH)
    pl.semaphore_wait(barrier, n_my - 1)
    slots[m] = x_ref[...]
    copies = []
    for e in range(1, n_my):
        b = lax.rem(m + e, n_my)
        copy = remote(x_ref, slots.at[m], send.at[e], recv.at[e], (j, a, b))
        copy.start()
        copies.append(copy)
    for copy in copies:
        copy.wait_send()
    for copy in copies:
        copy.wait_recv()
    o_ref[...] = jnp.sum(slots[...], axis=0)


def sum_over_my(values, kernel_id):
    n_my = lax.axis_size("my")
    row = values.reshape(1, -1)
    total = pl.pallas_call(
        functools.partial(sum_kernel, n_my),
        out_shape=jax.ShapeDtypeStruct(row.shape, row.dtype),
        in_specs=[pl.BlockSpec(memory_space=pltpu.VMEM)],
        out_specs=pl.BlockSpec(memory_space=pltpu.VMEM),
        scratch_shapes=[
            pltpu.VMEM((n_my,) + row.shape, row.dtype),
            pltpu.SemaphoreType.DMA((n_my,)),
            pltpu.SemaphoreType.DMA((n_my,)),
        ],
        compiler_params=pltpu.CompilerParams(has_side_effects=True, collective_id=kernel_id),
    )(row)
    return total.reshape(values.shape)


def row_scale(stream_f, kernel_id):
    partial_sq = jnp.sum(stream_f * stream_f, axis=1)
    row_total = sum_over_my(partial_sq, kernel_id)
    return lax.rsqrt(row_total / D + EPSILON)


def shards(
    context,
    resid_in,
    out_weight,
    norm_gain,
    gate_weight,
    up_weight,
    down_weight,
    routes,
    gate_probs,
    final_gain,
):
    ep_count = lax.axis_size("ep")
    slot_dev = max(1, EXPERTS // ep_count)
    slot_total = slot_dev * ep_count
    replicas = slot_total // EXPERTS
    capacity = MOST // replicas
    tok_rows = context.shape[0]
    feat_block = resid_in.shape[1]
    piece_units = gate_weight.shape[1]
    slot_rows = ep_count * capacity

    projected = jnp.dot(context, out_weight, preferred_element_type=jnp.float32)
    stream = (projected + resid_in.astype(jnp.float32)).astype(jnp.bfloat16)
    stream_f = stream.astype(jnp.float32)
    normed = (stream_f * row_scale(stream_f, 2)[:, None] * norm_gain[None, :]).astype(jnp.bfloat16)
    chosen = routes.reshape(-1)
    onehot = (chosen[:, None] == jnp.arange(EXPERTS, dtype=jnp.int32)[None, :]).astype(jnp.int32)
    before = jnp.cumsum(onehot, axis=0) - onehot
    ranking = jnp.sum(before * onehot, axis=1)
    slot_index = chosen * replicas + ranking % replicas
    target = slot_index * capacity + ranking // replicas
    row_ids = jnp.arange(tok_rows * TOPK, dtype=jnp.int32) // TOPK
    source = jnp.full((slot_total * capacity,), tok_rows, jnp.int32).at[target].set(row_ids)
    padded = jnp.concatenate([normed, jnp.zeros((1, feat_block), jnp.bfloat16)], axis=0)
    packed = padded[source].reshape(ep_count, capacity, feat_block)
    tok, w_gate, w_up, w_down = move_all(
        packed, gate_weight, up_weight, down_weight,
        ep_count, lax.axis_size("mx"), lax.axis_size("my"), replicas,
    )
    tokens_in = tok.reshape(slot_rows, D)
    gate_proj = jnp.einsum("rd,spd->rsp", tokens_in, w_gate, preferred_element_type=jnp.float32)
    up_proj = jnp.einsum("rd,spd->rsp", tokens_in, w_up, preferred_element_type=jnp.float32)
    hidden = (jax.nn.silu(gate_proj) * up_proj).astype(jnp.bfloat16)
    expert_out = jnp.einsum("rsp,spd->rd", hidden, w_down, preferred_element_type=jnp.float32)
    expert_out = expert_out.reshape(slot_dev, slot_rows, D)
    returned = send_back(
        expert_out.reshape(slot_rows, D).astype(jnp.bfloat16), ep_count, lax.axis_size("my"), capacity
    ).reshape(slot_total * capacity, feat_block)
    picked = returned[target].reshape(tok_rows, TOPK, feat_block).astype(jnp.float32)
    weights_norm = gate_probs / jnp.sum(gate_probs, axis=1, keepdims=True)
    mixed = jnp.sum(weights_norm[:, :, None] * picked, axis=1)
    updated = stream_f + mixed
    normed_out = (updated * row_scale(updated, 3)[:, None] * final_gain[None, :]).astype(jnp.bfloat16)
    return (normed_out, updated.astype(jnp.bfloat16))


def solution(mesh):
    placed = (
        P(("ep", "mx"), None),
        P(("ep", "mx"), "my"),
        P(None, "my"),
        P("my"),
        P(None, ("ep", "my"), "mx"),
        P(None, ("ep", "my"), "mx"),
        P(None, ("ep", "my"), "mx"),
        P(("ep", "mx"), None),
        P(("ep", "mx"), None),
        P("my"),
    )
    return jax.shard_map(
        shards,
        mesh=mesh,
        in_specs=placed,
        out_specs=(P(("ep", "mx"), "my"), P(("ep", "mx"), "my")),
        check_vma=False,
    )
```

```python
import functools

import jax
import jax.numpy as jnp
import numpy as np
from jax import lax
from jax.experimental import pallas as pl
from jax.experimental.pallas import tpu as pltpu
from jax.sharding import PartitionSpec as P

D = 2048
EXPERTS = 8
TOPK = 2
MOST = 96


EPSILON = 1e-06
MESH = pl.DeviceIdType.MESH


def remote(src, dst, send, recv, device):
    return pltpu.make_async_remote_copy(
        src_ref=src, dst_ref=dst, send_sem=send, recv_sem=recv,
        device_id=device, device_id_type=MESH,
    )


def move_kernel(n_ep, n_mx, n_my, replicas, packed_ref, gate_ref, up_ref, down_ref,
                tok_ref, gate_out, up_out, down_out, tok_sems, send_z, recv_z, fwd_send, fwd_recv,
                send_x, recv_x, local_sem):
    j = lax.axis_index("ep")
    a = lax.axis_index("mx")
    m = lax.axis_index("my")
    fb = packed_ref.shape[2]
    wb = gate_ref.shape[2]
    cols_m = pl.ds(pl.multiple_of(m * fb, fb), fb)
    cols_a = pl.ds(pl.multiple_of(a * wb, wb), wb)
    barrier = pltpu.get_barrier_semaphore()
    peers = [(lax.rem(j + d, n_ep), a, m) for d in range(1, n_ep)]
    peers += [(j, lax.rem(a + e, n_mx), m) for e in range(1, n_mx)]
    peers += [(j, a, lax.rem(m + e, n_my)) for e in range(1, n_my)]
    for peer in peers:
        pl.semaphore_signal(barrier, inc=1, device_id=peer, device_id_type=MESH)
    pl.semaphore_wait(barrier, len(peers))
    pending = []
    weights = (gate_ref, up_ref, down_ref)
    outs = (gate_out, up_out, down_out)

    half_ring = n_ep // 2
    side = half_ring - 1
    parity = lax.rem(j, 2)
    partner = j + 1 - 2 * parity

    def start_direct(k):
        local = pltpu.make_async_copy(
            weights[k].at[j // replicas], outs[k].at[j, :, cols_a], local_sem.at[k])
        local.start()
        direct = []
        for d in range(1, side + 1):
            sign = 1 - 2 * lax.rem(j + d, 2)
            t = lax.rem(j + n_ep + sign * d, n_ep)
            copy = remote(weights[k].at[t // replicas], outs[k].at[j, :, cols_a],
                          send_z.at[k, d], recv_z.at[k, d], (t, a, m))
            copy.start()
            direct.append(copy)
        return local, direct

    def start_forward(k):
        forward = []
        for d in range(0, side + 1):
            src = lax.rem(j + n_ep - d + 2 * parity * d, n_ep)
            copy = remote(outs[k].at[src, :, cols_a], outs[k].at[src, :, cols_a],
                          fwd_send.at[k, d], fwd_recv.at[k, d], (partner, a, m))
            copy.start()
            forward.append(copy)
        return forward

    local, direct = start_direct(0)
    tok_local = pltpu.make_async_copy(packed_ref.at[j], tok_ref.at[j, :, cols_m], tok_sems.at[0, 0])
    tok_local.start()
    tok_z = []
    for d in range(1, n_ep):
        t = lax.rem(j + d, n_ep)
        copy = remote(packed_ref.at[t], tok_ref.at[j, :, cols_m], tok_sems.at[1, d], tok_sems.at[2, d], (t, a, m))
        copy.start()
        tok_z.append(copy)
    tok_my = []
    x_copies = []
    right = lax.rem(a + 1, n_mx)
    left = lax.rem(a + n_mx - 1, n_mx)
    half = n_ep // 2
    cols_l = pl.ds(pl.multiple_of(left * wb, wb), wb)
    cols_r = pl.ds(pl.multiple_of(right * wb, wb), wb)

    def relay(k, to_right, to_left):
        to_right.wait_recv()
        fwd_right = remote(outs[k].at[pl.ds(0, half), :, cols_l], outs[k].at[pl.ds(0, half), :, cols_l],
                           send_x.at[k, 2], recv_x.at[k, 2], (j, right, m))
        fwd_right.start()
        to_left.wait_recv()
        fwd_left = remote(outs[k].at[pl.ds(half, half), :, cols_r], outs[k].at[pl.ds(half, half), :, cols_r],
                          send_x.at[k, 3], recv_x.at[k, 3], (j, left, m))
        fwd_left.start()
        pending.extend([to_right, to_left])
        x_copies.extend([fwd_right, fwd_left])

    waiting = None
    for k in range(3):
        local.wait()
        for copy in direct:
            copy.wait_recv()
        pending.extend(direct)
        forward = start_forward(k)
        if k + 1 < 3:
            local, direct = start_direct(k + 1)
        if waiting is not None:
            relay(*waiting)
        for copy in forward:
            copy.wait_recv()
        pending.extend(forward)
        to_right = remote(outs[k].at[:, :, cols_a], outs[k].at[:, :, cols_a],
                          send_x.at[k, 0], recv_x.at[k, 0], (j, right, m))
        to_left = remote(outs[k].at[:, :, cols_a], outs[k].at[:, :, cols_a],
                         send_x.at[k, 1], recv_x.at[k, 1], (j, left, m))
        to_right.start()
        to_left.start()
        waiting = (k, to_right, to_left)
        if k == 0:
            tok_local.wait()
            for copy in tok_z:
                copy.wait_recv()
            pending.extend(tok_z)
            for e in range(1, n_my):
                b = lax.rem(m + e, n_my)
                copy = remote(tok_ref.at[:, :, cols_m], tok_ref.at[:, :, cols_m], tok_sems.at[3, e], tok_sems.at[4, e], (j, a, b))
                copy.start()
                tok_my.append(copy)
            pending.extend(tok_my)
    relay(*waiting)
    pending.extend(x_copies)
    for copy in pending:
        copy.wait_send()
    for copy in tok_my + x_copies:
        copy.wait_recv()


def move_all(packed, gate_weight, up_weight, down_weight, n_ep, n_mx, n_my, replicas):
    _, rows, fb = packed.shape
    _, units, wb = gate_weight.shape
    return pl.pallas_call(
        functools.partial(move_kernel, n_ep, n_mx, n_my, replicas),
        out_shape=(
            jax.ShapeDtypeStruct((n_ep, rows, n_my * fb), packed.dtype),
        ) + (jax.ShapeDtypeStruct((n_ep, units, n_mx * wb), gate_weight.dtype),) * 3,
        in_specs=[pl.BlockSpec(memory_space=pl.ANY)] * 4,
        out_specs=(pl.BlockSpec(memory_space=pl.ANY),) * 4,
        scratch_shapes=[
            pltpu.SemaphoreType.DMA((5, max(n_ep, n_my))),
            pltpu.SemaphoreType.DMA((3, n_ep)),
            pltpu.SemaphoreType.DMA((3, n_ep)),
            pltpu.SemaphoreType.DMA((3, n_ep)),
            pltpu.SemaphoreType.DMA((3, n_ep)),
            pltpu.SemaphoreType.DMA((3, max(n_mx, 4))),
            pltpu.SemaphoreType.DMA((3, max(n_mx, 4))),
            pltpu.SemaphoreType.DMA((3,)),
        ],
        compiler_params=pltpu.CompilerParams(has_side_effects=True, collective_id=0),
    )(packed, gate_weight, up_weight, down_weight)


def back_kernel(n_ep, n_my, ex_ref, out_ref, rx_core, chip_part, rx_y, result, sems):
    j = lax.axis_index("ep")
    a = lax.axis_index("mx")
    m = lax.axis_index("my")
    fb = out_ref.shape[2]
    cap = out_ref.shape[1]
    chips = n_my // 2
    core = lax.rem(m, 2)
    y = m // 2
    partner = m + 1 - 2 * core
    barrier = pltpu.get_barrier_semaphore()
    peers = [(j, a, partner)]
    peers += [(j, a, lax.rem(y + e, chips) * 2 + core) for e in range(1, chips)]
    peers += [(lax.rem(j + d, n_ep), a, m) for d in range(1, n_ep)]
    for peer in peers:
        pl.semaphore_signal(barrier, inc=1, device_id=peer, device_id_type=MESH)
    pl.semaphore_wait(barrier, len(peers))

    def cols(block):
        return pl.ds(pl.multiple_of(block * fb, fb), fb)

    rows = result.shape[0]
    half_rows = rows // 2
    half_slots = n_ep // 2
    to_core = []
    for h in range(2):
        part = pl.ds(h * half_rows, half_rows)
        for i in range(chips):
            copy = remote(ex_ref.at[part, cols(1 - core + 2 * i)], rx_core.at[i, part],
                          sems.at[0, i + chips * h], sems.at[1, i + chips * h], (j, a, partner))
            copy.start()
            to_core.append(copy)
    to_y = []
    for h in range(2):
        part = pl.ds(h * half_rows, half_rows)
        for copy in to_core[h * chips:(h + 1) * chips]:
            copy.wait_recv()
        for i in range(chips):
            own = ex_ref[part, cols(core + 2 * i)].astype(jnp.float32)
            chip_part[i, part] = (own + rx_core[i, part].astype(jnp.float32)).astype(chip_part.dtype)
        for e in range(1, chips):
            other = lax.rem(y + e, chips)
            copy = remote(chip_part.at[other, part], rx_y.at[e - 1, part],
                          sems.at[2 + 2 * h, e], sems.at[3 + 2 * h, e], (j, a, other * 2 + core))
            copy.start()
            to_y.append(copy)
    to_z = []
    for h in range(2):
        part = pl.ds(h * half_rows, half_rows)
        for copy in to_y[h * (chips - 1):(h + 1) * (chips - 1)]:
            copy.wait_recv()
        total = chip_part[y, part].astype(jnp.float32)
        for e in range(1, chips):
            total = total + rx_y[e - 1, part].astype(jnp.float32)
        result[part] = total.astype(result.dtype)
        for t in range(h * half_slots, (h + 1) * half_slots):
            rows_t = result.at[pl.ds(t * cap, cap)]

            @pl.when(t == j)
            def _():
                local = pltpu.make_async_copy(rows_t, out_ref.at[j], sems.at[6, t])
                local.start()
                local.wait()

            copy = remote(rows_t, out_ref.at[j], sems.at[7, t], sems.at[8, j], (t, a, m))

            @pl.when(t != j)
            def _():
                copy.start()

            to_z.append((t, copy))
    for copy in to_core + to_y:
        copy.wait_send()
    for t, copy in to_z:
        @pl.when(t != j)
        def _():
            copy.wait_send()
    for s in range(n_ep):
        incoming = remote(result.at[pl.ds(0, cap)], out_ref.at[s], sems.at[7, s], sems.at[8, s], (s, a, m))

        @pl.when(s != j)
        def _():
            incoming.wait_recv()


def send_back(ex, n_ep, n_my, cap):
    rows, width = ex.shape
    fb = width // n_my
    return pl.pallas_call(
        functools.partial(back_kernel, n_ep, n_my),
        out_shape=jax.ShapeDtypeStruct((n_ep, cap, fb), ex.dtype),
        in_specs=[pl.BlockSpec(memory_space=pltpu.VMEM)],
        out_specs=pl.BlockSpec(memory_space=pl.ANY),
        scratch_shapes=[
            pltpu.VMEM((n_my // 2, rows, fb), ex.dtype),
            pltpu.VMEM((n_my // 2, rows, fb), ex.dtype),
            pltpu.VMEM((n_my // 2 - 1, rows, fb), ex.dtype),
            pltpu.VMEM((rows, fb), ex.dtype),
            pltpu.SemaphoreType.DMA((9, max(n_ep, n_my))),
        ],
        compiler_params=pltpu.CompilerParams(has_side_effects=True, collective_id=1),
    )(ex)


def sum_kernel(n_my, x_ref, o_ref, slots, send, recv):
    j = lax.axis_index("ep")
    a = lax.axis_index("mx")
    m = lax.axis_index("my")
    barrier = pltpu.get_barrier_semaphore()
    for e in range(1, n_my):
        pl.semaphore_signal(barrier, inc=1, device_id=(j, a, lax.rem(m + e, n_my)), device_id_type=MESH)
    pl.semaphore_wait(barrier, n_my - 1)
    slots[m] = x_ref[...]
    copies = []
    for e in range(1, n_my):
        b = lax.rem(m + e, n_my)
        copy = remote(x_ref, slots.at[m], send.at[e], recv.at[e], (j, a, b))
        copy.start()
        copies.append(copy)
    for copy in copies:
        copy.wait_send()
    for copy in copies:
        copy.wait_recv()
    o_ref[...] = jnp.sum(slots[...], axis=0)


def sum_over_my(values, kernel_id):
    n_my = lax.axis_size("my")
    row = values.reshape(1, -1)
    total = pl.pallas_call(
        functools.partial(sum_kernel, n_my),
        out_shape=jax.ShapeDtypeStruct(row.shape, row.dtype),
        in_specs=[pl.BlockSpec(memory_space=pltpu.VMEM)],
        out_specs=pl.BlockSpec(memory_space=pltpu.VMEM),
        scratch_shapes=[
            pltpu.VMEM((n_my,) + row.shape, row.dtype),
            pltpu.SemaphoreType.DMA((n_my,)),
            pltpu.SemaphoreType.DMA((n_my,)),
        ],
        compiler_params=pltpu.CompilerParams(has_side_effects=True, collective_id=kernel_id),
    )(row)
    return total.reshape(values.shape)


def row_scale(stream_f, kernel_id):
    partial_sq = jnp.sum(stream_f * stream_f, axis=1)
    row_total = sum_over_my(partial_sq, kernel_id)
    return lax.rsqrt(row_total / D + EPSILON)


def shards(
    context,
    resid_in,
    out_weight,
    norm_gain,
    gate_weight,
    up_weight,
    down_weight,
    routes,
    gate_probs,
    final_gain,
):
    ep_count = lax.axis_size("ep")
    slot_dev = max(1, EXPERTS // ep_count)
    slot_total = slot_dev * ep_count
    replicas = slot_total // EXPERTS
    capacity = MOST // replicas
    tok_rows = context.shape[0]
    feat_block = resid_in.shape[1]
    piece_units = gate_weight.shape[1]
    slot_rows = ep_count * capacity

    projected = jnp.dot(context, out_weight, preferred_element_type=jnp.float32)
    stream = (projected + resid_in.astype(jnp.float32)).astype(jnp.bfloat16)
    stream_f = stream.astype(jnp.float32)
    normed = (stream_f * row_scale(stream_f, 2)[:, None] * norm_gain[None, :]).astype(jnp.bfloat16)
    chosen = routes.reshape(-1)
    onehot = (chosen[:, None] == jnp.arange(EXPERTS, dtype=jnp.int32)[None, :]).astype(jnp.int32)
    before = jnp.cumsum(onehot, axis=0) - onehot
    ranking = jnp.sum(before * onehot, axis=1)
    slot_index = chosen * replicas + ranking % replicas
    target = slot_index * capacity + ranking // replicas
    row_ids = jnp.arange(tok_rows * TOPK, dtype=jnp.int32) // TOPK
    source = jnp.full((slot_total * capacity,), tok_rows, jnp.int32).at[target].set(row_ids)
    padded = jnp.concatenate([normed, jnp.zeros((1, feat_block), jnp.bfloat16)], axis=0)
    packed = padded[source].reshape(ep_count, capacity, feat_block)
    tok, w_gate, w_up, w_down = move_all(
        packed, gate_weight, up_weight, down_weight,
        ep_count, lax.axis_size("mx"), lax.axis_size("my"), replicas,
    )
    tokens_in = tok.reshape(slot_rows, D)
    gate_proj = jnp.einsum("rd,spd->rsp", tokens_in, w_gate, preferred_element_type=jnp.float32)
    up_proj = jnp.einsum("rd,spd->rsp", tokens_in, w_up, preferred_element_type=jnp.float32)
    hidden = (jax.nn.silu(gate_proj) * up_proj).astype(jnp.bfloat16)
    expert_out = jnp.einsum("rsp,spd->rd", hidden, w_down, preferred_element_type=jnp.float32)
    expert_out = expert_out.reshape(slot_dev, slot_rows, D)
    returned = send_back(
        expert_out.reshape(slot_rows, D).astype(jnp.bfloat16), ep_count, lax.axis_size("my"), capacity
    ).reshape(slot_total * capacity, feat_block)
    picked = returned[target].reshape(tok_rows, TOPK, feat_block).astype(jnp.float32)
    weights_norm = gate_probs / jnp.sum(gate_probs, axis=1, keepdims=True)
    mixed = jnp.sum(weights_norm[:, :, None] * picked, axis=1)
    updated = stream_f + mixed
    normed_out = (updated * row_scale(updated, 3)[:, None] * final_gain[None, :]).astype(jnp.bfloat16)
    return (normed_out, updated.astype(jnp.bfloat16))


def solution(mesh):
    placed = (
        P(("ep", "mx"), None),
        P(("ep", "mx"), "my"),
        P(None, "my"),
        P("my"),
        P(None, ("ep", "my"), "mx"),
        P(None, ("ep", "my"), "mx"),
        P(None, ("ep", "my"), "mx"),
        P(("ep", "mx"), None),
        P(("ep", "mx"), None),
        P("my"),
    )
    return jax.shard_map(
        shards,
        mesh=mesh,
        in_specs=placed,
        out_specs=(P(("ep", "mx"), "my"), P(("ep", "mx"), "my")),
        check_vma=False,
    )
```

```python
import functools

import jax
import jax.numpy as jnp
import numpy as np
from jax import lax
from jax.experimental import pallas as pl
from jax.experimental.pallas import tpu as pltpu
from jax.sharding import PartitionSpec as P

D = 2048
EXPERTS = 8
TOPK = 2
MOST = 96


EPSILON = 1e-06
MESH = pl.DeviceIdType.MESH


def remote(src, dst, send, recv, device):
    return pltpu.make_async_remote_copy(
        src_ref=src, dst_ref=dst, send_sem=send, recv_sem=recv,
        device_id=device, device_id_type=MESH,
    )


def move_kernel(n_ep, n_mx, n_my, replicas, packed_ref, gate_ref, up_ref, down_ref,
                tok_ref, gate_out, up_out, down_out, tok_sems, send_z, recv_z, fwd_send, fwd_recv,
                send_x, recv_x, local_sem):
    j = lax.axis_index("ep")
    a = lax.axis_index("mx")
    m = lax.axis_index("my")
    fb = packed_ref.shape[2]
    wb = gate_ref.shape[2]
    cols_m = pl.ds(pl.multiple_of(m * fb, fb), fb)
    cols_a = pl.ds(pl.multiple_of(a * wb, wb), wb)
    barrier = pltpu.get_barrier_semaphore()
    peers = [(lax.rem(j + d, n_ep), a, m) for d in range(1, n_ep)]
    peers += [(j, lax.rem(a + e, n_mx), m) for e in range(1, n_mx)]
    peers += [(j, a, lax.rem(m + e, n_my)) for e in range(1, n_my)]
    for peer in peers:
        pl.semaphore_signal(barrier, inc=1, device_id=peer, device_id_type=MESH)
    pl.semaphore_wait(barrier, len(peers))
    pending = []
    weights = (gate_ref, up_ref, down_ref)
    outs = (gate_out, up_out, down_out)

    half_ring = n_ep // 2
    side = half_ring - 1
    parity = lax.rem(j, 2)
    partner = j + 1 - 2 * parity

    def start_direct(k):
        local = pltpu.make_async_copy(
            weights[k].at[j // replicas], outs[k].at[j, :, cols_a], local_sem.at[k])
        local.start()
        direct = []
        for d in range(1, side + 1):
            sign = 1 - 2 * lax.rem(j + d, 2)
            t = lax.rem(j + n_ep + sign * d, n_ep)
            copy = remote(weights[k].at[t // replicas], outs[k].at[j, :, cols_a],
                          send_z.at[k, d], recv_z.at[k, d], (t, a, m))
            copy.start()
            direct.append(copy)
        return local, direct

    def start_forward(k):
        forward = []
        for d in range(0, side + 1):
            src = lax.rem(j + n_ep - d + 2 * parity * d, n_ep)
            copy = remote(outs[k].at[src, :, cols_a], outs[k].at[src, :, cols_a],
                          fwd_send.at[k, d], fwd_recv.at[k, d], (partner, a, m))
            copy.start()
            forward.append(copy)
        return forward

    local, direct = start_direct(0)
    tok_local = pltpu.make_async_copy(packed_ref.at[j], tok_ref.at[j, :, cols_m], tok_sems.at[0, 0])
    tok_local.start()
    tok_z = []
    for d in range(1, n_ep):
        t = lax.rem(j + d, n_ep)
        copy = remote(packed_ref.at[t], tok_ref.at[j, :, cols_m], tok_sems.at[1, d], tok_sems.at[2, d], (t, a, m))
        copy.start()
        tok_z.append(copy)
    tok_my = []
    x_copies = []
    right = lax.rem(a + 1, n_mx)
    left = lax.rem(a + n_mx - 1, n_mx)
    half = n_ep // 2
    cols_l = pl.ds(pl.multiple_of(left * wb, wb), wb)
    cols_r = pl.ds(pl.multiple_of(right * wb, wb), wb)

    def relay(k, to_right, to_left):
        to_right.wait_recv()
        fwd_right = remote(outs[k].at[pl.ds(0, half), :, cols_l], outs[k].at[pl.ds(0, half), :, cols_l],
                           send_x.at[k, 2], recv_x.at[k, 2], (j, right, m))
        fwd_right.start()
        to_left.wait_recv()
        fwd_left = remote(outs[k].at[pl.ds(half, half), :, cols_r], outs[k].at[pl.ds(half, half), :, cols_r],
                          send_x.at[k, 3], recv_x.at[k, 3], (j, left, m))
        fwd_left.start()
        pending.extend([to_right, to_left])
        x_copies.extend([fwd_right, fwd_left])

    waiting = None
    for k in range(3):
        local.wait()
        for copy in direct:
            copy.wait_recv()
        pending.extend(direct)
        forward = start_forward(k)
        if k + 1 < 3:
            local, direct = start_direct(k + 1)
        if waiting is not None:
            relay(*waiting)
        for copy in forward:
            copy.wait_recv()
        pending.extend(forward)
        to_right = remote(outs[k].at[:, :, cols_a], outs[k].at[:, :, cols_a],
                          send_x.at[k, 0], recv_x.at[k, 0], (j, right, m))
        to_left = remote(outs[k].at[:, :, cols_a], outs[k].at[:, :, cols_a],
                         send_x.at[k, 1], recv_x.at[k, 1], (j, left, m))
        to_right.start()
        to_left.start()
        waiting = (k, to_right, to_left)
        if k == 1:
            tok_local.wait()
            for copy in tok_z:
                copy.wait_recv()
            pending.extend(tok_z)
            for e in range(1, n_my):
                b = lax.rem(m + e, n_my)
                copy = remote(tok_ref.at[:, :, cols_m], tok_ref.at[:, :, cols_m], tok_sems.at[3, e], tok_sems.at[4, e], (j, a, b))
                copy.start()
                tok_my.append(copy)
            pending.extend(tok_my)
    relay(*waiting)
    pending.extend(x_copies)
    for copy in pending:
        copy.wait_send()
    for copy in tok_my + x_copies:
        copy.wait_recv()


def move_all(packed, gate_weight, up_weight, down_weight, n_ep, n_mx, n_my, replicas):
    _, rows, fb = packed.shape
    _, units, wb = gate_weight.shape
    return pl.pallas_call(
        functools.partial(move_kernel, n_ep, n_mx, n_my, replicas),
        out_shape=(
            jax.ShapeDtypeStruct((n_ep, rows, n_my * fb), packed.dtype),
        ) + (jax.ShapeDtypeStruct((n_ep, units, n_mx * wb), gate_weight.dtype),) * 3,
        in_specs=[pl.BlockSpec(memory_space=pl.ANY)] * 4,
        out_specs=(pl.BlockSpec(memory_space=pl.ANY),) * 4,
        scratch_shapes=[
            pltpu.SemaphoreType.DMA((5, max(n_ep, n_my))),
            pltpu.SemaphoreType.DMA((3, n_ep)),
            pltpu.SemaphoreType.DMA((3, n_ep)),
            pltpu.SemaphoreType.DMA((3, n_ep)),
            pltpu.SemaphoreType.DMA((3, n_ep)),
            pltpu.SemaphoreType.DMA((3, max(n_mx, 4))),
            pltpu.SemaphoreType.DMA((3, max(n_mx, 4))),
            pltpu.SemaphoreType.DMA((3,)),
        ],
        compiler_params=pltpu.CompilerParams(has_side_effects=True, collective_id=0),
    )(packed, gate_weight, up_weight, down_weight)


def back_kernel(n_ep, n_my, ex_ref, out_ref, rx_core, chip_part, rx_y, result, sems):
    j = lax.axis_index("ep")
    a = lax.axis_index("mx")
    m = lax.axis_index("my")
    fb = out_ref.shape[2]
    cap = out_ref.shape[1]
    chips = n_my // 2
    core = lax.rem(m, 2)
    y = m // 2
    partner = m + 1 - 2 * core
    barrier = pltpu.get_barrier_semaphore()
    peers = [(j, a, partner)]
    peers += [(j, a, lax.rem(y + e, chips) * 2 + core) for e in range(1, chips)]
    peers += [(lax.rem(j + d, n_ep), a, m) for d in range(1, n_ep)]
    for peer in peers:
        pl.semaphore_signal(barrier, inc=1, device_id=peer, device_id_type=MESH)
    pl.semaphore_wait(barrier, len(peers))

    def cols(block):
        return pl.ds(pl.multiple_of(block * fb, fb), fb)

    rows = result.shape[0]
    half_rows = rows // 2
    half_slots = n_ep // 2
    to_core = []
    for h in range(2):
        part = pl.ds(h * half_rows, half_rows)
        for i in range(chips):
            copy = remote(ex_ref.at[part, cols(1 - core + 2 * i)], rx_core.at[i, part],
                          sems.at[0, i + chips * h], sems.at[1, i + chips * h], (j, a, partner))
            copy.start()
            to_core.append(copy)
    to_y = []
    for h in range(2):
        part = pl.ds(h * half_rows, half_rows)
        for copy in to_core[h * chips:(h + 1) * chips]:
            copy.wait_recv()
        for i in range(chips):
            own = ex_ref[part, cols(core + 2 * i)].astype(jnp.float32)
            chip_part[i, part] = (own + rx_core[i, part].astype(jnp.float32)).astype(chip_part.dtype)
        for e in range(1, chips):
            other = lax.rem(y + e, chips)
            copy = remote(chip_part.at[other, part], rx_y.at[e - 1, part],
                          sems.at[2 + 2 * h, e], sems.at[3 + 2 * h, e], (j, a, other * 2 + core))
            copy.start()
            to_y.append(copy)
    to_z = []
    for h in range(2):
        part = pl.ds(h * half_rows, half_rows)
        for copy in to_y[h * (chips - 1):(h + 1) * (chips - 1)]:
            copy.wait_recv()
        total = chip_part[y, part].astype(jnp.float32)
        for e in range(1, chips):
            total = total + rx_y[e - 1, part].astype(jnp.float32)
        result[part] = total.astype(result.dtype)
        for t in range(h * half_slots, (h + 1) * half_slots):
            rows_t = result.at[pl.ds(t * cap, cap)]

            @pl.when(t == j)
            def _():
                local = pltpu.make_async_copy(rows_t, out_ref.at[j], sems.at[6, t])
                local.start()
                local.wait()

            copy = remote(rows_t, out_ref.at[j], sems.at[7, t], sems.at[8, j], (t, a, m))

            @pl.when(t != j)
            def _():
                copy.start()

            to_z.append((t, copy))
    for copy in to_core + to_y:
        copy.wait_send()
    for t, copy in to_z:
        @pl.when(t != j)
        def _():
            copy.wait_send()
    for s in range(n_ep):
        incoming = remote(result.at[pl.ds(0, cap)], out_ref.at[s], sems.at[7, s], sems.at[8, s], (s, a, m))

        @pl.when(s != j)
        def _():
            incoming.wait_recv()


def send_back(ex, n_ep, n_my, cap):
    rows, width = ex.shape
    fb = width // n_my
    return pl.pallas_call(
        functools.partial(back_kernel, n_ep, n_my),
        out_shape=jax.ShapeDtypeStruct((n_ep, cap, fb), ex.dtype),
        in_specs=[pl.BlockSpec(memory_space=pltpu.VMEM)],
        out_specs=pl.BlockSpec(memory_space=pl.ANY),
        scratch_shapes=[
            pltpu.VMEM((n_my // 2, rows, fb), ex.dtype),
            pltpu.VMEM((n_my // 2, rows, fb), ex.dtype),
            pltpu.VMEM((n_my // 2 - 1, rows, fb), ex.dtype),
            pltpu.VMEM((rows, fb), ex.dtype),
            pltpu.SemaphoreType.DMA((9, max(n_ep, n_my))),
        ],
        compiler_params=pltpu.CompilerParams(has_side_effects=True, collective_id=1),
    )(ex)


def sum_kernel(n_my, x_ref, o_ref, slots, send, recv):
    j = lax.axis_index("ep")
    a = lax.axis_index("mx")
    m = lax.axis_index("my")
    barrier = pltpu.get_barrier_semaphore()
    for e in range(1, n_my):
        pl.semaphore_signal(barrier, inc=1, device_id=(j, a, lax.rem(m + e, n_my)), device_id_type=MESH)
    pl.semaphore_wait(barrier, n_my - 1)
    slots[m] = x_ref[...]
    copies = []
    for e in range(1, n_my):
        b = lax.rem(m + e, n_my)
        copy = remote(x_ref, slots.at[m], send.at[e], recv.at[e], (j, a, b))
        copy.start()
        copies.append(copy)
    for copy in copies:
        copy.wait_send()
    for copy in copies:
        copy.wait_recv()
    o_ref[...] = jnp.sum(slots[...], axis=0)


def sum_over_my(values, kernel_id):
    n_my = lax.axis_size("my")
    row = values.reshape(1, -1)
    total = pl.pallas_call(
        functools.partial(sum_kernel, n_my),
        out_shape=jax.ShapeDtypeStruct(row.shape, row.dtype),
        in_specs=[pl.BlockSpec(memory_space=pltpu.VMEM)],
        out_specs=pl.BlockSpec(memory_space=pltpu.VMEM),
        scratch_shapes=[
            pltpu.VMEM((n_my,) + row.shape, row.dtype),
            pltpu.SemaphoreType.DMA((n_my,)),
            pltpu.SemaphoreType.DMA((n_my,)),
        ],
        compiler_params=pltpu.CompilerParams(has_side_effects=True, collective_id=kernel_id),
    )(row)
    return total.reshape(values.shape)


def row_scale(stream_f, kernel_id):
    partial_sq = jnp.sum(stream_f * stream_f, axis=1)
    row_total = sum_over_my(partial_sq, kernel_id)
    return lax.rsqrt(row_total / D + EPSILON)


def shards(
    context,
    resid_in,
    out_weight,
    norm_gain,
    gate_weight,
    up_weight,
    down_weight,
    routes,
    gate_probs,
    final_gain,
):
    ep_count = lax.axis_size("ep")
    slot_dev = max(1, EXPERTS // ep_count)
    slot_total = slot_dev * ep_count
    replicas = slot_total // EXPERTS
    capacity = MOST // replicas
    tok_rows = context.shape[0]
    feat_block = resid_in.shape[1]
    piece_units = gate_weight.shape[1]
    slot_rows = ep_count * capacity

    projected = jnp.dot(context, out_weight, preferred_element_type=jnp.float32)
    stream = (projected + resid_in.astype(jnp.float32)).astype(jnp.bfloat16)
    stream_f = stream.astype(jnp.float32)
    normed = (stream_f * row_scale(stream_f, 2)[:, None] * norm_gain[None, :]).astype(jnp.bfloat16)
    chosen = routes.reshape(-1)
    onehot = (chosen[:, None] == jnp.arange(EXPERTS, dtype=jnp.int32)[None, :]).astype(jnp.int32)
    before = jnp.cumsum(onehot, axis=0) - onehot
    ranking = jnp.sum(before * onehot, axis=1)
    slot_index = chosen * replicas + ranking % replicas
    target = slot_index * capacity + ranking // replicas
    row_ids = jnp.arange(tok_rows * TOPK, dtype=jnp.int32) // TOPK
    source = jnp.full((slot_total * capacity,), tok_rows, jnp.int32).at[target].set(row_ids)
    padded = jnp.concatenate([normed, jnp.zeros((1, feat_block), jnp.bfloat16)], axis=0)
    packed = padded[source].reshape(ep_count, capacity, feat_block)
    tok, w_gate, w_up, w_down = move_all(
        packed, gate_weight, up_weight, down_weight,
        ep_count, lax.axis_size("mx"), lax.axis_size("my"), replicas,
    )
    tokens_in = tok.reshape(slot_rows, D)
    gate_proj = jnp.einsum("rd,spd->rsp", tokens_in, w_gate, preferred_element_type=jnp.float32)
    up_proj = jnp.einsum("rd,spd->rsp", tokens_in, w_up, preferred_element_type=jnp.float32)
    hidden = (jax.nn.silu(gate_proj) * up_proj).astype(jnp.bfloat16)
    expert_out = jnp.einsum("rsp,spd->rd", hidden, w_down, preferred_element_type=jnp.float32)
    expert_out = expert_out.reshape(slot_dev, slot_rows, D)
    returned = send_back(
        expert_out.reshape(slot_rows, D).astype(jnp.bfloat16), ep_count, lax.axis_size("my"), capacity
    ).reshape(slot_total * capacity, feat_block)
    picked = returned[target].reshape(tok_rows, TOPK, feat_block).astype(jnp.float32)
    weights_norm = gate_probs / jnp.sum(gate_probs, axis=1, keepdims=True)
    mixed = jnp.sum(weights_norm[:, :, None] * picked, axis=1)
    updated = stream_f + mixed
    normed_out = (updated * row_scale(updated, 3)[:, None] * final_gain[None, :]).astype(jnp.bfloat16)
    return (normed_out, updated.astype(jnp.bfloat16))


def solution(mesh):
    placed = (
        P(("ep", "mx"), None),
        P(("ep", "mx"), "my"),
        P(None, "my"),
        P("my"),
        P(None, ("ep", "my"), "mx"),
        P(None, ("ep", "my"), "mx"),
        P(None, ("ep", "my"), "mx"),
        P(("ep", "mx"), None),
        P(("ep", "mx"), None),
        P("my"),
    )
    return jax.shard_map(
        shards,
        mesh=mesh,
        in_specs=placed,
        out_specs=(P(("ep", "mx"), "my"), P(("ep", "mx"), "my")),
        check_vma=False,
    )
```

```python
import functools

import jax
import jax.numpy as jnp
import numpy as np
from jax import lax
from jax.experimental import pallas as pl
from jax.experimental.pallas import tpu as pltpu
from jax.sharding import PartitionSpec as P

D = 2048
EXPERTS = 8
TOPK = 2
MOST = 96


EPSILON = 1e-06
MESH = pl.DeviceIdType.MESH


def remote(src, dst, send, recv, device):
    return pltpu.make_async_remote_copy(
        src_ref=src, dst_ref=dst, send_sem=send, recv_sem=recv,
        device_id=device, device_id_type=MESH,
    )


def move_kernel(n_ep, n_mx, n_my, replicas, packed_ref, gate_ref, up_ref, down_ref,
                tok_ref, gate_out, up_out, down_out, tok_sems, send_z, recv_z, fwd_send, fwd_recv,
                send_x, recv_x, local_sem):
    j = lax.axis_index("ep")
    a = lax.axis_index("mx")
    m = lax.axis_index("my")
    fb = packed_ref.shape[2]
    wb = gate_ref.shape[2]
    cols_m = pl.ds(pl.multiple_of(m * fb, fb), fb)
    cols_a = pl.ds(pl.multiple_of(a * wb, wb), wb)
    barrier = pltpu.get_barrier_semaphore()
    peers = [(lax.rem(j + d, n_ep), a, m) for d in range(1, n_ep)]
    peers += [(j, lax.rem(a + e, n_mx), m) for e in range(1, n_mx)]
    peers += [(j, a, lax.rem(m + e, n_my)) for e in range(1, n_my)]
    for peer in peers:
        pl.semaphore_signal(barrier, inc=1, device_id=peer, device_id_type=MESH)
    pl.semaphore_wait(barrier, len(peers))
    pending = []
    weights = (gate_ref, up_ref, down_ref)
    outs = (gate_out, up_out, down_out)

    half_ring = n_ep // 2
    side = half_ring - 1
    parity = lax.rem(j, 2)
    partner = j + 1 - 2 * parity

    def start_direct(k):
        local = pltpu.make_async_copy(
            weights[k].at[j // replicas], outs[k].at[j, :, cols_a], local_sem.at[k])
        local.start()
        direct = []
        for d in range(1, side + 1):
            sign = 1 - 2 * lax.rem(j + d, 2)
            t = lax.rem(j + n_ep + sign * d, n_ep)
            copy = remote(weights[k].at[t // replicas], outs[k].at[j, :, cols_a],
                          send_z.at[k, d], recv_z.at[k, d], (t, a, m))
            copy.start()
            direct.append(copy)
        return local, direct

    def start_forward(k):
        forward = []
        for d in range(0, side + 1):
            src = lax.rem(j + n_ep - d + 2 * parity * d, n_ep)
            copy = remote(outs[k].at[src, :, cols_a], outs[k].at[src, :, cols_a],
                          fwd_send.at[k, d], fwd_recv.at[k, d], (partner, a, m))
            copy.start()
            forward.append(copy)
        return forward

    local, direct = start_direct(0)
    tok_local = pltpu.make_async_copy(packed_ref.at[j], tok_ref.at[j, :, cols_m], tok_sems.at[0, 0])
    tok_local.start()
    tok_z = []
    for d in range(1, n_ep):
        t = lax.rem(j + d, n_ep)
        copy = remote(packed_ref.at[t], tok_ref.at[j, :, cols_m], tok_sems.at[1, d], tok_sems.at[2, d], (t, a, m))
        copy.start()
        tok_z.append(copy)
    tok_my = []
    x_copies = []
    right = lax.rem(a + 1, n_mx)
    left = lax.rem(a + n_mx - 1, n_mx)
    half = n_ep // 2
    cols_l = pl.ds(pl.multiple_of(left * wb, wb), wb)
    cols_r = pl.ds(pl.multiple_of(right * wb, wb), wb)

    def relay(k, to_right, to_left):
        to_right.wait_recv()
        fwd_right = remote(outs[k].at[pl.ds(0, half), :, cols_l], outs[k].at[pl.ds(0, half), :, cols_l],
                           send_x.at[k, 2], recv_x.at[k, 2], (j, right, m))
        fwd_right.start()
        to_left.wait_recv()
        fwd_left = remote(outs[k].at[pl.ds(half, half), :, cols_r], outs[k].at[pl.ds(half, half), :, cols_r],
                          send_x.at[k, 3], recv_x.at[k, 3], (j, left, m))
        fwd_left.start()
        pending.extend([to_right, to_left])
        x_copies.extend([fwd_right, fwd_left])

    waiting = None
    for k in range(3):
        if waiting is not None:
            relay(*waiting)
        local.wait()
        for copy in direct:
            copy.wait_recv()
        pending.extend(direct)
        forward = start_forward(k)
        if k + 1 < 3:
            local, direct = start_direct(k + 1)
        for copy in forward:
            copy.wait_recv()
        pending.extend(forward)
        to_right = remote(outs[k].at[:, :, cols_a], outs[k].at[:, :, cols_a],
                          send_x.at[k, 0], recv_x.at[k, 0], (j, right, m))
        to_left = remote(outs[k].at[:, :, cols_a], outs[k].at[:, :, cols_a],
                         send_x.at[k, 1], recv_x.at[k, 1], (j, left, m))
        to_right.start()
        to_left.start()
        waiting = (k, to_right, to_left)
        if k == 0:
            tok_local.wait()
            for copy in tok_z:
                copy.wait_recv()
            pending.extend(tok_z)
            for e in range(1, n_my):
                b = lax.rem(m + e, n_my)
                copy = remote(tok_ref.at[:, :, cols_m], tok_ref.at[:, :, cols_m], tok_sems.at[3, e], tok_sems.at[4, e], (j, a, b))
                copy.start()
                tok_my.append(copy)
            pending.extend(tok_my)
    relay(*waiting)
    pending.extend(x_copies)
    for copy in pending:
        copy.wait_send()
    for copy in tok_my + x_copies:
        copy.wait_recv()


def move_all(packed, gate_weight, up_weight, down_weight, n_ep, n_mx, n_my, replicas):
    _, rows, fb = packed.shape
    _, units, wb = gate_weight.shape
    return pl.pallas_call(
        functools.partial(move_kernel, n_ep, n_mx, n_my, replicas),
        out_shape=(
            jax.ShapeDtypeStruct((n_ep, rows, n_my * fb), packed.dtype),
        ) + (jax.ShapeDtypeStruct((n_ep, units, n_mx * wb), gate_weight.dtype),) * 3,
        in_specs=[pl.BlockSpec(memory_space=pl.ANY)] * 4,
        out_specs=(pl.BlockSpec(memory_space=pl.ANY),) * 4,
        scratch_shapes=[
            pltpu.SemaphoreType.DMA((5, max(n_ep, n_my))),
            pltpu.SemaphoreType.DMA((3, n_ep)),
            pltpu.SemaphoreType.DMA((3, n_ep)),
            pltpu.SemaphoreType.DMA((3, n_ep)),
            pltpu.SemaphoreType.DMA((3, n_ep)),
            pltpu.SemaphoreType.DMA((3, max(n_mx, 4))),
            pltpu.SemaphoreType.DMA((3, max(n_mx, 4))),
            pltpu.SemaphoreType.DMA((3,)),
        ],
        compiler_params=pltpu.CompilerParams(has_side_effects=True, collective_id=0),
    )(packed, gate_weight, up_weight, down_weight)


def back_kernel(n_ep, n_my, ex_ref, out_ref, rx_core, chip_part, rx_y, result, sems):
    j = lax.axis_index("ep")
    a = lax.axis_index("mx")
    m = lax.axis_index("my")
    fb = out_ref.shape[2]
    cap = out_ref.shape[1]
    chips = n_my // 2
    core = lax.rem(m, 2)
    y = m // 2
    partner = m + 1 - 2 * core
    barrier = pltpu.get_barrier_semaphore()
    peers = [(j, a, partner)]
    peers += [(j, a, lax.rem(y + e, chips) * 2 + core) for e in range(1, chips)]
    peers += [(lax.rem(j + d, n_ep), a, m) for d in range(1, n_ep)]
    for peer in peers:
        pl.semaphore_signal(barrier, inc=1, device_id=peer, device_id_type=MESH)
    pl.semaphore_wait(barrier, len(peers))

    def cols(block):
        return pl.ds(pl.multiple_of(block * fb, fb), fb)

    rows = result.shape[0]
    half_rows = rows // 2
    half_slots = n_ep // 2
    to_core = []
    for h in range(2):
        part = pl.ds(h * half_rows, half_rows)
        for i in range(chips):
            copy = remote(ex_ref.at[part, cols(1 - core + 2 * i)], rx_core.at[i, part],
                          sems.at[0, i + chips * h], sems.at[1, i + chips * h], (j, a, partner))
            copy.start()
            to_core.append(copy)
    to_y = []
    for h in range(2):
        part = pl.ds(h * half_rows, half_rows)
        for copy in to_core[h * chips:(h + 1) * chips]:
            copy.wait_recv()
        for i in range(chips):
            own = ex_ref[part, cols(core + 2 * i)].astype(jnp.float32)
            chip_part[i, part] = (own + rx_core[i, part].astype(jnp.float32)).astype(chip_part.dtype)
        for e in range(1, chips):
            other = lax.rem(y + e, chips)
            copy = remote(chip_part.at[other, part], rx_y.at[e - 1, part],
                          sems.at[2 + 2 * h, e], sems.at[3 + 2 * h, e], (j, a, other * 2 + core))
            copy.start()
            to_y.append(copy)
    to_z = []
    for h in range(2):
        part = pl.ds(h * half_rows, half_rows)
        for copy in to_y[h * (chips - 1):(h + 1) * (chips - 1)]:
            copy.wait_recv()
        total = chip_part[y, part].astype(jnp.float32)
        for e in range(1, chips):
            total = total + rx_y[e - 1, part].astype(jnp.float32)
        result[part] = total.astype(result.dtype)
        for t in range(h * half_slots, (h + 1) * half_slots):
            rows_t = result.at[pl.ds(t * cap, cap)]

            @pl.when(t == j)
            def _():
                local = pltpu.make_async_copy(rows_t, out_ref.at[j], sems.at[6, t])
                local.start()
                local.wait()

            copy = remote(rows_t, out_ref.at[j], sems.at[7, t], sems.at[8, j], (t, a, m))

            @pl.when(t != j)
            def _():
                copy.start()

            to_z.append((t, copy))
    for copy in to_core + to_y:
        copy.wait_send()
    for t, copy in to_z:
        @pl.when(t != j)
        def _():
            copy.wait_send()
    for s in range(n_ep):
        incoming = remote(result.at[pl.ds(0, cap)], out_ref.at[s], sems.at[7, s], sems.at[8, s], (s, a, m))

        @pl.when(s != j)
        def _():
            incoming.wait_recv()


def send_back(ex, n_ep, n_my, cap):
    rows, width = ex.shape
    fb = width // n_my
    return pl.pallas_call(
        functools.partial(back_kernel, n_ep, n_my),
        out_shape=jax.ShapeDtypeStruct((n_ep, cap, fb), ex.dtype),
        in_specs=[pl.BlockSpec(memory_space=pltpu.VMEM)],
        out_specs=pl.BlockSpec(memory_space=pl.ANY),
        scratch_shapes=[
            pltpu.VMEM((n_my // 2, rows, fb), ex.dtype),
            pltpu.VMEM((n_my // 2, rows, fb), ex.dtype),
            pltpu.VMEM((n_my // 2 - 1, rows, fb), ex.dtype),
            pltpu.VMEM((rows, fb), ex.dtype),
            pltpu.SemaphoreType.DMA((9, max(n_ep, n_my))),
        ],
        compiler_params=pltpu.CompilerParams(has_side_effects=True, collective_id=1),
    )(ex)


def sum_kernel(n_my, x_ref, o_ref, slots, send, recv):
    j = lax.axis_index("ep")
    a = lax.axis_index("mx")
    m = lax.axis_index("my")
    barrier = pltpu.get_barrier_semaphore()
    for e in range(1, n_my):
        pl.semaphore_signal(barrier, inc=1, device_id=(j, a, lax.rem(m + e, n_my)), device_id_type=MESH)
    pl.semaphore_wait(barrier, n_my - 1)
    slots[m] = x_ref[...]
    copies = []
    for e in range(1, n_my):
        b = lax.rem(m + e, n_my)
        copy = remote(x_ref, slots.at[m], send.at[e], recv.at[e], (j, a, b))
        copy.start()
        copies.append(copy)
    for copy in copies:
        copy.wait_send()
    for copy in copies:
        copy.wait_recv()
    o_ref[...] = jnp.sum(slots[...], axis=0)


def sum_over_my(values, kernel_id):
    n_my = lax.axis_size("my")
    row = values.reshape(1, -1)
    total = pl.pallas_call(
        functools.partial(sum_kernel, n_my),
        out_shape=jax.ShapeDtypeStruct(row.shape, row.dtype),
        in_specs=[pl.BlockSpec(memory_space=pltpu.VMEM)],
        out_specs=pl.BlockSpec(memory_space=pltpu.VMEM),
        scratch_shapes=[
            pltpu.VMEM((n_my,) + row.shape, row.dtype),
            pltpu.SemaphoreType.DMA((n_my,)),
            pltpu.SemaphoreType.DMA((n_my,)),
        ],
        compiler_params=pltpu.CompilerParams(has_side_effects=True, collective_id=kernel_id),
    )(row)
    return total.reshape(values.shape)


def row_scale(stream_f, kernel_id):
    partial_sq = jnp.sum(stream_f * stream_f, axis=1)
    row_total = sum_over_my(partial_sq, kernel_id)
    return lax.rsqrt(row_total / D + EPSILON)


def shards(
    context,
    resid_in,
    out_weight,
    norm_gain,
    gate_weight,
    up_weight,
    down_weight,
    routes,
    gate_probs,
    final_gain,
):
    ep_count = lax.axis_size("ep")
    slot_dev = max(1, EXPERTS // ep_count)
    slot_total = slot_dev * ep_count
    replicas = slot_total // EXPERTS
    capacity = MOST // replicas
    tok_rows = context.shape[0]
    feat_block = resid_in.shape[1]
    piece_units = gate_weight.shape[1]
    slot_rows = ep_count * capacity

    projected = jnp.dot(context, out_weight, preferred_element_type=jnp.float32)
    stream = (projected + resid_in.astype(jnp.float32)).astype(jnp.bfloat16)
    stream_f = stream.astype(jnp.float32)
    normed = (stream_f * row_scale(stream_f, 2)[:, None] * norm_gain[None, :]).astype(jnp.bfloat16)
    chosen = routes.reshape(-1)
    onehot = (chosen[:, None] == jnp.arange(EXPERTS, dtype=jnp.int32)[None, :]).astype(jnp.int32)
    before = jnp.cumsum(onehot, axis=0) - onehot
    ranking = jnp.sum(before * onehot, axis=1)
    slot_index = chosen * replicas + ranking % replicas
    target = slot_index * capacity + ranking // replicas
    row_ids = jnp.arange(tok_rows * TOPK, dtype=jnp.int32) // TOPK
    source = jnp.full((slot_total * capacity,), tok_rows, jnp.int32).at[target].set(row_ids)
    padded = jnp.concatenate([normed, jnp.zeros((1, feat_block), jnp.bfloat16)], axis=0)
    packed = padded[source].reshape(ep_count, capacity, feat_block)
    tok, w_gate, w_up, w_down = move_all(
        packed, gate_weight, up_weight, down_weight,
        ep_count, lax.axis_size("mx"), lax.axis_size("my"), replicas,
    )
    tokens_in = tok.reshape(slot_rows, D)
    gate_proj = jnp.einsum("rd,spd->rsp", tokens_in, w_gate, preferred_element_type=jnp.float32)
    up_proj = jnp.einsum("rd,spd->rsp", tokens_in, w_up, preferred_element_type=jnp.float32)
    hidden = (jax.nn.silu(gate_proj) * up_proj).astype(jnp.bfloat16)
    expert_out = jnp.einsum("rsp,spd->rd", hidden, w_down, preferred_element_type=jnp.float32)
    expert_out = expert_out.reshape(slot_dev, slot_rows, D)
    returned = send_back(
        expert_out.reshape(slot_rows, D).astype(jnp.bfloat16), ep_count, lax.axis_size("my"), capacity
    ).reshape(slot_total * capacity, feat_block)
    picked = returned[target].reshape(tok_rows, TOPK, feat_block).astype(jnp.float32)
    weights_norm = gate_probs / jnp.sum(gate_probs, axis=1, keepdims=True)
    mixed = jnp.sum(weights_norm[:, :, None] * picked, axis=1)
    updated = stream_f + mixed
    normed_out = (updated * row_scale(updated, 3)[:, None] * final_gain[None, :]).astype(jnp.bfloat16)
    return (normed_out, updated.astype(jnp.bfloat16))


def solution(mesh):
    placed = (
        P(("ep", "mx"), None),
        P(("ep", "mx"), "my"),
        P(None, "my"),
        P("my"),
        P(None, ("ep", "my"), "mx"),
        P(None, ("ep", "my"), "mx"),
        P(None, ("ep", "my"), "mx"),
        P(("ep", "mx"), None),
        P(("ep", "mx"), None),
        P("my"),
    )
    return jax.shard_map(
        shards,
        mesh=mesh,
        in_specs=placed,
        out_specs=(P(("ep", "mx"), "my"), P(("ep", "mx"), "my")),
        check_vma=False,
    )
```

```python
import functools

import jax
import jax.numpy as jnp
import numpy as np
from jax import lax
from jax.experimental import pallas as pl
from jax.experimental.pallas import tpu as pltpu
from jax.sharding import PartitionSpec as P

D = 2048
EXPERTS = 8
TOPK = 2
MOST = 96


EPSILON = 1e-06
MESH = pl.DeviceIdType.MESH


def remote(src, dst, send, recv, device):
    return pltpu.make_async_remote_copy(
        src_ref=src, dst_ref=dst, send_sem=send, recv_sem=recv,
        device_id=device, device_id_type=MESH,
    )


def move_kernel(n_ep, n_mx, n_my, replicas, packed_ref, gate_ref, up_ref, down_ref,
                tok_ref, gate_out, up_out, down_out, tok_sems, send_z, recv_z, fwd_send, fwd_recv,
                send_x, recv_x, local_sem):
    j = lax.axis_index("ep")
    a = lax.axis_index("mx")
    m = lax.axis_index("my")
    fb = packed_ref.shape[2]
    wb = gate_ref.shape[2]
    cols_m = pl.ds(pl.multiple_of(m * fb, fb), fb)
    cols_a = pl.ds(pl.multiple_of(a * wb, wb), wb)
    barrier = pltpu.get_barrier_semaphore()
    peers = [(lax.rem(j + d, n_ep), a, m) for d in range(1, n_ep)]
    peers += [(j, lax.rem(a + e, n_mx), m) for e in range(1, n_mx)]
    peers += [(j, a, lax.rem(m + e, n_my)) for e in range(1, n_my)]
    for peer in peers:
        pl.semaphore_signal(barrier, inc=1, device_id=peer, device_id_type=MESH)
    pl.semaphore_wait(barrier, len(peers))
    pending = []
    weights = (gate_ref, up_ref, down_ref)
    outs = (gate_out, up_out, down_out)

    half_ring = n_ep // 2
    side = half_ring - 1
    parity = lax.rem(j, 2)
    partner = j + 1 - 2 * parity

    def start_direct(k):
        local = pltpu.make_async_copy(
            weights[k].at[j // replicas], outs[k].at[j, :, cols_a], local_sem.at[k])
        local.start()
        direct = []
        for d in range(1, side + 1):
            sign = 1 - 2 * lax.rem(j + d, 2)
            t = lax.rem(j + n_ep + sign * d, n_ep)
            copy = remote(weights[k].at[t // replicas], outs[k].at[j, :, cols_a],
                          send_z.at[k, d], recv_z.at[k, d], (t, a, m))
            copy.start()
            direct.append(copy)
        return local, direct

    def start_forward(k, first, last):
        forward = []
        for d in range(first, last):
            src = lax.rem(j + n_ep - d + 2 * parity * d, n_ep)
            copy = remote(outs[k].at[src, :, cols_a], outs[k].at[src, :, cols_a],
                          fwd_send.at[k, d], fwd_recv.at[k, d], (partner, a, m))
            copy.start()
            forward.append(copy)
        return forward

    local, direct = start_direct(0)
    tok_local = pltpu.make_async_copy(packed_ref.at[j], tok_ref.at[j, :, cols_m], tok_sems.at[0, 0])
    tok_local.start()
    tok_z = []
    for d in range(1, n_ep):
        t = lax.rem(j + d, n_ep)
        copy = remote(packed_ref.at[t], tok_ref.at[j, :, cols_m], tok_sems.at[1, d], tok_sems.at[2, d], (t, a, m))
        copy.start()
        tok_z.append(copy)
    tok_my = []
    x_copies = []
    right = lax.rem(a + 1, n_mx)
    left = lax.rem(a + n_mx - 1, n_mx)
    half = n_ep // 2
    cols_l = pl.ds(pl.multiple_of(left * wb, wb), wb)
    cols_r = pl.ds(pl.multiple_of(right * wb, wb), wb)

    def relay(k, to_right, to_left):
        to_right.wait_recv()
        fwd_right = remote(outs[k].at[pl.ds(0, half), :, cols_l], outs[k].at[pl.ds(0, half), :, cols_l],
                           send_x.at[k, 2], recv_x.at[k, 2], (j, right, m))
        fwd_right.start()
        to_left.wait_recv()
        fwd_left = remote(outs[k].at[pl.ds(half, half), :, cols_r], outs[k].at[pl.ds(half, half), :, cols_r],
                          send_x.at[k, 3], recv_x.at[k, 3], (j, left, m))
        fwd_left.start()
        pending.extend([to_right, to_left])
        x_copies.extend([fwd_right, fwd_left])

    waiting = None
    for k in range(3):
        local.wait()
        forward = start_forward(k, 0, 1)
        for copy in direct:
            copy.wait_recv()
        pending.extend(direct)
        forward += start_forward(k, 1, side + 1)
        if k + 1 < 3:
            local, direct = start_direct(k + 1)
        if waiting is not None:
            relay(*waiting)
        for copy in forward:
            copy.wait_recv()
        pending.extend(forward)
        to_right = remote(outs[k].at[:, :, cols_a], outs[k].at[:, :, cols_a],
                          send_x.at[k, 0], recv_x.at[k, 0], (j, right, m))
        to_left = remote(outs[k].at[:, :, cols_a], outs[k].at[:, :, cols_a],
                         send_x.at[k, 1], recv_x.at[k, 1], (j, left, m))
        to_right.start()
        to_left.start()
        waiting = (k, to_right, to_left)
        if k == 0:
            tok_local.wait()
            for copy in tok_z:
                copy.wait_recv()
            pending.extend(tok_z)
            for e in range(1, n_my):
                b = lax.rem(m + e, n_my)
                copy = remote(tok_ref.at[:, :, cols_m], tok_ref.at[:, :, cols_m], tok_sems.at[3, e], tok_sems.at[4, e], (j, a, b))
                copy.start()
                tok_my.append(copy)
            pending.extend(tok_my)
    relay(*waiting)
    pending.extend(x_copies)
    for copy in pending:
        copy.wait_send()
    for copy in tok_my + x_copies:
        copy.wait_recv()


def move_all(packed, gate_weight, up_weight, down_weight, n_ep, n_mx, n_my, replicas):
    _, rows, fb = packed.shape
    _, units, wb = gate_weight.shape
    return pl.pallas_call(
        functools.partial(move_kernel, n_ep, n_mx, n_my, replicas),
        out_shape=(
            jax.ShapeDtypeStruct((n_ep, rows, n_my * fb), packed.dtype),
        ) + (jax.ShapeDtypeStruct((n_ep, units, n_mx * wb), gate_weight.dtype),) * 3,
        in_specs=[pl.BlockSpec(memory_space=pl.ANY)] * 4,
        out_specs=(pl.BlockSpec(memory_space=pl.ANY),) * 4,
        scratch_shapes=[
            pltpu.SemaphoreType.DMA((5, max(n_ep, n_my))),
            pltpu.SemaphoreType.DMA((3, n_ep)),
            pltpu.SemaphoreType.DMA((3, n_ep)),
            pltpu.SemaphoreType.DMA((3, n_ep)),
            pltpu.SemaphoreType.DMA((3, n_ep)),
            pltpu.SemaphoreType.DMA((3, max(n_mx, 4))),
            pltpu.SemaphoreType.DMA((3, max(n_mx, 4))),
            pltpu.SemaphoreType.DMA((3,)),
        ],
        compiler_params=pltpu.CompilerParams(has_side_effects=True, collective_id=0),
    )(packed, gate_weight, up_weight, down_weight)


def back_kernel(n_ep, n_my, ex_ref, out_ref, rx_core, chip_part, rx_y, result, sems):
    j = lax.axis_index("ep")
    a = lax.axis_index("mx")
    m = lax.axis_index("my")
    fb = out_ref.shape[2]
    cap = out_ref.shape[1]
    chips = n_my // 2
    core = lax.rem(m, 2)
    y = m // 2
    partner = m + 1 - 2 * core
    barrier = pltpu.get_barrier_semaphore()
    peers = [(j, a, partner)]
    peers += [(j, a, lax.rem(y + e, chips) * 2 + core) for e in range(1, chips)]
    peers += [(lax.rem(j + d, n_ep), a, m) for d in range(1, n_ep)]
    for peer in peers:
        pl.semaphore_signal(barrier, inc=1, device_id=peer, device_id_type=MESH)
    pl.semaphore_wait(barrier, len(peers))

    def cols(block):
        return pl.ds(pl.multiple_of(block * fb, fb), fb)

    rows = result.shape[0]
    half_rows = rows // 2
    half_slots = n_ep // 2
    to_core = []
    for h in range(2):
        part = pl.ds(h * half_rows, half_rows)
        for i in range(chips):
            copy = remote(ex_ref.at[part, cols(1 - core + 2 * i)], rx_core.at[i, part],
                          sems.at[0, i + chips * h], sems.at[1, i + chips * h], (j, a, partner))
            copy.start()
            to_core.append(copy)
    to_y = []
    for h in range(2):
        part = pl.ds(h * half_rows, half_rows)
        for copy in to_core[h * chips:(h + 1) * chips]:
            copy.wait_recv()
        for i in range(chips):
            own = ex_ref[part, cols(core + 2 * i)].astype(jnp.float32)
            chip_part[i, part] = (own + rx_core[i, part].astype(jnp.float32)).astype(chip_part.dtype)
        for e in range(1, chips):
            other = lax.rem(y + e, chips)
            copy = remote(chip_part.at[other, part], rx_y.at[e - 1, part],
                          sems.at[2 + 2 * h, e], sems.at[3 + 2 * h, e], (j, a, other * 2 + core))
            copy.start()
            to_y.append(copy)
    to_z = []
    for h in range(2):
        part = pl.ds(h * half_rows, half_rows)
        for copy in to_y[h * (chips - 1):(h + 1) * (chips - 1)]:
            copy.wait_recv()
        total = chip_part[y, part].astype(jnp.float32)
        for e in range(1, chips):
            total = total + rx_y[e - 1, part].astype(jnp.float32)
        result[part] = total.astype(result.dtype)
        for t in range(h * half_slots, (h + 1) * half_slots):
            rows_t = result.at[pl.ds(t * cap, cap)]

            @pl.when(t == j)
            def _():
                local = pltpu.make_async_copy(rows_t, out_ref.at[j], sems.at[6, t])
                local.start()
                local.wait()

            copy = remote(rows_t, out_ref.at[j], sems.at[7, t], sems.at[8, j], (t, a, m))

            @pl.when(t != j)
            def _():
                copy.start()

            to_z.append((t, copy))
    for copy in to_core + to_y:
        copy.wait_send()
    for t, copy in to_z:
        @pl.when(t != j)
        def _():
            copy.wait_send()
    for s in range(n_ep):
        incoming = remote(result.at[pl.ds(0, cap)], out_ref.at[s], sems.at[7, s], sems.at[8, s], (s, a, m))

        @pl.when(s != j)
        def _():
            incoming.wait_recv()


def send_back(ex, n_ep, n_my, cap):
    rows, width = ex.shape
    fb = width // n_my
    return pl.pallas_call(
        functools.partial(back_kernel, n_ep, n_my),
        out_shape=jax.ShapeDtypeStruct((n_ep, cap, fb), ex.dtype),
        in_specs=[pl.BlockSpec(memory_space=pltpu.VMEM)],
        out_specs=pl.BlockSpec(memory_space=pl.ANY),
        scratch_shapes=[
            pltpu.VMEM((n_my // 2, rows, fb), ex.dtype),
            pltpu.VMEM((n_my // 2, rows, fb), ex.dtype),
            pltpu.VMEM((n_my // 2 - 1, rows, fb), ex.dtype),
            pltpu.VMEM((rows, fb), ex.dtype),
            pltpu.SemaphoreType.DMA((9, max(n_ep, n_my))),
        ],
        compiler_params=pltpu.CompilerParams(has_side_effects=True, collective_id=1),
    )(ex)


def sum_kernel(n_my, x_ref, o_ref, slots, send, recv):
    j = lax.axis_index("ep")
    a = lax.axis_index("mx")
    m = lax.axis_index("my")
    barrier = pltpu.get_barrier_semaphore()
    for e in range(1, n_my):
        pl.semaphore_signal(barrier, inc=1, device_id=(j, a, lax.rem(m + e, n_my)), device_id_type=MESH)
    pl.semaphore_wait(barrier, n_my - 1)
    slots[m] = x_ref[...]
    copies = []
    for e in range(1, n_my):
        b = lax.rem(m + e, n_my)
        copy = remote(x_ref, slots.at[m], send.at[e], recv.at[e], (j, a, b))
        copy.start()
        copies.append(copy)
    for copy in copies:
        copy.wait_send()
    for copy in copies:
        copy.wait_recv()
    o_ref[...] = jnp.sum(slots[...], axis=0)


def sum_over_my(values, kernel_id):
    n_my = lax.axis_size("my")
    row = values.reshape(1, -1)
    total = pl.pallas_call(
        functools.partial(sum_kernel, n_my),
        out_shape=jax.ShapeDtypeStruct(row.shape, row.dtype),
        in_specs=[pl.BlockSpec(memory_space=pltpu.VMEM)],
        out_specs=pl.BlockSpec(memory_space=pltpu.VMEM),
        scratch_shapes=[
            pltpu.VMEM((n_my,) + row.shape, row.dtype),
            pltpu.SemaphoreType.DMA((n_my,)),
            pltpu.SemaphoreType.DMA((n_my,)),
        ],
        compiler_params=pltpu.CompilerParams(has_side_effects=True, collective_id=kernel_id),
    )(row)
    return total.reshape(values.shape)


def row_scale(stream_f, kernel_id):
    partial_sq = jnp.sum(stream_f * stream_f, axis=1)
    row_total = sum_over_my(partial_sq, kernel_id)
    return lax.rsqrt(row_total / D + EPSILON)


def shards(
    context,
    resid_in,
    out_weight,
    norm_gain,
    gate_weight,
    up_weight,
    down_weight,
    routes,
    gate_probs,
    final_gain,
):
    ep_count = lax.axis_size("ep")
    slot_dev = max(1, EXPERTS // ep_count)
    slot_total = slot_dev * ep_count
    replicas = slot_total // EXPERTS
    capacity = MOST // replicas
    tok_rows = context.shape[0]
    feat_block = resid_in.shape[1]
    piece_units = gate_weight.shape[1]
    slot_rows = ep_count * capacity

    projected = jnp.dot(context, out_weight, preferred_element_type=jnp.float32)
    stream = (projected + resid_in.astype(jnp.float32)).astype(jnp.bfloat16)
    stream_f = stream.astype(jnp.float32)
    normed = (stream_f * row_scale(stream_f, 2)[:, None] * norm_gain[None, :]).astype(jnp.bfloat16)
    chosen = routes.reshape(-1)
    onehot = (chosen[:, None] == jnp.arange(EXPERTS, dtype=jnp.int32)[None, :]).astype(jnp.int32)
    before = jnp.cumsum(onehot, axis=0) - onehot
    ranking = jnp.sum(before * onehot, axis=1)
    slot_index = chosen * replicas + ranking % replicas
    target = slot_index * capacity + ranking // replicas
    row_ids = jnp.arange(tok_rows * TOPK, dtype=jnp.int32) // TOPK
    source = jnp.full((slot_total * capacity,), tok_rows, jnp.int32).at[target].set(row_ids)
    padded = jnp.concatenate([normed, jnp.zeros((1, feat_block), jnp.bfloat16)], axis=0)
    packed = padded[source].reshape(ep_count, capacity, feat_block)
    tok, w_gate, w_up, w_down = move_all(
        packed, gate_weight, up_weight, down_weight,
        ep_count, lax.axis_size("mx"), lax.axis_size("my"), replicas,
    )
    tokens_in = tok.reshape(slot_rows, D)
    gate_proj = jnp.einsum("rd,spd->rsp", tokens_in, w_gate, preferred_element_type=jnp.float32)
    up_proj = jnp.einsum("rd,spd->rsp", tokens_in, w_up, preferred_element_type=jnp.float32)
    hidden = (jax.nn.silu(gate_proj) * up_proj).astype(jnp.bfloat16)
    expert_out = jnp.einsum("rsp,spd->rd", hidden, w_down, preferred_element_type=jnp.float32)
    expert_out = expert_out.reshape(slot_dev, slot_rows, D)
    returned = send_back(
        expert_out.reshape(slot_rows, D).astype(jnp.bfloat16), ep_count, lax.axis_size("my"), capacity
    ).reshape(slot_total * capacity, feat_block)
    picked = returned[target].reshape(tok_rows, TOPK, feat_block).astype(jnp.float32)
    weights_norm = gate_probs / jnp.sum(gate_probs, axis=1, keepdims=True)
    mixed = jnp.sum(weights_norm[:, :, None] * picked, axis=1)
    updated = stream_f + mixed
    normed_out = (updated * row_scale(updated, 3)[:, None] * final_gain[None, :]).astype(jnp.bfloat16)
    return (normed_out, updated.astype(jnp.bfloat16))


def solution(mesh):
    placed = (
        P(("ep", "mx"), None),
        P(("ep", "mx"), "my"),
        P(None, "my"),
        P("my"),
        P(None, ("ep", "my"), "mx"),
        P(None, ("ep", "my"), "mx"),
        P(None, ("ep", "my"), "mx"),
        P(("ep", "mx"), None),
        P(("ep", "mx"), None),
        P("my"),
    )
    return jax.shard_map(
        shards,
        mesh=mesh,
        in_specs=placed,
        out_specs=(P(("ep", "mx"), "my"), P(("ep", "mx"), "my")),
        check_vma=False,
    )
```

```python
import functools

import jax
import jax.numpy as jnp
import numpy as np
from jax import lax
from jax.experimental import pallas as pl
from jax.experimental.pallas import tpu as pltpu
from jax.sharding import PartitionSpec as P

D = 2048
EXPERTS = 8
TOPK = 2
MOST = 96


EPSILON = 1e-06
MESH = pl.DeviceIdType.MESH


def remote(src, dst, send, recv, device):
    return pltpu.make_async_remote_copy(
        src_ref=src, dst_ref=dst, send_sem=send, recv_sem=recv,
        device_id=device, device_id_type=MESH,
    )


def move_kernel(n_ep, n_mx, n_my, replicas, packed_ref, gate_ref, up_ref, down_ref,
                tok_ref, gate_out, up_out, down_out, tok_sems, send_z, recv_z, fwd_send, fwd_recv,
                send_x, recv_x, local_sem):
    j = lax.axis_index("ep")
    a = lax.axis_index("mx")
    m = lax.axis_index("my")
    fb = packed_ref.shape[2]
    wb = gate_ref.shape[2]
    cols_m = pl.ds(pl.multiple_of(m * fb, fb), fb)
    cols_a = pl.ds(pl.multiple_of(a * wb, wb), wb)
    barrier = pltpu.get_barrier_semaphore()
    peers = [(lax.rem(j + d, n_ep), a, m) for d in range(1, n_ep)]
    peers += [(j, lax.rem(a + e, n_mx), m) for e in range(1, n_mx)]
    peers += [(j, a, lax.rem(m + e, n_my)) for e in range(1, n_my)]
    for peer in peers:
        pl.semaphore_signal(barrier, inc=1, device_id=peer, device_id_type=MESH)
    pl.semaphore_wait(barrier, len(peers))
    pending = []
    weights = (gate_ref, up_ref, down_ref)
    outs = (gate_out, up_out, down_out)

    half_ring = n_ep // 2
    side = half_ring - 1
    parity = lax.rem(j, 2)
    partner = j + 1 - 2 * parity

    def start_direct(k):
        local = pltpu.make_async_copy(
            weights[k].at[j // replicas], outs[k].at[j, :, cols_a], local_sem.at[k])
        local.start()
        direct = []
        for d in range(1, side + 1):
            sign = 1 - 2 * lax.rem(j + d, 2)
            t = lax.rem(j + n_ep + sign * d, n_ep)
            copy = remote(weights[k].at[t // replicas], outs[k].at[j, :, cols_a],
                          send_z.at[k, d], recv_z.at[k, d], (t, a, m))
            copy.start()
            direct.append(copy)
        return local, direct

    def start_forward(k, first, last):
        forward = []
        for d in range(first, last):
            src = lax.rem(j + n_ep - d + 2 * parity * d, n_ep)
            copy = remote(outs[k].at[src, :, cols_a], outs[k].at[src, :, cols_a],
                          fwd_send.at[k, d], fwd_recv.at[k, d], (partner, a, m))
            copy.start()
            forward.append(copy)
        return forward

    local, direct = start_direct(0)
    tok_local = pltpu.make_async_copy(packed_ref.at[j], tok_ref.at[j, :, cols_m], tok_sems.at[0, 0])
    tok_local.start()
    tok_z = []
    for d in range(1, n_ep):
        t = lax.rem(j + d, n_ep)
        copy = remote(packed_ref.at[t], tok_ref.at[j, :, cols_m], tok_sems.at[1, d], tok_sems.at[2, d], (t, a, m))
        copy.start()
        tok_z.append(copy)
    tok_my = []
    x_copies = []
    right = lax.rem(a + 1, n_mx)
    left = lax.rem(a + n_mx - 1, n_mx)
    half = n_ep // 2
    cols_l = pl.ds(pl.multiple_of(left * wb, wb), wb)
    cols_r = pl.ds(pl.multiple_of(right * wb, wb), wb)

    def relay(k, to_right, to_left):
        to_right.wait_recv()
        fwd_right = remote(outs[k].at[pl.ds(0, half), :, cols_l], outs[k].at[pl.ds(0, half), :, cols_l],
                           send_x.at[k, 2], recv_x.at[k, 2], (j, right, m))
        fwd_right.start()
        to_left.wait_recv()
        fwd_left = remote(outs[k].at[pl.ds(half, half), :, cols_r], outs[k].at[pl.ds(half, half), :, cols_r],
                          send_x.at[k, 3], recv_x.at[k, 3], (j, left, m))
        fwd_left.start()
        pending.extend([to_right, to_left])
        x_copies.extend([fwd_right, fwd_left])

    waiting = None
    for k in range(3):
        local.wait()
        forward = start_forward(k, 0, 1)
        arriving = direct
        if k + 1 < 3:
            local, direct = start_direct(k + 1)
        for copy in arriving:
            copy.wait_recv()
        pending.extend(arriving)
        forward += start_forward(k, 1, side + 1)
        if waiting is not None:
            relay(*waiting)
        for copy in forward:
            copy.wait_recv()
        pending.extend(forward)
        to_right = remote(outs[k].at[:, :, cols_a], outs[k].at[:, :, cols_a],
                          send_x.at[k, 0], recv_x.at[k, 0], (j, right, m))
        to_left = remote(outs[k].at[:, :, cols_a], outs[k].at[:, :, cols_a],
                         send_x.at[k, 1], recv_x.at[k, 1], (j, left, m))
        to_right.start()
        to_left.start()
        waiting = (k, to_right, to_left)
        if k == 0:
            tok_local.wait()
            for copy in tok_z:
                copy.wait_recv()
            pending.extend(tok_z)
            for e in range(1, n_my):
                b = lax.rem(m + e, n_my)
                copy = remote(tok_ref.at[:, :, cols_m], tok_ref.at[:, :, cols_m], tok_sems.at[3, e], tok_sems.at[4, e], (j, a, b))
                copy.start()
                tok_my.append(copy)
            pending.extend(tok_my)
    relay(*waiting)
    pending.extend(x_copies)
    for copy in pending:
        copy.wait_send()
    for copy in tok_my + x_copies:
        copy.wait_recv()


def move_all(packed, gate_weight, up_weight, down_weight, n_ep, n_mx, n_my, replicas):
    _, rows, fb = packed.shape
    _, units, wb = gate_weight.shape
    return pl.pallas_call(
        functools.partial(move_kernel, n_ep, n_mx, n_my, replicas),
        out_shape=(
            jax.ShapeDtypeStruct((n_ep, rows, n_my * fb), packed.dtype),
        ) + (jax.ShapeDtypeStruct((n_ep, units, n_mx * wb), gate_weight.dtype),) * 3,
        in_specs=[pl.BlockSpec(memory_space=pl.ANY)] * 4,
        out_specs=(pl.BlockSpec(memory_space=pl.ANY),) * 4,
        scratch_shapes=[
            pltpu.SemaphoreType.DMA((5, max(n_ep, n_my))),
            pltpu.SemaphoreType.DMA((3, n_ep)),
            pltpu.SemaphoreType.DMA((3, n_ep)),
            pltpu.SemaphoreType.DMA((3, n_ep)),
            pltpu.SemaphoreType.DMA((3, n_ep)),
            pltpu.SemaphoreType.DMA((3, max(n_mx, 4))),
            pltpu.SemaphoreType.DMA((3, max(n_mx, 4))),
            pltpu.SemaphoreType.DMA((3,)),
        ],
        compiler_params=pltpu.CompilerParams(has_side_effects=True, collective_id=0),
    )(packed, gate_weight, up_weight, down_weight)


def back_kernel(n_ep, n_my, ex_ref, out_ref, rx_core, chip_part, rx_y, result, sems):
    j = lax.axis_index("ep")
    a = lax.axis_index("mx")
    m = lax.axis_index("my")
    fb = out_ref.shape[2]
    cap = out_ref.shape[1]
    chips = n_my // 2
    core = lax.rem(m, 2)
    y = m // 2
    partner = m + 1 - 2 * core
    barrier = pltpu.get_barrier_semaphore()
    peers = [(j, a, partner)]
    peers += [(j, a, lax.rem(y + e, chips) * 2 + core) for e in range(1, chips)]
    peers += [(lax.rem(j + d, n_ep), a, m) for d in range(1, n_ep)]
    for peer in peers:
        pl.semaphore_signal(barrier, inc=1, device_id=peer, device_id_type=MESH)
    pl.semaphore_wait(barrier, len(peers))

    def cols(block):
        return pl.ds(pl.multiple_of(block * fb, fb), fb)

    rows = result.shape[0]
    half_rows = rows // 2
    half_slots = n_ep // 2
    to_core = []
    for h in range(2):
        part = pl.ds(h * half_rows, half_rows)
        for i in range(chips):
            copy = remote(ex_ref.at[part, cols(1 - core + 2 * i)], rx_core.at[i, part],
                          sems.at[0, i + chips * h], sems.at[1, i + chips * h], (j, a, partner))
            copy.start()
            to_core.append(copy)
    to_y = []
    for h in range(2):
        part = pl.ds(h * half_rows, half_rows)
        for copy in to_core[h * chips:(h + 1) * chips]:
            copy.wait_recv()
        for i in range(chips):
            own = ex_ref[part, cols(core + 2 * i)].astype(jnp.float32)
            chip_part[i, part] = (own + rx_core[i, part].astype(jnp.float32)).astype(chip_part.dtype)
        for e in range(1, chips):
            other = lax.rem(y + e, chips)
            copy = remote(chip_part.at[other, part], rx_y.at[e - 1, part],
                          sems.at[2 + 2 * h, e], sems.at[3 + 2 * h, e], (j, a, other * 2 + core))
            copy.start()
            to_y.append(copy)
    to_z = []
    for h in range(2):
        part = pl.ds(h * half_rows, half_rows)
        for copy in to_y[h * (chips - 1):(h + 1) * (chips - 1)]:
            copy.wait_recv()
        total = chip_part[y, part].astype(jnp.float32)
        for e in range(1, chips):
            total = total + rx_y[e - 1, part].astype(jnp.float32)
        result[part] = total.astype(result.dtype)
        for t in range(h * half_slots, (h + 1) * half_slots):
            rows_t = result.at[pl.ds(t * cap, cap)]

            @pl.when(t == j)
            def _():
                local = pltpu.make_async_copy(rows_t, out_ref.at[j], sems.at[6, t])
                local.start()
                local.wait()

            copy = remote(rows_t, out_ref.at[j], sems.at[7, t], sems.at[8, j], (t, a, m))

            @pl.when(t != j)
            def _():
                copy.start()

            to_z.append((t, copy))
    for copy in to_core + to_y:
        copy.wait_send()
    for t, copy in to_z:
        @pl.when(t != j)
        def _():
            copy.wait_send()
    for s in range(n_ep):
        incoming = remote(result.at[pl.ds(0, cap)], out_ref.at[s], sems.at[7, s], sems.at[8, s], (s, a, m))

        @pl.when(s != j)
        def _():
            incoming.wait_recv()


def send_back(ex, n_ep, n_my, cap):
    rows, width = ex.shape
    fb = width // n_my
    return pl.pallas_call(
        functools.partial(back_kernel, n_ep, n_my),
        out_shape=jax.ShapeDtypeStruct((n_ep, cap, fb), ex.dtype),
        in_specs=[pl.BlockSpec(memory_space=pltpu.VMEM)],
        out_specs=pl.BlockSpec(memory_space=pl.ANY),
        scratch_shapes=[
            pltpu.VMEM((n_my // 2, rows, fb), ex.dtype),
            pltpu.VMEM((n_my // 2, rows, fb), ex.dtype),
            pltpu.VMEM((n_my // 2 - 1, rows, fb), ex.dtype),
            pltpu.VMEM((rows, fb), ex.dtype),
            pltpu.SemaphoreType.DMA((9, max(n_ep, n_my))),
        ],
        compiler_params=pltpu.CompilerParams(has_side_effects=True, collective_id=1),
    )(ex)


def sum_kernel(n_my, x_ref, o_ref, slots, send, recv):
    j = lax.axis_index("ep")
    a = lax.axis_index("mx")
    m = lax.axis_index("my")
    barrier = pltpu.get_barrier_semaphore()
    for e in range(1, n_my):
        pl.semaphore_signal(barrier, inc=1, device_id=(j, a, lax.rem(m + e, n_my)), device_id_type=MESH)
    pl.semaphore_wait(barrier, n_my - 1)
    slots[m] = x_ref[...]
    copies = []
    for e in range(1, n_my):
        b = lax.rem(m + e, n_my)
        copy = remote(x_ref, slots.at[m], send.at[e], recv.at[e], (j, a, b))
        copy.start()
        copies.append(copy)
    for copy in copies:
        copy.wait_send()
    for copy in copies:
        copy.wait_recv()
    o_ref[...] = jnp.sum(slots[...], axis=0)


def sum_over_my(values, kernel_id):
    n_my = lax.axis_size("my")
    row = values.reshape(1, -1)
    total = pl.pallas_call(
        functools.partial(sum_kernel, n_my),
        out_shape=jax.ShapeDtypeStruct(row.shape, row.dtype),
        in_specs=[pl.BlockSpec(memory_space=pltpu.VMEM)],
        out_specs=pl.BlockSpec(memory_space=pltpu.VMEM),
        scratch_shapes=[
            pltpu.VMEM((n_my,) + row.shape, row.dtype),
            pltpu.SemaphoreType.DMA((n_my,)),
            pltpu.SemaphoreType.DMA((n_my,)),
        ],
        compiler_params=pltpu.CompilerParams(has_side_effects=True, collective_id=kernel_id),
    )(row)
    return total.reshape(values.shape)


def row_scale(stream_f, kernel_id):
    partial_sq = jnp.sum(stream_f * stream_f, axis=1)
    row_total = sum_over_my(partial_sq, kernel_id)
    return lax.rsqrt(row_total / D + EPSILON)


def shards(
    context,
    resid_in,
    out_weight,
    norm_gain,
    gate_weight,
    up_weight,
    down_weight,
    routes,
    gate_probs,
    final_gain,
):
    ep_count = lax.axis_size("ep")
    slot_dev = max(1, EXPERTS // ep_count)
    slot_total = slot_dev * ep_count
    replicas = slot_total // EXPERTS
    capacity = MOST // replicas
    tok_rows = context.shape[0]
    feat_block = resid_in.shape[1]
    piece_units = gate_weight.shape[1]
    slot_rows = ep_count * capacity

    projected = jnp.dot(context, out_weight, preferred_element_type=jnp.float32)
    stream = (projected + resid_in.astype(jnp.float32)).astype(jnp.bfloat16)
    stream_f = stream.astype(jnp.float32)
    normed = (stream_f * row_scale(stream_f, 2)[:, None] * norm_gain[None, :]).astype(jnp.bfloat16)
    chosen = routes.reshape(-1)
    onehot = (chosen[:, None] == jnp.arange(EXPERTS, dtype=jnp.int32)[None, :]).astype(jnp.int32)
    before = jnp.cumsum(onehot, axis=0) - onehot
    ranking = jnp.sum(before * onehot, axis=1)
    slot_index = chosen * replicas + ranking % replicas
    target = slot_index * capacity + ranking // replicas
    row_ids = jnp.arange(tok_rows * TOPK, dtype=jnp.int32) // TOPK
    source = jnp.full((slot_total * capacity,), tok_rows, jnp.int32).at[target].set(row_ids)
    padded = jnp.concatenate([normed, jnp.zeros((1, feat_block), jnp.bfloat16)], axis=0)
    packed = padded[source].reshape(ep_count, capacity, feat_block)
    tok, w_gate, w_up, w_down = move_all(
        packed, gate_weight, up_weight, down_weight,
        ep_count, lax.axis_size("mx"), lax.axis_size("my"), replicas,
    )
    tokens_in = tok.reshape(slot_rows, D)
    gate_proj = jnp.einsum("rd,spd->rsp", tokens_in, w_gate, preferred_element_type=jnp.float32)
    up_proj = jnp.einsum("rd,spd->rsp", tokens_in, w_up, preferred_element_type=jnp.float32)
    hidden = (jax.nn.silu(gate_proj) * up_proj).astype(jnp.bfloat16)
    expert_out = jnp.einsum("rsp,spd->rd", hidden, w_down, preferred_element_type=jnp.float32)
    expert_out = expert_out.reshape(slot_dev, slot_rows, D)
    returned = send_back(
        expert_out.reshape(slot_rows, D).astype(jnp.bfloat16), ep_count, lax.axis_size("my"), capacity
    ).reshape(slot_total * capacity, feat_block)
    picked = returned[target].reshape(tok_rows, TOPK, feat_block).astype(jnp.float32)
    weights_norm = gate_probs / jnp.sum(gate_probs, axis=1, keepdims=True)
    mixed = jnp.sum(weights_norm[:, :, None] * picked, axis=1)
    updated = stream_f + mixed
    normed_out = (updated * row_scale(updated, 3)[:, None] * final_gain[None, :]).astype(jnp.bfloat16)
    return (normed_out, updated.astype(jnp.bfloat16))


def solution(mesh):
    placed = (
        P(("ep", "mx"), None),
        P(("ep", "mx"), "my"),
        P(None, "my"),
        P("my"),
        P(None, ("ep", "my"), "mx"),
        P(None, ("ep", "my"), "mx"),
        P(None, ("ep", "my"), "mx"),
        P(("ep", "mx"), None),
        P(("ep", "mx"), None),
        P("my"),
    )
    return jax.shard_map(
        shards,
        mesh=mesh,
        in_specs=placed,
        out_specs=(P(("ep", "mx"), "my"), P(("ep", "mx"), "my")),
        check_vma=False,
    )
```
